32 devices in a mesh: gx: 4 (over z), gy: 8 (over y, x, core).
Axes of the slice: x: 2, y: 2, z: 4, core: 2. Of those that a mesh axis runs over, the one named last changes fastest.
Arguments:
- object_field: float32 [2, 2, 512, 1024], P(None, None, 'gx', 'gy'), may hold values from -1 to 1
- probe: float32 [2, 128, 128], replicated, may hold values from -0.5 to 0.5
- propagator: float32 [128, 128], replicated, may hold values from -3.140625 to 3.140625
- offsets: int32 [4, 8, 12, 2], P('gx', 'gy'), may hold values from 0 to 128
- counts: int32 [4, 8], P('gx', 'gy'), may hold values from 1 to 12, as said below
- intensity: float32 [4, 8, 12, 128, 128], P('gx', 'gy'), may hold values from 0.1 to 4
Outputs:
- updated_object: float32 [2, 2, 512, 1024], P(None, None, 'gx', 'gy')
The draws below stay inside these ranges and needn't reach their ends.
Inputs may be any that keep to these rules, and one draw needn't show every extreme that they name: `counts`: some tile has all 12 slots live in every draw; positions are live in slot order.
All inputs are finite; a program needn't handle non-finite values.
Results may differ from the reference program's by a relative error of at most 0.0003.
Values sent between devices are 32-bit elements; how exact they have to be, the bound alone decides.
No kernel may reach another device: no remote copies, remote signals or barrier semaphores. Data moves between devices by JAX's collectives and lax.ppermute only.
A program may use at most 64 MiB of HBM per device.

```python
import math
import jax
import jax.numpy as jnp
from jax import lax

PROBE = 128
HALO = 64
TILE = 128
BATCH = 2
NB = 6
POS = 12
TILES_X = 4
TILES_Y = 8
NX = 512
NY = 1024


def draw_counts(key, part):
    keys = jax.random.split(jax.random.fold_in(key, 7), 2)
    values = jax.random.randint(keys[0], (TILES_X * TILES_Y,), 1, POS + 1, dtype=jnp.int32)
    chosen = jax.random.randint(keys[1], (), 0, TILES_X * TILES_Y, dtype=jnp.int32)
    values = values.at[chosen].set(POS)
    return values.reshape(TILES_X, TILES_Y)


def with_ends(array, rng, least, largest):
    extent = array.shape
    spot = [jax.random.randint(jax.random.fold_in(rng, axis), (), 0, extent[axis]) for axis in range(len(extent))]
    array = array.at[tuple(spot)].set(least)
    longest = extent.index(max(extent))
    spot[longest] = (spot[longest] + 1) % extent[longest]
    return array.at[tuple(spot)].set(largest)


def block_levels(own_key, extent, pieces, smallest, largest):
    loudness = 1.0
    for position, parts in pieces:
        steps = jax.random.uniform(jax.random.fold_in(jax.random.fold_in(own_key, 6), position), (parts,), jnp.float32, smallest / len(pieces), largest / len(pieces))
        loudness = loudness * jnp.repeat(jnp.exp(steps), extent[position] // parts).reshape((-1,) + (1,) * (len(extent) - 1 - position))
    return loudness


def setup_inputs(seed: int = 0) -> dict:
    splits = jax.random.split(jax.random.key(seed), 7)
    return {
        "object_field": jnp.clip(jax.random.uniform(splits[0], (2, 2, NX, NY), jnp.float32, -1.0, 1.0) * block_levels(splits[0], (2, 2, NX, NY), ((2, 4), (3, 8)), -0.4, 0.0), -1.0, 1.0),
        "probe": jnp.clip(jax.random.uniform(splits[1], (2, PROBE, PROBE), jnp.float32, -0.5, 0.5), -0.5, 0.5),
        "propagator": jnp.clip(jax.random.uniform(splits[2], (PROBE, PROBE), jnp.float32, -3.140625, 3.140625), -3.140625, 3.140625),
        "offsets": with_ends(jax.random.randint(splits[3], (TILES_X, TILES_Y, POS, 2), 0, TILE + 1), jax.random.fold_in(splits[3], 1), 0, TILE).astype(jnp.int32),
        "counts": draw_counts(jax.random.fold_in(splits[6], 71), 0),
        "intensity": jnp.clip(jnp.exp(math.log(4.0) - 3.6888794 * jax.random.uniform(splits[5], (TILES_X, TILES_Y, POS, PROBE, PROBE), jnp.float32) ** block_levels(splits[5], (TILES_X, TILES_Y, POS, PROBE, PROBE), ((0, 4), (1, 8)), -0.2, 0.2)), 0.1, 4.0),
    }


def product(first, second):
    return (first[0] * second[0] - first[1] * second[1], first[0] * second[1] + first[1] * second[0])

def conjugate(field):
    return (field[0], -field[1])

def tables(width):
    index = jnp.arange(width, dtype=jnp.int32)
    phase = (index[:, None] * index[None, :] % width).astype(jnp.float32) * (2.0 * math.pi / width)
    return (jnp.cos(phase) / math.sqrt(width), jnp.sin(phase) / math.sqrt(width))

def left_mul(matrix, field):
    return jnp.einsum('ij,...jk->...ik', matrix, field, precision=lax.Precision.HIGHEST)

def right_mul(field, matrix):
    return jnp.einsum('...ij,jk->...ik', field, matrix, precision=lax.Precision.HIGHEST)

def transform(field, basis, direction):
    cosine = basis[0]
    signed = direction * basis[1]
    first_real = left_mul(cosine, field[0]) - left_mul(signed, field[1])
    first_imag = left_mul(cosine, field[1]) + left_mul(signed, field[0])
    return (right_mul(first_real, cosine) - right_mul(first_imag, signed), right_mul(first_imag, cosine) + right_mul(first_real, signed))

def gradients(probe_pair, wave_pair, patches, measured, basis):
    slice_one = (patches[:, 0, 0], patches[:, 0, 1])
    slice_two = (patches[:, 1, 0], patches[:, 1, 1])
    entrance = product(probe_pair, slice_one)
    spectrum = product(transform(entrance, basis, -1.0), wave_pair)
    inner_wave = transform(spectrum, basis, 1.0)
    farfield = transform(product(inner_wave, slice_two), basis, -1.0)
    excess = farfield[0] * farfield[0] + farfield[1] * farfield[1] - measured
    back_exit = transform((excess * farfield[0], excess * farfield[1]), basis, 1.0)
    grad_two = product(conjugate(inner_wave), back_exit)
    back_inner = product(conjugate(slice_two), back_exit)
    back_spec = product(conjugate(wave_pair), transform(back_inner, basis, -1.0))
    grad_one = product(conjugate(probe_pair), transform(back_spec, basis, 1.0))
    return jnp.stack([jnp.stack(grad_one, 1), jnp.stack(grad_two, 1)], 1)

def reference(object_field, probe, propagator, offsets, counts, intensity):
    width = PROBE
    margin = HALO
    basis = tables(width)
    probe_pair = (probe[0], probe[1])
    wave_pair = (jnp.cos(propagator), jnp.sin(propagator))
    field = object_field
    zero = jnp.zeros((), jnp.int32)
    for period in range(NB):
        padded = jnp.pad(field, ((0, 0), (0, 0), (margin, margin), (margin, margin)))
        first_slot = period * BATCH

        def visit(total, tile_number):
            row_tile = (tile_number // TILES_Y).astype(jnp.int32)
            col_tile = (tile_number % TILES_Y).astype(jnp.int32)
            starts = []
            patches = []
            for member in range(BATCH):
                row_start = (row_tile * TILE + offsets[row_tile, col_tile, first_slot + member, 0]).astype(jnp.int32)
                col_start = (col_tile * TILE + offsets[row_tile, col_tile, first_slot + member, 1]).astype(jnp.int32)
                starts.append((zero, zero, row_start, col_start))
                patches.append(lax.dynamic_slice(padded, (zero, zero, row_start, col_start), (2, 2, width, width)))
            measured = intensity[row_tile, col_tile, first_slot:first_slot + BATCH]
            live = first_slot + jnp.arange(BATCH, dtype=jnp.int32) < counts[row_tile, col_tile]
            grads = gradients(probe_pair, wave_pair, jnp.stack(patches), measured, basis)
            grads = grads * live.astype(jnp.float32)[:, None, None, None, None]
            for member in range(BATCH):
                current = lax.dynamic_slice(total, starts[member], (2, 2, width, width))
                total = lax.dynamic_update_slice(total, current + grads[member], starts[member])
            return (total, None)
        total, _ = lax.scan(visit, jnp.zeros_like(padded), jnp.arange(TILES_X * TILES_Y, dtype=jnp.int32))
        field = field - 0.08 * total[:, :, margin:-margin, margin:-margin]
    return field
```

```python
import functools
import math

import jax
import jax.numpy as jnp
import numpy as np
from jax import lax
from jax.experimental import pallas as pl
from jax.experimental.pallas import tpu as pltpu
from jax.sharding import PartitionSpec as P

BATCH = 2
NB = 6
STEP = 0.08
F32 = jnp.float32
BF16 = jnp.bfloat16


def pairs(size, first):
    return [p for i in range(first, size - 1, 2) for p in ((i, i + 1), (i + 1, i))]


def swap(value, axis, slot):
    return lax.ppermute(value, axis, pairs(lax.axis_size(axis), slot))


def dft_tables(n):
    index = np.arange(n)
    phase = (index[:, None] * index[None, :] % n) * (2.0 * math.pi / n)
    c, s = np.cos(phase) / math.sqrt(n), np.sin(phase) / math.sqrt(n)
    fwd = np.block([[c, -s], [s, c]]).astype(np.float32)
    inv = np.block([[c, s], [-s, c]]).astype(np.float32)
    out = []
    for m in (fwd, inv):
        hi = m.astype(jnp.bfloat16)
        lo = (m - hi.astype(np.float32)).astype(jnp.bfloat16)
        out += [hi, lo]
    return np.stack(out)


def split(x):
    hi = x.astype(BF16)
    return hi, (x - hi.astype(F32)).astype(BF16)


def dot(a, b):
    return jnp.dot(a, b, preferred_element_type=F32)


def right(x, tab, inverse):
    hi, lo = split(x)
    mh, ml = tab[2 * inverse], tab[2 * inverse + 1]
    return dot(hi, mh) + (dot(lo, mh) + dot(hi, ml))


def left(x, tab, inverse):
    hi, lo = split(x)
    mh, ml = tab[2 - 2 * inverse], tab[3 - 2 * inverse]
    return dot(mh, hi) + (dot(mh, lo) + dot(ml, hi))


def blocks(x):
    n = x.shape[0] // 2
    return x[:n, :n], x[:n, n:], x[n:, :n], x[n:, n:]


def join(a, b, c, d):
    return jnp.concatenate([jnp.concatenate([a, b], 1), jnp.concatenate([c, d], 1)], 0)


def turn(x):
    a, b, c, d = blocks(x)
    return join(a, c, b, d)


def cmul(a, b):
    return a[0] * b[0] - a[1] * b[1], a[0] * b[1] + a[1] * b[0]


def conj_mul(a, b):
    return a[0] * b[0] + a[1] * b[1], a[0] * b[1] - a[1] * b[0]


def slot_masks(start, parity, n, dim):
    i = lax.broadcasted_iota(jnp.int32, (n, n), dim)
    return (1 - 2 * parity) * (i - start) - parity < 0


def gather(obj, rows, cols):
    return tuple(
        jnp.where(rows, jnp.where(cols, obj[0, 0, p], obj[0, 1, p]), jnp.where(cols, obj[1, 0, p], obj[1, 1, p]))
        for p in range(2)
    )


def pick(mask, slot, x):
    return jnp.where(mask, x, 0.0) if slot == 0 else jnp.where(mask, 0.0, x)


def valid(parity, index, size, slot, n, dim):
    i = lax.broadcasted_iota(jnp.int32, (n, n), dim)
    half = (1 - parity) if slot == 0 else parity
    low = jnp.where(jnp.logical_and(half == 0, index == 0), n // 2, 0)
    high = jnp.where(jnp.logical_and(half == 1, index == size - 1), n // 2, n)
    return jnp.logical_and(i >= low, i < high)


def where_is(info):
    return info[0], info[1], info[0] % 2, info[1] % 2


def advance(obj_in, obj_out, sums, info, sizes, first):
    ax, ay, px, py = where_is(info)
    n = obj_out.shape[-1]
    for tr in range(2):
        for tc in range(2):
            if not first:
                inside = jnp.logical_and(valid(px, ax, sizes[0], tr, n, 0), valid(py, ay, sizes[1], tc, n, 1))
            for p in range(2):
                s = sums(tr, tc, p)
                obj_out[tr, tc, p] = s if first else obj_in[tr, tc, p] - jnp.where(inside, STEP * s, 0.0)


def patch_masks(info, offsets, slot, n):
    _, _, px, py = where_is(info)
    return (
        slot_masks(offsets[slot, 0], px, n, 0),
        slot_masks(offsets[slot, 1], py, n, 1),
    )


def kernel_a(period, sizes, first, info, offsets, *refs):
    if first:
        te0, te1, to0, to1, z, probe, wave, tab, obj_out, inner = refs[0], refs[1], refs[2], refs[3], refs[4:8], *refs[8:]
        obj_in = None
    else:
        obj_in, te0, te1, to0, to1 = refs[:5]
        z, (probe, wave, tab, obj_out, inner) = refs[5:9], refs[9:]
    own = ((te0, to0), (te1, to1))
    got = ((z[0], z[2]), (z[1], z[3]))
    advance(obj_in, obj_out, lambda tr, tc, p: own[tr][tc][p] + got[tr][tc][p], info, sizes, first)
    n = obj_out.shape[-1]
    parts = []
    for m in range(BATCH):
        rows, cols = patch_masks(info, offsets, period * BATCH + m, n)
        parts += cmul((probe[m, 0], probe[m, 1]), gather(obj_out, rows, cols))
    x = left(turn(right(join(*parts), tab, 0)), tab, 0)
    a, b, c, d = blocks(x)
    q = (wave[0], wave[1])
    (ar, ai), (br, bi) = cmul((a, c), q), cmul((b, d), q)
    x = right(turn(left(join(ar, br, ai, bi), tab, 1)), tab, 1)
    inner[...] = x


def kernel_b(period, sizes, first, info, offsets, counts, *refs):
    if first:
        ue, uo, ve, vo, inner, measured, tab, obj_out, back, h0, h1 = refs
        obj_in = None
    else:
        obj_in, ue, uo, ve, vo, inner, measured, tab, obj_out, back, h0, h1 = refs
    own, got = (ue, uo), (ve, vo)
    advance(obj_in, obj_out, lambda tr, tc, p: own[tc][tr, p] + got[tc][tr, p], info, sizes, first)
    n = obj_out.shape[-1]
    masks = [patch_masks(info, offsets, period * BATCH + m, n) for m in range(BATCH)]
    a, b, c, d = blocks(inner[...])
    waves = ((a, b), (c, d))
    seconds = [gather(obj_out, *masks[m]) for m in range(BATCH)]
    parts = []
    for m in range(BATCH):
        parts += cmul(waves[m], seconds[m])
    x = left(turn(right(join(*parts), tab, 0)), tab, 0)
    a, b, c, d = blocks(x)
    e0 = a * a + c * c - measured[0]
    e1 = b * b + d * d - measured[1]
    x = right(turn(left(join(e0 * a, e1 * b, e0 * c, e1 * d), tab, 1)), tab, 1)
    a, b, c, d = blocks(x)
    back_waves = ((a, b), (c, d))
    total = [[[0.0, 0.0], [0.0, 0.0]], [[0.0, 0.0], [0.0, 0.0]]]
    for m in range(BATCH):
        live = jnp.where(period * BATCH + m < counts[0], 1.0, 0.0)
        grad = conj_mul(waves[m], back_waves[m])
        br, bi = conj_mul(seconds[m], back_waves[m])
        back[m * n : (m + 1) * n, :n] = br
        back[m * n : (m + 1) * n, n:] = bi
        rows, cols = masks[m]
        for p in range(2):
            g = grad[p] * live
            for tr in range(2):
                gr = pick(rows, tr, g)
                for tc in range(2):
                    total[tr][tc][p] = total[tr][tc][p] + pick(cols, tc, gr)
    for tc in range(2):
        for p in range(2):
            h0[tc, p] = total[0][tc][p]
            h1[tc, p] = total[1][tc][p]


def kernel_c(period, sizes, info, offsets, counts, back, probe, wave, tab, ge, go):
    n = ge.shape[-1]
    x = left(turn(right(back[...], tab, 0)), tab, 0)
    a, b, c, d = blocks(x)
    q = (wave[0], wave[1])
    (ar, ai), (br, bi) = conj_mul(q, (a, c)), conj_mul(q, (b, d))
    x = right(turn(left(join(ar, br, ai, bi), tab, 1)), tab, 1)
    a, b, c, d = blocks(x)
    waves = ((a, b), (c, d))
    total = [[[0.0, 0.0], [0.0, 0.0]], [[0.0, 0.0], [0.0, 0.0]]]
    for m in range(BATCH):
        live = jnp.where(period * BATCH + m < counts[0], 1.0, 0.0)
        grad = conj_mul((probe[m, 0], probe[m, 1]), waves[m])
        rows, cols = patch_masks(info, offsets, period * BATCH + m, n)
        for p in range(2):
            g = grad[p] * live
            for tr in range(2):
                gr = pick(rows, tr, g)
                for tc in range(2):
                    total[tr][tc][p] = total[tr][tc][p] + pick(cols, tc, gr)
    for tr in range(2):
        for p in range(2):
            ge[tr, p] = total[tr][0][p]
            go[tr, p] = total[tr][1][p]


def kernel_roll(period, offsets, probe, out):
    n = out.shape[-1]
    for m in range(BATCH):
        r = lax.rem(offsets[period * BATCH + m, 0], n)
        q = lax.rem(offsets[period * BATCH + m, 1], n)
        for p in range(2):
            out[m, p] = pltpu.roll(pltpu.roll(probe[p], r, 0), q, 1)


def kernel_place(info, tile, ge, go, h0, h1):
    _, _, px, py = where_is(info)
    n = tile.shape[-1]
    rows, cols = slot_masks(n // 2, px, n, 0), slot_masks(n // 2, py, n, 1)
    for s in range(2):
        for p in range(2):
            x = pltpu.roll(pltpu.roll(tile[s, p], n // 2, 0), n // 2, 1)
            for tr in range(2):
                for tc in range(2):
                    y = pick(cols, tc, pick(rows, tr, x))
                    if s == 0:
                        (ge, go)[tc][tr, p] = y
                    else:
                        (h0, h1)[tr][tc, p] = y


def kernel_end(sizes, info, obj0, te0, te1, to0, to1, z0, z1, z2, z3, obj1, ue, uo, ve, vo, out):
    ax, ay, px, py = where_is(info)
    n = out.shape[-1]
    rows, cols = slot_masks(n // 2, px, n, 0), slot_masks(n // 2, py, n, 1)

    def quad(mask_r, mask_c, f):
        return jnp.where(
            mask_r,
            jnp.where(mask_c, f(0, 0), f(0, 1)),
            jnp.where(mask_c, f(1, 0), f(1, 1)),
        )

    own = ((te0, to0), (te1, to1))
    got = ((z0, z2), (z1, z3))
    for p in range(2):
        a = quad(rows, cols, lambda tr, tc: obj0[tr, tc, p] - STEP * (own[tr][tc][p] + got[tr][tc][p]))
        b = quad(rows, cols, lambda tr, tc: obj1[tr, tc, p] - STEP * ((ue, uo)[tc][tr, p] + (ve, vo)[tc][tr, p]))
        for s, x in enumerate((a, b)):
            out[s, p] = pltpu.roll(pltpu.roll(x, n // 2, 0), n // 2, 1)


def kernel_fold(g, r, t0, t1):
    t0[...] = g[0] + r[0]
    t1[...] = g[1] + r[1]


def kernel_fold2(h0, h1, y0, y1, ue, uo):
    for tr, (h, y) in enumerate(((h0, y0), (h1, y1))):
        for tc, u in enumerate((ue, uo)):
            u[tr] = h[tc] + y[tc]


def call(kernel, name, scalars, arrays, outs):
    return pl.pallas_call(
        kernel,
        out_shape=[jax.ShapeDtypeStruct(s, F32) for s in outs],
        in_specs=[pl.BlockSpec(memory_space=pltpu.SMEM)] * len(scalars)
        + [pl.BlockSpec(memory_space=pltpu.VMEM)] * len(arrays),
        out_specs=[pl.BlockSpec(memory_space=pltpu.VMEM)] * len(outs),
        name=name,
    )(*scalars, *arrays)


def local(object_field, probe, propagator, offsets, counts, intensity):
    n = probe.shape[1]
    sizes = (lax.axis_size("gx"), lax.axis_size("gy"))
    info = jnp.stack([lax.axis_index("gx"), lax.axis_index("gy")]).astype(jnp.int32)
    offs = offsets[0, 0]
    count = counts[0]
    tab = jnp.asarray(dft_tables(n))
    wave = jnp.stack([jnp.cos(propagator), jnp.sin(propagator)])
    pair, quad, half, block = (2, n, n), (2, 2, 2, n, n), (2, 2, n, n), (2 * n, 2 * n)

    def exchange0(ge, go):
        re, ro = swap(ge, "gy", 0), swap(go, "gy", 1)
        te0, te1 = call(kernel_fold, "fold_e", [], [ge, re], [pair, pair])
        z0, z1 = swap(te0, "gx", 0), swap(te1, "gx", 1)
        to0, to1 = call(kernel_fold, "fold_o", [], [go, ro], [pair, pair])
        z2, z3 = swap(to0, "gx", 0), swap(to1, "gx", 1)
        return te0, te1, to0, to1, z0, z1, z2, z3

    def exchange1(h0, h1):
        y0, y1 = swap(h0, "gx", 0), swap(h1, "gx", 1)
        ue, uo = call(kernel_fold2, "fold_2", [], [h0, h1, y0, y1], [half, half])
        ve, vo = swap(ue, "gy", 0), swap(uo, "gy", 1)
        return ue, uo, ve, vo

    probes = [
        call(functools.partial(kernel_roll, b), "roll", [offs], [probe], [(2, 2, n, n)])[0] for b in range(NB)
    ]
    ge, go, h0, h1 = call(kernel_place, "place", [info], [object_field], [half] * 4)
    sums0 = exchange0(ge, go)
    sums1 = exchange1(h0, h1)
    obj0, obj1 = [], []
    for b in range(NB):
        first = b == 0
        out0, inner = call(
            functools.partial(kernel_a, b, sizes, first), "wave_in", [info, offs],
            [*obj0, *sums0, probes[b], wave, tab], [quad, block],
        )
        measured = intensity[0, 0, b * BATCH : (b + 1) * BATCH]
        out1, back, h0, h1 = call(
            functools.partial(kernel_b, b, sizes, first), "residual", [info, offs, count],
            [*obj1, *sums1, inner, measured, tab], [quad, block, half, half],
        )
        ge, go = call(
            functools.partial(kernel_c, b, sizes), "wave_back", [info, offs, count],
            [back, probes[b], wave, tab], [half, half],
        )
        obj0, obj1 = [out0], [out1]
        sums1 = exchange1(h0, h1)
        sums0 = exchange0(ge, go)
    (out,) = call(
        functools.partial(kernel_end, sizes), "finish", [info], [*obj0, *sums0, *obj1, *sums1], [object_field.shape]
    )
    return out


def solution(mesh):
    in_specs = (
        P(None, None, "gx", "gy"),
        P(),
        P(),
        P("gx", "gy", None, None),
        P("gx", "gy"),
        P("gx", "gy", None, None, None),
    )
    out_specs = P(None, None, "gx", "gy")
    return jax.shard_map(local, mesh=mesh, in_specs=in_specs, out_specs=out_specs, check_vma=False)
```

```python
import functools
import math

import jax
import jax.numpy as jnp
import numpy as np
from jax import lax
from jax.experimental import pallas as pl
from jax.experimental.pallas import tpu as pltpu
from jax.sharding import PartitionSpec as P

BATCH = 2
NB = 6
STEP = 0.08
F32 = jnp.float32
BF16 = jnp.bfloat16


def pairs(size, first):
    return [p for i in range(first, size - 1, 2) for p in ((i, i + 1), (i + 1, i))]


def swap(value, axis, slot):
    return lax.ppermute(value, axis, pairs(lax.axis_size(axis), slot))


def dft_tables(n):
    index = np.arange(n)
    phase = (index[:, None] * index[None, :] % n) * (2.0 * math.pi / n)
    c, s = np.cos(phase) / math.sqrt(n), np.sin(phase) / math.sqrt(n)
    fwd = np.block([[c, -s], [s, c]]).astype(np.float32)
    inv = np.block([[c, s], [-s, c]]).astype(np.float32)
    out = []
    for m in (fwd, inv):
        hi = m.astype(jnp.bfloat16)
        lo = (m - hi.astype(np.float32)).astype(jnp.bfloat16)
        out += [hi, lo]
    return np.stack(out)


def split(x):
    hi = x.astype(BF16)
    return hi, (x - hi.astype(F32)).astype(BF16)


def dot(a, b):
    return jnp.dot(a, b, preferred_element_type=F32)


def right(x, tab, inverse):
    hi, lo = split(x)
    mh, ml = tab[2 * inverse], tab[2 * inverse + 1]
    return dot(hi, mh) + (dot(lo, mh) + dot(hi, ml))


def left(x, tab, inverse):
    hi, lo = split(x)
    mh, ml = tab[2 - 2 * inverse], tab[3 - 2 * inverse]
    return dot(mh, hi) + (dot(mh, lo) + dot(ml, hi))


def blocks(x):
    n = x.shape[0] // 2
    return x[:n, :n], x[:n, n:], x[n:, :n], x[n:, n:]


def join(a, b, c, d):
    return jnp.concatenate([jnp.concatenate([a, b], 1), jnp.concatenate([c, d], 1)], 0)


def turn(x):
    a, b, c, d = blocks(x)
    return join(a, c, b, d)


def cmul(a, b):
    return a[0] * b[0] - a[1] * b[1], a[0] * b[1] + a[1] * b[0]


def conj_mul(a, b):
    return a[0] * b[0] + a[1] * b[1], a[0] * b[1] - a[1] * b[0]


def slot_masks(start, parity, n, dim):
    i = lax.broadcasted_iota(jnp.int32, (n, n), dim)
    return (1 - 2 * parity) * (i - start) - parity < 0


def gather(obj, rows, cols):
    return tuple(
        jnp.where(rows, jnp.where(cols, obj[0, 0, p], obj[0, 1, p]), jnp.where(cols, obj[1, 0, p], obj[1, 1, p]))
        for p in range(2)
    )


def pick(mask, slot, x):
    return jnp.where(mask, x, 0.0) if slot == 0 else jnp.where(mask, 0.0, x)


def valid(parity, index, size, slot, n, dim):
    i = lax.broadcasted_iota(jnp.int32, (n, n), dim)
    half = (1 - parity) if slot == 0 else parity
    low = jnp.where(jnp.logical_and(half == 0, index == 0), n // 2, 0)
    high = jnp.where(jnp.logical_and(half == 1, index == size - 1), n // 2, n)
    return jnp.logical_and(i >= low, i < high)


def where_is(info):
    return info[0], info[1], info[0] % 2, info[1] % 2


def advance(obj_in, obj_out, sums, info, sizes, first):
    ax, ay, px, py = where_is(info)
    n = obj_out.shape[-1]
    for tr in range(2):
        for tc in range(2):
            if not first:
                inside = jnp.logical_and(valid(px, ax, sizes[0], tr, n, 0), valid(py, ay, sizes[1], tc, n, 1))
            for p in range(2):
                s = sums(tr, tc, p)
                obj_out[tr, tc, p] = s if first else obj_in[tr, tc, p] - jnp.where(inside, STEP * s, 0.0)


def patch_masks(info, offsets, slot, n):
    _, _, px, py = where_is(info)
    return (
        slot_masks(offsets[slot, 0], px, n, 0),
        slot_masks(offsets[slot, 1], py, n, 1),
    )


def kernel_a(period, sizes, first, info, offsets, *refs):
    if first:
        te0, te1, to0, to1, z, probe, wave, tab, obj_out, inner = refs[0], refs[1], refs[2], refs[3], refs[4:8], *refs[8:]
        obj_in = None
    else:
        obj_in, te0, te1, to0, to1 = refs[:5]
        z, (probe, wave, tab, obj_out, inner) = refs[5:9], refs[9:]
    own = ((te0, to0), (te1, to1))
    got = ((z[0], z[2]), (z[1], z[3]))
    advance(obj_in, obj_out, lambda tr, tc, p: own[tr][tc][p] + got[tr][tc][p], info, sizes, first)
    n = obj_out.shape[-1]
    parts = []
    for m in range(BATCH):
        rows, cols = patch_masks(info, offsets, period * BATCH + m, n)
        parts += cmul((probe[m, 0], probe[m, 1]), gather(obj_out, rows, cols))
    x = left(turn(right(join(*parts), tab, 0)), tab, 0)
    a, b, c, d = blocks(x)
    q = (wave[0], wave[1])
    (ar, ai), (br, bi) = cmul((a, c), q), cmul((b, d), q)
    x = right(turn(left(join(ar, br, ai, bi), tab, 1)), tab, 1)
    inner[...] = x


def kernel_b(period, sizes, first, info, offsets, counts, *refs):
    if first:
        ue, uo, ve, vo, inner, measured, tab, obj_out, back, h0, h1 = refs
        obj_in = None
    else:
        obj_in, ue, uo, ve, vo, inner, measured, tab, obj_out, back, h0, h1 = refs
    own, got = (ue, uo), (ve, vo)
    advance(obj_in, obj_out, lambda tr, tc, p: own[tc][tr, p] + got[tc][tr, p], info, sizes, first)
    n = obj_out.shape[-1]
    masks = [patch_masks(info, offsets, period * BATCH + m, n) for m in range(BATCH)]
    a, b, c, d = blocks(inner[...])
    waves = ((a, b), (c, d))
    seconds = [gather(obj_out, *masks[m]) for m in range(BATCH)]
    parts = []
    for m in range(BATCH):
        parts += cmul(waves[m], seconds[m])
    x = left(turn(right(join(*parts), tab, 0)), tab, 0)
    a, b, c, d = blocks(x)
    e0 = a * a + c * c - measured[0]
    e1 = b * b + d * d - measured[1]
    x = right(turn(left(join(e0 * a, e1 * b, e0 * c, e1 * d), tab, 1)), tab, 1)
    a, b, c, d = blocks(x)
    back_waves = ((a, b), (c, d))
    total = [[[0.0, 0.0], [0.0, 0.0]], [[0.0, 0.0], [0.0, 0.0]]]
    for m in range(BATCH):
        live = jnp.where(period * BATCH + m < counts[0], 1.0, 0.0)
        grad = conj_mul(waves[m], back_waves[m])
        br, bi = conj_mul(seconds[m], back_waves[m])
        back[m * n : (m + 1) * n, :n] = br
        back[m * n : (m + 1) * n, n:] = bi
        rows, cols = masks[m]
        for p in range(2):
            g = grad[p] * live
            for tr in range(2):
                gr = pick(rows, tr, g)
                for tc in range(2):
                    total[tr][tc][p] = total[tr][tc][p] + pick(cols, tc, gr)
    for tc in range(2):
        for p in range(2):
            h0[tc, p] = total[0][tc][p]
            h1[tc, p] = total[1][tc][p]


def kernel_c(period, sizes, info, offsets, counts, back, probe, wave, tab, ge, go):
    n = ge.shape[-1]
    x = left(turn(right(back[...], tab, 0)), tab, 0)
    a, b, c, d = blocks(x)
    q = (wave[0], wave[1])
    (ar, ai), (br, bi) = conj_mul(q, (a, c)), conj_mul(q, (b, d))
    x = right(turn(left(join(ar, br, ai, bi), tab, 1)), tab, 1)
    a, b, c, d = blocks(x)
    waves = ((a, b), (c, d))
    total = [[[0.0, 0.0], [0.0, 0.0]], [[0.0, 0.0], [0.0, 0.0]]]
    for m in range(BATCH):
        live = jnp.where(period * BATCH + m < counts[0], 1.0, 0.0)
        grad = conj_mul((probe[m, 0], probe[m, 1]), waves[m])
        rows, cols = patch_masks(info, offsets, period * BATCH + m, n)
        for p in range(2):
            g = grad[p] * live
            for tr in range(2):
                gr = pick(rows, tr, g)
                for tc in range(2):
                    total[tr][tc][p] = total[tr][tc][p] + pick(cols, tc, gr)
    for tr in range(2):
        for p in range(2):
            ge[tr, p] = total[tr][0][p]
            go[tr, p] = total[tr][1][p]


def kernel_roll(period, offsets, probe, out):
    n = out.shape[-1]
    for m in range(BATCH):
        r = lax.rem(offsets[period * BATCH + m, 0], n)
        q = lax.rem(offsets[period * BATCH + m, 1], n)
        for p in range(2):
            out[m, p] = pltpu.roll(pltpu.roll(probe[p], r, 0), q, 1)


def kernel_place(info, tile, ge, go, h0, h1):
    _, _, px, py = where_is(info)
    n = tile.shape[-1]
    rows, cols = slot_masks(n // 2, px, n, 0), slot_masks(n // 2, py, n, 1)
    for s in range(2):
        for p in range(2):
            x = pltpu.roll(pltpu.roll(tile[s, p], n // 2, 0), n // 2, 1)
            for tr in range(2):
                for tc in range(2):
                    y = pick(cols, tc, pick(rows, tr, x))
                    if s == 0:
                        (ge, go)[tc][tr, p] = y
                    else:
                        (h0, h1)[tr][tc, p] = y


def kernel_end(sizes, info, obj0, te0, te1, to0, to1, z0, z1, z2, z3, obj1, ue, uo, ve, vo, out):
    ax, ay, px, py = where_is(info)
    n = out.shape[-1]
    rows, cols = slot_masks(n // 2, px, n, 0), slot_masks(n // 2, py, n, 1)

    def quad(mask_r, mask_c, f):
        return jnp.where(
            mask_r,
            jnp.where(mask_c, f(0, 0), f(0, 1)),
            jnp.where(mask_c, f(1, 0), f(1, 1)),
        )

    own = ((te0, to0), (te1, to1))
    got = ((z0, z2), (z1, z3))
    for p in range(2):
        a = quad(rows, cols, lambda tr, tc: obj0[tr, tc, p] - STEP * (own[tr][tc][p] + got[tr][tc][p]))
        b = quad(rows, cols, lambda tr, tc: obj1[tr, tc, p] - STEP * ((ue, uo)[tc][tr, p] + (ve, vo)[tc][tr, p]))
        for s, x in enumerate((a, b)):
            out[s, p] = pltpu.roll(pltpu.roll(x, n // 2, 0), n // 2, 1)


def kernel_fold(g, r, t0, t1):
    t0[...] = g[0] + r[0]
    t1[...] = g[1] + r[1]


def kernel_fold2(h0, h1, y0, y1, ue, uo):
    for tr, (h, y) in enumerate(((h0, y0), (h1, y1))):
        for tc, u in enumerate((ue, uo)):
            u[tr] = h[tc] + y[tc]


def call(kernel, name, scalars, arrays, outs):
    return pl.pallas_call(
        kernel,
        out_shape=[jax.ShapeDtypeStruct(s, F32) for s in outs],
        in_specs=[pl.BlockSpec(memory_space=pltpu.SMEM)] * len(scalars)
        + [pl.BlockSpec(memory_space=pltpu.VMEM)] * len(arrays),
        out_specs=[pl.BlockSpec(memory_space=pltpu.VMEM)] * len(outs),
        name=name,
        compiler_params=pltpu.CompilerParams(vmem_limit_bytes=12 * 1024 * 1024),
    )(*scalars, *arrays)


def local(object_field, probe, propagator, offsets, counts, intensity):
    n = probe.shape[1]
    sizes = (lax.axis_size("gx"), lax.axis_size("gy"))
    info = jnp.stack([lax.axis_index("gx"), lax.axis_index("gy")]).astype(jnp.int32)
    offs = offsets[0, 0]
    count = counts[0]
    tab = jnp.asarray(dft_tables(n))
    wave = jnp.stack([jnp.cos(propagator), jnp.sin(propagator)])
    pair, quad, half, block = (2, n, n), (2, 2, 2, n, n), (2, 2, n, n), (2 * n, 2 * n)

    def exchange0(ge, go):
        re, ro = swap(ge, "gy", 0), swap(go, "gy", 1)
        te = ge + re
        te0, te1 = te[0], te[1]
        z0, z1 = swap(te0, "gx", 0), swap(te1, "gx", 1)
        to = go + ro
        to0, to1 = to[0], to[1]
        z2, z3 = swap(to0, "gx", 0), swap(to1, "gx", 1)
        return te0, te1, to0, to1, z0, z1, z2, z3

    def exchange1(h0, h1):
        y0, y1 = swap(h0, "gx", 0), swap(h1, "gx", 1)
        t0, t1 = h0 + y0, h1 + y1
        ue, uo = jnp.stack([t0[0], t1[0]]), jnp.stack([t0[1], t1[1]])
        ve, vo = swap(ue, "gy", 0), swap(uo, "gy", 1)
        return ue, uo, ve, vo

    probes = [
        call(functools.partial(kernel_roll, b), "roll", [offs], [probe], [(2, 2, n, n)])[0] for b in range(NB)
    ]
    ge, go, h0, h1 = call(kernel_place, "place", [info], [object_field], [half] * 4)
    sums0 = exchange0(ge, go)
    sums1 = exchange1(h0, h1)
    obj0, obj1 = [], []
    for b in range(NB):
        first = b == 0
        out0, inner = call(
            functools.partial(kernel_a, b, sizes, first), "wave_in", [info, offs],
            [*obj0, *sums0, probes[b], wave, tab], [quad, block],
        )
        measured = intensity[0, 0, b * BATCH : (b + 1) * BATCH]
        out1, back, h0, h1 = call(
            functools.partial(kernel_b, b, sizes, first), "residual", [info, offs, count],
            [*obj1, *sums1, inner, measured, tab], [quad, block, half, half],
        )
        ge, go = call(
            functools.partial(kernel_c, b, sizes), "wave_back", [info, offs, count],
            [back, probes[b], wave, tab], [half, half],
        )
        obj0, obj1 = [out0], [out1]
        sums1 = exchange1(h0, h1)
        sums0 = exchange0(ge, go)
    (out,) = call(
        functools.partial(kernel_end, sizes), "finish", [info], [*obj0, *sums0, *obj1, *sums1], [object_field.shape]
    )
    return out


def solution(mesh):
    in_specs = (
        P(None, None, "gx", "gy"),
        P(),
        P(),
        P("gx", "gy", None, None),
        P("gx", "gy"),
        P("gx", "gy", None, None, None),
    )
    out_specs = P(None, None, "gx", "gy")
    return jax.shard_map(local, mesh=mesh, in_specs=in_specs, out_specs=out_specs, check_vma=False)
```

```python
import functools
import math

import jax
import jax.numpy as jnp
import numpy as np
from jax import lax
from jax.experimental import pallas as pl
from jax.experimental.pallas import tpu as pltpu
from jax.sharding import PartitionSpec as P

BATCH = 2
NB = 6
STEP = 0.08
F32 = jnp.float32
BF16 = jnp.bfloat16


def chip_order(size):
    chips = size // 2
    return [k if 2 * k < chips else chips // 2 + chips - 1 - k for k in range(chips)]


def both(pairs):
    return [p for i, j in pairs for p in ((i, j), (j, i))]


def swap_core(value):
    size = lax.axis_size("gy")
    return lax.ppermute(value, "gy", both([(i, i + 1) for i in range(0, size, 2)]))


def swap_cols(value):
    order = chip_order(lax.axis_size("gy"))
    return lax.ppermute(value, "gy", both([(2 * i + 1, 2 * j) for i, j in zip(order, order[1:])]))


def swap_rows(value):
    height, width = lax.axis_size("gx"), lax.axis_size("gy")
    route = [(a * width + c, (a + 1) * width + c + 1) for a in range(height - 1) for c in range(0, width, 2)]
    return lax.ppermute(value, ("gx", "gy"), both(route))


def place_tiles(value):
    order = chip_order(lax.axis_size("gy"))
    return lax.ppermute(value, "gy", [(2 * i + m, 2 * j + m) for i, j in enumerate(order) for m in range(2)])


def dft_tables(n):
    index = np.arange(n)
    phase = (index[:, None] * index[None, :] % n) * (2.0 * math.pi / n)
    c, s = np.cos(phase) / math.sqrt(n), np.sin(phase) / math.sqrt(n)
    fwd = np.block([[c, -s], [s, c]]).astype(np.float32)
    inv = np.block([[c, s], [-s, c]]).astype(np.float32)
    out = []
    for m in (fwd, inv):
        hi = m.astype(jnp.bfloat16)
        lo = (m - hi.astype(np.float32)).astype(jnp.bfloat16)
        out += [hi, lo]
    return np.stack(out)


def split(x):
    hi = x.astype(BF16)
    return hi, (x - hi.astype(F32)).astype(BF16)


def dot(a, b):
    return jnp.dot(a, b, preferred_element_type=F32)


def right(x, tab, inverse):
    hi, lo = split(x)
    mh, ml = tab[2 * inverse], tab[2 * inverse + 1]
    return dot(hi, mh) + (dot(lo, mh) + dot(hi, ml))


def left(x, tab, inverse):
    hi, lo = split(x)
    mh, ml = tab[2 - 2 * inverse], tab[3 - 2 * inverse]
    return dot(mh, hi) + (dot(mh, lo) + dot(ml, hi))


def blocks(x):
    n = x.shape[0] // 2
    return x[:n, :n], x[:n, n:], x[n:, :n], x[n:, n:]


def join(a, b, c, d):
    return jnp.concatenate([jnp.concatenate([a, b], 1), jnp.concatenate([c, d], 1)], 0)


def turn(x):
    a, b, c, d = blocks(x)
    return join(a, c, b, d)


def cmul(a, b):
    return a[0] * b[0] - a[1] * b[1], a[0] * b[1] + a[1] * b[0]


def conj_mul(a, b):
    return a[0] * b[0] + a[1] * b[1], a[0] * b[1] - a[1] * b[0]


def slot_masks(start, parity, n, dim):
    i = lax.broadcasted_iota(jnp.int32, (n, n), dim)
    return (1 - 2 * parity) * (i - start) - parity < 0


def gather(obj, rows, cols):
    return tuple(
        jnp.where(rows, jnp.where(cols, obj[0, 0, p], obj[0, 1, p]), jnp.where(cols, obj[1, 0, p], obj[1, 1, p]))
        for p in range(2)
    )


def pick(mask, slot, x):
    return jnp.where(mask, x, 0.0) if slot == 0 else jnp.where(mask, 0.0, x)


def valid(parity, index, size, slot, n, dim):
    i = lax.broadcasted_iota(jnp.int32, (n, n), dim)
    half = (1 - parity) if slot == 0 else parity
    low = jnp.where(jnp.logical_and(half == 0, index == 0), n // 2, 0)
    high = jnp.where(jnp.logical_and(half == 1, index == size - 1), n // 2, n)
    return jnp.logical_and(i >= low, i < high)


def where_is(info):
    return info[0], info[1], info[1] % 2


def advance(obj_in, obj_out, sums, info, sizes, first):
    ax, ay, core = where_is(info)
    n = obj_out.shape[-1]
    for tr in range(2):
        for tc in range(2):
            if not first:
                inside = jnp.logical_and(valid(core, ax, sizes[0], tr, n, 0), valid(core, ay, sizes[1], tc, n, 1))
            for p in range(2):
                s = sums(tr, tc, p)
                obj_out[tr, tc, p] = s if first else obj_in[tr, tc, p] - jnp.where(inside, STEP * s, 0.0)


def patch_masks(info, offsets, slot, n):
    core = where_is(info)[2]
    return slot_masks(offsets[slot, 0], core, n, 0), slot_masks(offsets[slot, 1], core, n, 1)


def slice1_sum(near, other, outer, got, tr, tc, p):
    if tc == 0:
        return (near, other)[tr][0, p]
    return outer[tr, p] + got[1 - tr, p]


def kernel_a(period, sizes, first, info, offsets, *refs):
    obj_in = None if first else refs[0]
    near, far, other, probe, wave, tab, obj_out, inner = refs[0 if first else 1 :]
    parts0 = ((near[0], far), (other[0], other[1]))
    advance(obj_in, obj_out, lambda tr, tc, p: parts0[tr][tc][p], info, sizes, first)
    n = obj_out.shape[-1]
    parts = []
    for m in range(BATCH):
        rows, cols = patch_masks(info, offsets, period * BATCH + m, n)
        parts += cmul((probe[m, 0], probe[m, 1]), gather(obj_out, rows, cols))
    x = left(turn(right(join(*parts), tab, 0)), tab, 0)
    a, b, c, d = blocks(x)
    q = (wave[0], wave[1])
    (ar, ai), (br, bi) = cmul((a, c), q), cmul((b, d), q)
    x = right(turn(left(join(ar, br, ai, bi), tab, 1)), tab, 1)
    inner[...] = x


def kernel_b(period, sizes, first, info, offsets, counts, *refs):
    obj_in = None if first else refs[0]
    near, other, outer, got, inner, measured, tab, obj_out, back, h0, h1 = refs[0 if first else 1 :]
    advance(obj_in, obj_out, lambda tr, tc, p: slice1_sum(near, other, outer, got, tr, tc, p), info, sizes, first)
    n = obj_out.shape[-1]
    masks = [patch_masks(info, offsets, period * BATCH + m, n) for m in range(BATCH)]
    a, b, c, d = blocks(inner[...])
    waves = ((a, b), (c, d))
    seconds = [gather(obj_out, *masks[m]) for m in range(BATCH)]
    parts = []
    for m in range(BATCH):
        parts += cmul(waves[m], seconds[m])
    x = left(turn(right(join(*parts), tab, 0)), tab, 0)
    a, b, c, d = blocks(x)
    e0 = a * a + c * c - measured[0]
    e1 = b * b + d * d - measured[1]
    x = right(turn(left(join(e0 * a, e1 * b, e0 * c, e1 * d), tab, 1)), tab, 1)
    a, b, c, d = blocks(x)
    back_waves = ((a, b), (c, d))
    total = [[[0.0, 0.0], [0.0, 0.0]], [[0.0, 0.0], [0.0, 0.0]]]
    for m in range(BATCH):
        live = jnp.where(period * BATCH + m < counts[0], 1.0, 0.0)
        grad = conj_mul(waves[m], back_waves[m])
        br, bi = conj_mul(seconds[m], back_waves[m])
        back[m * n : (m + 1) * n, :n] = br
        back[m * n : (m + 1) * n, n:] = bi
        rows, cols = masks[m]
        for p in range(2):
            g = grad[p] * live
            for tr in range(2):
                gr = pick(rows, tr, g)
                for tc in range(2):
                    total[tr][tc][p] = total[tr][tc][p] + pick(cols, tc, gr)
    for tc in range(2):
        for p in range(2):
            h0[tc, p] = total[0][tc][p]
            h1[tc, p] = total[1][tc][p]


def kernel_c(period, sizes, info, offsets, counts, back, probe, wave, tab, ge, go):
    n = ge.shape[-1]
    x = left(turn(right(back[...], tab, 0)), tab, 0)
    a, b, c, d = blocks(x)
    q = (wave[0], wave[1])
    (ar, ai), (br, bi) = conj_mul(q, (a, c)), conj_mul(q, (b, d))
    x = right(turn(left(join(ar, br, ai, bi), tab, 1)), tab, 1)
    a, b, c, d = blocks(x)
    waves = ((a, b), (c, d))
    total = [[[0.0, 0.0], [0.0, 0.0]], [[0.0, 0.0], [0.0, 0.0]]]
    for m in range(BATCH):
        live = jnp.where(period * BATCH + m < counts[0], 1.0, 0.0)
        grad = conj_mul((probe[m, 0], probe[m, 1]), waves[m])
        rows, cols = patch_masks(info, offsets, period * BATCH + m, n)
        for p in range(2):
            g = grad[p] * live
            for tr in range(2):
                gr = pick(rows, tr, g)
                for tc in range(2):
                    total[tr][tc][p] = total[tr][tc][p] + pick(cols, tc, gr)
    for tr in range(2):
        for p in range(2):
            ge[tr, p] = total[tr][0][p]
            go[tr, p] = total[tr][1][p]


def kernel_roll(period, offsets, probe, out):
    n = out.shape[-1]
    for m in range(BATCH):
        r = lax.rem(offsets[period * BATCH + m, 0], n)
        q = lax.rem(offsets[period * BATCH + m, 1], n)
        for p in range(2):
            out[m, p] = pltpu.roll(pltpu.roll(probe[p], r, 0), q, 1)


def kernel_place(info, s0, s1, ge, go, h0, h1):
    core = where_is(info)[2]
    n = s0.shape[-1]
    rows, cols = slot_masks(n // 2, core, n, 0), slot_masks(n // 2, core, n, 1)
    for s in range(2):
        for p in range(2):
            x = pltpu.roll(pltpu.roll((s0, s1)[s][p], n // 2, 0), n // 2, 1)
            for tr in range(2):
                for tc in range(2):
                    y = pick(cols, tc, pick(rows, tr, x))
                    if s == 0:
                        (ge, go)[tc][tr, p] = y
                    else:
                        (h0, h1)[tr][tc, p] = y


def kernel_end(info, near, far, other, obj, out):
    parts = ((near[0], far), (other[0], other[1]))
    finish(info, obj, lambda tr, tc, p: parts[tr][tc][p], out)


def kernel_end1(info, near, other, outer, got, obj, out):
    finish(info, obj, lambda tr, tc, p: slice1_sum(near, other, outer, got, tr, tc, p), out)


def finish(info, obj, sums, out):
    core = where_is(info)[2]
    n = out.shape[-1]
    rows, cols = slot_masks(n // 2, core, n, 0), slot_masks(n // 2, core, n, 1)
    for p in range(2):
        q = [[obj[tr, tc, p] - STEP * sums(tr, tc, p) for tc in range(2)] for tr in range(2)]
        x = jnp.where(rows, jnp.where(cols, q[0][0], q[0][1]), jnp.where(cols, q[1][0], q[1][1]))
        out[p] = pltpu.roll(pltpu.roll(x, n // 2, 0), n // 2, 1)


def call(kernel, name, scalars, arrays, outs):
    return pl.pallas_call(
        kernel,
        out_shape=[jax.ShapeDtypeStruct(s, F32) for s in outs],
        in_specs=[pl.BlockSpec(memory_space=pltpu.SMEM)] * len(scalars)
        + [pl.BlockSpec(memory_space=pltpu.VMEM)] * len(arrays),
        out_specs=[pl.BlockSpec(memory_space=pltpu.VMEM)] * len(outs),
        name=name,
        compiler_params=pltpu.CompilerParams(vmem_limit_bytes=12 * 1024 * 1024),
    )(*scalars, *arrays)


def exchange0(ge, go):
    re, ro = swap_core(ge), swap_cols(go)
    inner = [ge[0] + re[1], ge[1] + re[0]]
    outer = [go[0] + ro[1], go[1] + ro[0]]
    rb = swap_core(outer[1])
    y = swap_rows(jnp.stack([outer[0], inner[0], rb]))
    near = jnp.stack([inner[0] + y[1], rb + y[0]])
    far = outer[0] + y[2]
    return near, far, swap_core(near)


def exchange1(h0, h1):
    r = swap_core(h1)
    mid = h0[0] + r[0]
    y = swap_rows(jnp.stack([h0[1], mid, r[1]]))
    near = jnp.stack([mid + y[1], r[1] + y[0]])
    other = swap_core(near)
    outer = jnp.stack([h0[1] + y[2], other[1]])
    return near, other, outer, swap_cols(outer)


def local(object_field, probe, propagator, offsets, counts, intensity):
    n = probe.shape[1]
    sizes = (lax.axis_size("gx"), lax.axis_size("gy"))
    slots = offsets.shape[2]
    order = jnp.asarray(chip_order(sizes[1]), jnp.int32)
    ay = lax.axis_index("gy")
    info = jnp.stack([lax.axis_index("gx"), 2 * order[ay // 2] + ay % 2]).astype(jnp.int32)
    meta = jnp.concatenate([offsets.reshape(-1), counts.reshape(-1)]).astype(F32)
    meta = jnp.pad(meta, (0, 8 * n - meta.shape[0])).reshape(8, n)
    packed = place_tiles(jnp.concatenate([object_field[0].reshape(2 * n, n), meta]))
    tile0 = packed[: 2 * n].reshape(2, n, n)
    meta = packed[2 * n :].reshape(-1)[: 2 * slots + 1].astype(jnp.int32)
    offs, count = meta[: 2 * slots].reshape(slots, 2), meta[2 * slots :]
    tile1 = place_tiles(object_field[1])
    levels = place_tiles(intensity[0, 0])
    tab = jnp.asarray(dft_tables(n))
    wave = jnp.stack([jnp.cos(propagator), jnp.sin(propagator)])
    pair, quad, half, block = (2, n, n), (2, 2, 2, n, n), (2, 2, n, n), (2 * n, 2 * n)

    probes = [
        call(functools.partial(kernel_roll, b), "roll", [offs], [probe], [(2, 2, n, n)])[0] for b in range(NB)
    ]
    ge, go, h0, h1 = call(kernel_place, "place", [info], [tile0, tile1], [half] * 4)
    sums0 = exchange0(ge, go)
    sums1 = exchange1(h0, h1)
    obj0, obj1 = [], []
    for b in range(NB):
        first = b == 0
        out0, inner = call(
            functools.partial(kernel_a, b, sizes, first), "wave_in", [info, offs],
            [*obj0, *sums0, probes[b], wave, tab], [quad, block],
        )
        measured = levels[b * BATCH : (b + 1) * BATCH]
        out1, back, h0, h1 = call(
            functools.partial(kernel_b, b, sizes, first), "residual", [info, offs, count],
            [*obj1, *sums1, inner, measured, tab], [quad, block, half, half],
        )
        ge, go = call(
            functools.partial(kernel_c, b, sizes), "wave_back", [info, offs, count],
            [back, probes[b], wave, tab], [half, half],
        )
        obj0, obj1 = [out0], [out1]
        sums1 = exchange1(h0, h1)
        sums0 = exchange0(ge, go)
    (last1,) = call(kernel_end1, "finish1", [info], [*sums1, *obj1], [pair])
    (last0,) = call(kernel_end, "finish0", [info], [*sums0, *obj0], [pair])
    return jnp.stack([place_tiles(last0), place_tiles(last1)])


def solution(mesh):
    in_specs = (
        P(None, None, "gx", "gy"),
        P(),
        P(),
        P("gx", "gy", None, None),
        P("gx", "gy"),
        P("gx", "gy", None, None, None),
    )
    out_specs = P(None, None, "gx", "gy")
    return jax.shard_map(local, mesh=mesh, in_specs=in_specs, out_specs=out_specs, check_vma=False)
```

```python
import functools
import math

import jax
import jax.numpy as jnp
import numpy as np
from jax import lax
from jax.experimental import pallas as pl
from jax.experimental.pallas import tpu as pltpu
from jax.sharding import PartitionSpec as P

BATCH = 2
NB = 6
STEP = 0.08
F32 = jnp.float32
BF16 = jnp.bfloat16


def chip_order(size):
    chips = size // 2
    return [k if 2 * k < chips else chips // 2 + chips - 1 - k for k in range(chips)]


def both(pairs):
    return [p for i, j in pairs for p in ((i, j), (j, i))]


def swap_core(value):
    size = lax.axis_size("gy")
    return lax.ppermute(value, "gy", both([(i, i + 1) for i in range(0, size, 2)]))


def swap_cols(value):
    order = chip_order(lax.axis_size("gy"))
    return lax.ppermute(value, "gy", both([(2 * i + 1, 2 * j) for i, j in zip(order, order[1:])]))


def place_tiles(value):
    order = chip_order(lax.axis_size("gy"))
    return lax.ppermute(value, "gy", [(2 * i + m, 2 * j + m) for i, j in enumerate(order) for m in range(2)])


def column(value):
    size = lax.axis_size("gx")
    shifts = [lax.ppermute(value, "gx", [(i, (i + k) % size) for i in range(size)]) for k in range(1, size)]
    return [value, *shifts]


def dft_tables(n):
    index = np.arange(n)
    phase = (index[:, None] * index[None, :] % n) * (2.0 * math.pi / n)
    c, s = np.cos(phase) / math.sqrt(n), np.sin(phase) / math.sqrt(n)
    fwd = np.block([[c, -s], [s, c]]).astype(np.float32)
    inv = np.block([[c, s], [-s, c]]).astype(np.float32)
    out = []
    for m in (fwd, inv):
        hi = m.astype(jnp.bfloat16)
        lo = (m - hi.astype(np.float32)).astype(jnp.bfloat16)
        out += [hi, lo]
    return np.stack(out)


def split(x):
    hi = x.astype(BF16)
    return hi, (x - hi.astype(F32)).astype(BF16)


def dot(a, b):
    return jnp.dot(a, b, preferred_element_type=F32)


def right(x, tab, inverse):
    n = x[0].shape[1]
    hi, lo = split(jnp.concatenate(x, 1))
    mh, ml = tab[2 * inverse], tab[2 * inverse + 1]
    y = dot(hi, mh) + (dot(lo, mh) + dot(hi, ml))
    return y[:, :n], y[:, n:]


def left(x, tab, inverse):
    n = x[0].shape[0]
    hi, lo = split(jnp.concatenate(x, 0))
    mh, ml = tab[2 - 2 * inverse], tab[3 - 2 * inverse]
    y = dot(mh, hi) + (dot(mh, lo) + dot(ml, hi))
    return y[:n], y[n:]


def side(x):
    n = x[0].shape[1]
    return tuple(jnp.concatenate([a[i : i + n] for i in range(0, a.shape[0], n)], 1) for a in x)


def stack(x):
    n = x[0].shape[0]
    return tuple(jnp.concatenate([a[:, i : i + n] for i in range(0, a.shape[1], n)], 0) for a in x)


def cmul(a, b):
    return a[0] * b[0] - a[1] * b[1], a[0] * b[1] + a[1] * b[0]


def conj_mul(a, b):
    return a[0] * b[0] + a[1] * b[1], a[0] * b[1] - a[1] * b[0]


def iota(n, dim):
    return lax.broadcasted_iota(jnp.int32, (n, n), dim)


def slot_mask(start, core, n):
    return (1 - 2 * core) * (iota(n, 1) - start) - core < 0


def pick(mask, slot, x):
    return jnp.where(mask, x, 0.0) if slot == 0 else jnp.where(mask, 0.0, x)


def masks_of(info, offsets, sizes, j, slot, n):
    tile = info[0] - j
    tile = jnp.where(tile < 0, tile + sizes[0], tile)
    r, q = offsets[j, 2 * slot], offsets[j, 2 * slot + 1]
    i = iota(n, 0)
    upper = i >= jnp.maximum(r, jnp.where(tile == 0, n // 2, 0))
    lower = i < jnp.minimum(r, jnp.where(tile == sizes[0] - 1, n // 2, n))
    return upper, lower, slot_mask(q, info[1] % 2, n)


def gather(obj, j, masks):
    upper, lower, cols = masks
    k = (j - 1) % obj.shape[0]
    return tuple(
        jnp.where(
            upper,
            jnp.where(cols, obj[j, 0, p], obj[j, 1, p]),
            jnp.where(lower, jnp.where(cols, obj[k, 0, p], obj[k, 1, p]), 0.0),
        )
        for p in range(2)
    )


def scatter(grads, masks, tiles, k, slot, p):
    total = 0.0
    for j, half in ((k, 0), ((k + 1) % tiles, 1)):
        for m in range(BATCH):
            rows = masks[j][m][half]
            total = total + pick(masks[j][m][2], slot, jnp.where(rows, grads[j][m][p], 0.0))
    return total


def emit(grads, masks, tiles, outs, last):
    for slot, out in enumerate(outs):
        for p in range(2):
            if last:
                n = out.shape[-1]
                mine = iota(n, 0) >= n // 2
                out[p] = jnp.where(
                    mine, scatter(grads, masks, tiles, 0, slot, p), scatter(grads, masks, tiles, tiles - 1, slot, p)
                )
            else:
                for k in range(tiles):
                    out[k, p] = scatter(grads, masks, tiles, k, slot, p)


def advance(obj_in, obj_out, sums, info, sizes, first):
    tiles, n = obj_out.shape[0], obj_out.shape[-1]
    if not first:
        core, j = info[1] % 2, iota(n, 1)
        low = jnp.where(jnp.logical_and(core == 0, info[1] == 0), n // 2, 0)
        high = jnp.where(jnp.logical_and(core == 1, info[1] == sizes[1] - 1), n // 2, n)
        inside = jnp.logical_and(j >= low, j < high)
    for slot in range(2):
        own, got = sums[2 * slot], sums[2 * slot + 1]
        for k in range(tiles):
            for p in range(2):
                s = own[k, p] + got[k, p]
                if not first:
                    s = STEP * s if slot == 0 else jnp.where(inside, STEP * s, 0.0)
                    s = obj_in[k, slot, p] - s
                obj_out[k, slot, p] = s


def rows_of(x, tiles, n):
    at = lambda a, j, m: a[(j * BATCH + m) * n : (j * BATCH + m + 1) * n]
    return [[(at(x[0], j, m), at(x[1], j, m)) for m in range(BATCH)] for j in range(tiles)]


def stacked(parts):
    flat = [part for row in parts for part in row]
    return tuple(jnp.concatenate([part[p] for part in flat], 0) for p in range(2))


def tiled(wave, count):
    return tuple(jnp.concatenate([wave[p]] * count, 1) for p in range(2))


def kernel_a(period, sizes, first, info, offsets, *refs):
    obj_in = None if first else refs[0]
    *sums, probe, wave, tab, obj_out, inner = refs[0 if first else 1 :]
    advance(obj_in, obj_out, sums, info, sizes, first)
    tiles, n = obj_out.shape[0], obj_out.shape[-1]
    parts = []
    for j in range(tiles):
        parts.append([])
        for m in range(BATCH):
            patch = gather(obj_out, j, masks_of(info, offsets, sizes, j, period * BATCH + m, n))
            parts[j].append(cmul((probe[j, m, 0], probe[j, m, 1]), patch))
    x = left(side(right(stacked(parts), tab, 0)), tab, 0)
    x = left(cmul(x, tiled(wave, tiles * BATCH)), tab, 1)
    x = right(stack(x), tab, 1)
    inner[0] = x[0]
    inner[1] = x[1]


def kernel_b(period, sizes, first, last, info, offsets, counts, *refs):
    obj_in = None if first else refs[0]
    *sums, inner, measured, tab, obj_out, back, he, ho = refs[0 if first else 1 :]
    advance(obj_in, obj_out, sums, info, sizes, first)
    tiles, n = obj_out.shape[0], obj_out.shape[-1]
    masks = [[masks_of(info, offsets, sizes, j, period * BATCH + m, n) for m in range(BATCH)] for j in range(tiles)]
    seconds = [[gather(obj_out, j, masks[j][m]) for m in range(BATCH)] for j in range(tiles)]
    waves = rows_of((inner[0], inner[1]), tiles, n)
    x = stacked([[cmul(waves[j][m], seconds[j][m]) for m in range(BATCH)] for j in range(tiles)])
    x = left(side(right(x, tab, 0)), tab, 0)
    level = jnp.concatenate([measured[j, m] for j in range(tiles) for m in range(BATCH)], 1)
    e = x[0] * x[0] + x[1] * x[1] - level
    x = right(stack(left((e * x[0], e * x[1]), tab, 1)), tab, 1)
    exits = rows_of(x, tiles, n)
    y = stacked([[conj_mul(seconds[j][m], exits[j][m]) for m in range(BATCH)] for j in range(tiles)])
    back[0] = y[0]
    back[1] = y[1]
    emit(live_grads(waves, exits, counts, period), masks, tiles, (he, ho), last)


def live_grads(forward, backward, counts, period):
    grads = []
    for j, row in enumerate(forward):
        grads.append([])
        for m, wave in enumerate(row):
            live = jnp.where(period * BATCH + m < counts[j], 1.0, 0.0)
            g = conj_mul(wave, backward[j][m])
            grads[j].append((g[0] * live, g[1] * live))
    return grads


def kernel_c(period, sizes, last, info, offsets, counts, back, probe, wave, tab, ge, go):
    tiles, n = probe.shape[0], probe.shape[-1]
    masks = [[masks_of(info, offsets, sizes, j, period * BATCH + m, n) for m in range(BATCH)] for j in range(tiles)]
    x = left(side(right((back[0], back[1]), tab, 0)), tab, 0)
    x = left(conj_mul(tiled(wave, tiles * BATCH), x), tab, 1)
    waves = rows_of(right(stack(x), tab, 1), tiles, n)
    probes = [[(probe[j, m, 0], probe[j, m, 1]) for m in range(BATCH)] for j in range(tiles)]
    emit(live_grads(probes, waves, counts, period), masks, tiles, (ge, go), last)


def kernel_roll(period, offsets, probe, out):
    tiles, n = out.shape[0], out.shape[-1]
    for j in range(tiles):
        for m in range(BATCH):
            r = lax.rem(offsets[j, 2 * (period * BATCH + m)], n)
            q = lax.rem(offsets[j, 2 * (period * BATCH + m) + 1], n)
            for p in range(2):
                out[j, m, p] = pltpu.roll(pltpu.roll(probe[p], r, 0), q, 1)


def kernel_place(info, *refs):
    *tiles, pe, po = refs
    n = pe.shape[-1]
    cols = slot_mask(n // 2, info[1] % 2, n)
    mine = iota(n, 0) >= n // 2
    for p in range(2):
        rolled = [pltpu.roll(pltpu.roll(tile[p], n // 2, 0), n // 2, 1) for tile in tiles]
        for k in range(len(tiles)):
            x = jnp.where(mine, rolled[k], rolled[(k + 1) % len(tiles)])
            pe[k, p] = pick(cols, 0, x)
            po[k, p] = pick(cols, 1, x)


def kernel_end(info, obj, fe, re, fo, ro, out):
    tiles, n = obj.shape[0], obj.shape[-1]
    cols = slot_mask(n // 2, info[1] % 2, n)
    mine = iota(n, 0) >= n // 2
    for p in range(2):
        x = [jnp.where(mine, obj[0, slot, p], obj[tiles - 1, slot, p]) for slot in range(2)]
        x = jnp.where(cols, x[0] - STEP * (fe[p] + re[p]), x[1] - STEP * (fo[p] + ro[p]))
        out[p] = pltpu.roll(pltpu.roll(x, n // 2, 0), n // 2, 1)


def call(kernel, name, scalars, arrays, outs):
    return pl.pallas_call(
        kernel,
        out_shape=[jax.ShapeDtypeStruct(s, F32) for s in outs],
        in_specs=[pl.BlockSpec(memory_space=pltpu.SMEM)] * len(scalars)
        + [pl.BlockSpec(memory_space=pltpu.VMEM)] * len(arrays),
        out_specs=[pl.BlockSpec(memory_space=pltpu.VMEM)] * len(outs),
        name=name,
        compiler_params=pltpu.CompilerParams(vmem_limit_bytes=20 * 1024 * 1024),
    )(*scalars, *arrays)


def after(value, other):
    return lax.optimization_barrier((value, other))[0]


def local(object_field, probe, propagator, offsets, counts, intensity):
    n = probe.shape[1]
    sizes = (lax.axis_size("gx"), lax.axis_size("gy"))
    tiles = sizes[0]
    slots = offsets.shape[2]
    ay = lax.axis_index("gy")
    chips = sizes[1] // 2
    chip = ay // 2
    chip = jnp.where(2 * chip < chips, chip, chips // 2 + chips - 1 - chip)
    info = jnp.stack([lax.axis_index("gx"), 2 * chip + ay % 2]).astype(jnp.int32)
    meta = jnp.concatenate([offsets.reshape(-1), counts.reshape(-1)]).astype(F32)
    meta = jnp.pad(meta, (0, n - meta.shape[0])).reshape(1, n)
    meta = jnp.broadcast_to(meta, (8, n))

    packed = column(place_tiles(jnp.concatenate([object_field[0].reshape(2 * n, n), meta])))
    tiles0 = [x[: 2 * n].reshape(2, n, n) for x in packed]
    meta = jnp.stack([x[2 * n, : 2 * slots + 1] for x in packed]).astype(jnp.int32)
    offs, count = meta[:, : 2 * slots], meta[:, 2 * slots]
    tiles1 = column(place_tiles(object_field[1]))
    tab = jnp.asarray(dft_tables(n))
    wave = jnp.stack([jnp.cos(propagator), jnp.sin(propagator)])
    pair, state = (2, n, n), (tiles, 2, 2, n, n)
    half, waves = (tiles, 2, n, n), (2, tiles * BATCH * n, n)

    def levels(first, last):
        chunk = place_tiles(intensity[0, 0, first * BATCH : last * BATCH])
        return chunk

    chunks = [(0, 1), (1, 2), (2, 4), (4, NB)]
    placed = [levels(*c) for c in chunks]
    measured = {}

    def fetch(index, value):
        parts = column(value)
        first, last = chunks[index]
        for b in range(first, last):
            at = (b - first) * BATCH
            measured[b] = jnp.stack([x[at : at + BATCH] for x in parts])

    probes = [
        call(functools.partial(kernel_roll, b), "roll", [offs], [probe], [(tiles, 2, 2, n, n)])[0] for b in range(NB)
    ]
    pe, po = call(kernel_place, "place", [info], tiles0, [half] * 2)
    sums0 = [pe, swap_core(pe), po, swap_cols(po)]
    pe, po = call(kernel_place, "place", [info], tiles1, [half] * 2)
    sums1 = [pe, swap_core(pe), po, swap_cols(po)]
    fetch(0, placed[0])
    obj0, obj1 = [], []
    for b in range(NB):
        first, last = b == 0, b == NB - 1
        part = pair if last else half
        out0, inner = call(
            functools.partial(kernel_a, b, sizes, first), "wave_in", [info, offs],
            [*obj0, *sums0, probes[b], wave, tab], [state, waves],
        )
        out1, back, he, ho = call(
            functools.partial(kernel_b, b, sizes, first, last), "residual", [info, offs, count],
            [*obj1, *sums1, inner, measured[b], tab], [state, waves, part, part],
        )
        ge, go = call(
            functools.partial(kernel_c, b, sizes, last), "wave_back", [info, offs, count],
            [back, probes[b], wave, tab], [part, part],
        )
        obj0, obj1 = [out0], [out1]
        re, ro = swap_core(ge), swap_cols(go)
        sums0 = [ge, re, go, ro]
        he, ho = after((he, ho), re)
        sums1 = [he, swap_core(he), ho, swap_cols(ho)]
        if b + 1 < len(chunks):
            fetch(b + 1, after(placed[b + 1], sums1[1]))
    (last1,) = call(kernel_end, "finish", [info], [*obj1, *sums1], [pair])
    (last0,) = call(kernel_end, "finish", [info], [*obj0, *sums0], [pair])
    return jnp.stack([place_tiles(last0), place_tiles(last1)])


def solution(mesh):
    in_specs = (
        P(None, None, "gx", "gy"),
        P(),
        P(),
        P("gx", "gy", None, None),
        P("gx", "gy"),
        P("gx", "gy", None, None, None),
    )
    out_specs = P(None, None, "gx", "gy")
    return jax.shard_map(local, mesh=mesh, in_specs=in_specs, out_specs=out_specs, check_vma=False)
```

```python
import functools
import math

import jax
import jax.numpy as jnp
import numpy as np
from jax import lax
from jax.experimental import pallas as pl
from jax.experimental.pallas import tpu as pltpu
from jax.sharding import PartitionSpec as P


BATCH = 2
NB = 6
STEP = 0.08
F32 = jnp.float32
BF16 = jnp.bfloat16


def chip_order(size):
    chips = size // 2
    return [k if 2 * k < chips else chips // 2 + chips - 1 - k for k in range(chips)]


def both(pairs):
    return [p for i, j in pairs for p in ((i, j), (j, i))]


def swap_core(value):
    size = lax.axis_size("gy")
    return lax.ppermute(value, "gy", both([(i, i + 1) for i in range(0, size, 2)]))


def swap_cols(value):
    order = chip_order(lax.axis_size("gy"))
    return lax.ppermute(value, "gy", both([(2 * i + 1, 2 * j) for i, j in zip(order, order[1:])]))


def place_tiles(value):
    order = chip_order(lax.axis_size("gy"))
    return lax.ppermute(value, "gy", [(2 * i + m, 2 * j + m) for i, j in enumerate(order) for m in range(2)])


def column(value):
    size = lax.axis_size("gx")
    parts = [value]
    for k in range(1, size):
        parts.append(lax.ppermute(value, "gx", [(i, (i + k) % size) for i in range(size)]))
    return parts


def dft_tables(n):
    index = np.arange(n)
    phase = (index[:, None] * index[None, :] % n) * (2.0 * math.pi / n)
    c, s = np.cos(phase) / math.sqrt(n), np.sin(phase) / math.sqrt(n)
    fwd = np.block([[c, -s], [s, c]]).astype(np.float32)
    inv = np.block([[c, s], [-s, c]]).astype(np.float32)
    out = []
    for m in (fwd, inv):
        hi = m.astype(jnp.bfloat16)
        lo = (m - hi.astype(np.float32)).astype(jnp.bfloat16)
        out += [hi, lo]
    return np.stack(out)


def split(x):
    hi = x.astype(BF16)
    return hi, (x - hi.astype(F32)).astype(BF16)


def dot(a, b):
    return jnp.dot(a, b, preferred_element_type=F32)


def right(x, tab, inverse):
    n = x[0].shape[1]
    hi, lo = split(jnp.concatenate(x, 1))
    mh, ml = tab[2 * inverse], tab[2 * inverse + 1]
    y = dot(hi, mh) + (dot(lo, mh) + dot(hi, ml))
    return y[:, :n], y[:, n:]


def left(x, tab, inverse):
    n = x[0].shape[0]
    hi, lo = split(jnp.concatenate(x, 0))
    mh, ml = tab[2 - 2 * inverse], tab[3 - 2 * inverse]
    y = dot(mh, hi) + (dot(mh, lo) + dot(ml, hi))
    return y[:n], y[n:]


def side(x):
    n = x[0].shape[1]
    return tuple(jnp.concatenate([a[i : i + n] for i in range(0, a.shape[0], n)], 1) for a in x)


def stack(x):
    n = x[0].shape[0]
    return tuple(jnp.concatenate([a[:, i : i + n] for i in range(0, a.shape[1], n)], 0) for a in x)


def cmul(a, b):
    return a[0] * b[0] - a[1] * b[1], a[0] * b[1] + a[1] * b[0]


def conj_mul(a, b):
    return a[0] * b[0] + a[1] * b[1], a[0] * b[1] - a[1] * b[0]


def iota(n, dim):
    return lax.broadcasted_iota(jnp.int32, (n, n), dim)


def slot_mask(start, core, n):
    return (1 - 2 * core) * (iota(n, 1) - start) - core < 0


def pick(mask, slot, x):
    return jnp.where(mask, x, 0.0) if slot == 0 else jnp.where(mask, 0.0, x)


def masks_of(info, offsets, sizes, j, slot, n):
    tile = info[0] - j
    tile = jnp.where(tile < 0, tile + sizes[0], tile)
    r, q = offsets[j, 2 * slot], offsets[j, 2 * slot + 1]
    i = iota(n, 0)
    upper = i >= jnp.maximum(r, jnp.where(tile == 0, n // 2, 0))
    lower = i < jnp.minimum(r, jnp.where(tile == sizes[0] - 1, n // 2, n))
    return upper, lower, slot_mask(q, info[1] % 2, n)


def gather(obj, j, masks):
    upper, lower, cols = masks
    k = (j - 1) % obj.shape[0]
    return tuple(
        jnp.where(
            upper,
            jnp.where(cols, obj[j, 0, p], obj[j, 1, p]),
            jnp.where(lower, jnp.where(cols, obj[k, 0, p], obj[k, 1, p]), 0.0),
        )
        for p in range(2)
    )


def scatter(grads, masks, tiles, k, slot, p):
    total = 0.0
    for j, half in ((k, 0), ((k + 1) % tiles, 1)):
        for m in range(BATCH):
            rows = masks[j][m][half]
            total = total + pick(masks[j][m][2], slot, jnp.where(rows, grads[j][m][p], 0.0))
    return total


def emit(grads, masks, tiles, outs, last):
    for slot, out in enumerate(outs):
        for p in range(2):
            if last:
                n = out.shape[-1]
                mine = iota(n, 0) >= n // 2
                out[p] = jnp.where(
                    mine, scatter(grads, masks, tiles, 0, slot, p), scatter(grads, masks, tiles, tiles - 1, slot, p)
                )
            else:
                for k in range(tiles):
                    out[k, p] = scatter(grads, masks, tiles, k, slot, p)


def advance(obj_in, obj_out, sums, info, sizes, first):
    tiles, n = obj_out.shape[0], obj_out.shape[-1]
    if not first:
        core, j = info[1] % 2, iota(n, 1)
        low = jnp.where(jnp.logical_and(core == 0, info[1] == 0), n // 2, 0)
        high = jnp.where(jnp.logical_and(core == 1, info[1] == sizes[1] - 1), n // 2, n)
        inside = jnp.logical_and(j >= low, j < high)
    for slot in range(2):
        own, got = sums[2 * slot], sums[2 * slot + 1]
        for k in range(tiles):
            for p in range(2):
                s = own[k, p] + got[k, p]
                if not first:
                    s = STEP * s if slot == 0 else jnp.where(inside, STEP * s, 0.0)
                    s = obj_in[k, slot, p] - s
                obj_out[k, slot, p] = s


def rows_of(x, tiles, n):
    at = lambda a, j, m: a[(j * BATCH + m) * n : (j * BATCH + m + 1) * n]
    return [[(at(x[0], j, m), at(x[1], j, m)) for m in range(BATCH)] for j in range(tiles)]


def stacked(parts):
    flat = [part for row in parts for part in row]
    return tuple(jnp.concatenate([part[p] for part in flat], 0) for p in range(2))


def tiled(wave, count):
    return tuple(jnp.concatenate([wave[p]] * count, 1) for p in range(2))


def kernel_a(period, sizes, first, info, offsets, *refs):
    obj_in = None if first else refs[0]
    *sums, probe, wave, tab, obj_out, inner = refs[0 if first else 1 :]
    advance(obj_in, obj_out, sums, info, sizes, first)
    tiles, n = obj_out.shape[0], obj_out.shape[-1]
    parts = []
    for j in range(tiles):
        parts.append([])
        for m in range(BATCH):
            patch = gather(obj_out, j, masks_of(info, offsets, sizes, j, period * BATCH + m, n))
            parts[j].append(cmul((probe[j, m, 0], probe[j, m, 1]), patch))
    x = left(side(right(stacked(parts), tab, 0)), tab, 0)
    x = left(cmul(x, tiled(wave, tiles * BATCH)), tab, 1)
    x = right(stack(x), tab, 1)
    inner[0] = x[0]
    inner[1] = x[1]


def kernel_b(period, sizes, first, last, tiles, info, offsets, counts, *refs):
    obj_in = None if first else refs[0]
    refs = refs[0 if first else 1 :]
    sums, inner, measured = refs[:4], refs[4], refs[5 : 5 + tiles]
    tab, obj_out, back, he, ho = refs[5 + tiles :]
    advance(obj_in, obj_out, sums, info, sizes, first)
    n = obj_out.shape[-1]
    masks = [[masks_of(info, offsets, sizes, j, period * BATCH + m, n) for m in range(BATCH)] for j in range(tiles)]
    seconds = [[gather(obj_out, j, masks[j][m]) for m in range(BATCH)] for j in range(tiles)]
    waves = rows_of((inner[0], inner[1]), tiles, n)
    x = stacked([[cmul(waves[j][m], seconds[j][m]) for m in range(BATCH)] for j in range(tiles)])
    x = left(side(right(x, tab, 0)), tab, 0)
    level = jnp.concatenate([measured[j][m] for j in range(tiles) for m in range(BATCH)], 1)
    e = x[0] * x[0] + x[1] * x[1] - level
    x = right(stack(left((e * x[0], e * x[1]), tab, 1)), tab, 1)
    exits = rows_of(x, tiles, n)
    y = stacked([[conj_mul(seconds[j][m], exits[j][m]) for m in range(BATCH)] for j in range(tiles)])
    back[0] = y[0]
    back[1] = y[1]
    emit(live_grads(waves, exits, counts, period), masks, tiles, (he, ho), last)


def live_grads(forward, backward, counts, period):
    grads = []
    for j, row in enumerate(forward):
        grads.append([])
        for m, wave in enumerate(row):
            live = jnp.where(period * BATCH + m < counts[j], 1.0, 0.0)
            g = conj_mul(wave, backward[j][m])
            grads[j].append((g[0] * live, g[1] * live))
    return grads


def kernel_c(period, sizes, last, info, offsets, counts, back, probe, wave, tab, ge, go):
    tiles, n = probe.shape[0], probe.shape[-1]
    masks = [[masks_of(info, offsets, sizes, j, period * BATCH + m, n) for m in range(BATCH)] for j in range(tiles)]
    x = left(side(right((back[0], back[1]), tab, 0)), tab, 0)
    x = left(conj_mul(tiled(wave, tiles * BATCH), x), tab, 1)
    waves = rows_of(right(stack(x), tab, 1), tiles, n)
    probes = [[(probe[j, m, 0], probe[j, m, 1]) for m in range(BATCH)] for j in range(tiles)]
    emit(live_grads(probes, waves, counts, period), masks, tiles, (ge, go), last)


def kernel_roll(period, offsets, probe, out):
    tiles, n = out.shape[0], out.shape[-1]
    for j in range(tiles):
        for m in range(BATCH):
            r = lax.rem(offsets[j, 2 * (period * BATCH + m)], n)
            q = lax.rem(offsets[j, 2 * (period * BATCH + m) + 1], n)
            for p in range(2):
                out[j, m, p] = pltpu.roll(pltpu.roll(probe[p], r, 0), q, 1)


def kernel_place(info, *refs):
    *tiles, pe, po = refs
    n = pe.shape[-1]
    cols = slot_mask(n // 2, info[1] % 2, n)
    mine = iota(n, 0) >= n // 2
    for p in range(2):
        rolled = [pltpu.roll(pltpu.roll(tile[p], n // 2, 0), n // 2, 1) for tile in tiles]
        for k in range(len(tiles)):
            x = jnp.where(mine, rolled[k], rolled[(k + 1) % len(tiles)])
            pe[k, p] = pick(cols, 0, x)
            po[k, p] = pick(cols, 1, x)


def kernel_end(info, obj, fe, re, fo, ro, out):
    tiles, n = obj.shape[0], obj.shape[-1]
    cols = slot_mask(n // 2, info[1] % 2, n)
    mine = iota(n, 0) >= n // 2
    for p in range(2):
        x = [jnp.where(mine, obj[0, slot, p], obj[tiles - 1, slot, p]) for slot in range(2)]
        x = jnp.where(cols, x[0] - STEP * (fe[p] + re[p]), x[1] - STEP * (fo[p] + ro[p]))
        out[p] = pltpu.roll(pltpu.roll(x, n // 2, 0), n // 2, 1)


def call(kernel, scalars, arrays, outs):
    return pl.pallas_call(
        kernel,
        out_shape=[jax.ShapeDtypeStruct(s, F32) for s in outs],
        in_specs=[pl.BlockSpec(memory_space=pltpu.SMEM)] * len(scalars)
        + [pl.BlockSpec(memory_space=pltpu.VMEM)] * len(arrays),
        out_specs=[pl.BlockSpec(memory_space=pltpu.VMEM)] * len(outs),
        compiler_params=pltpu.CompilerParams(vmem_limit_bytes=20 * 1024 * 1024),
    )(*scalars, *arrays)


def after(value, other):
    return lax.optimization_barrier((value, other))[0]


def local(object_field, probe, propagator, offsets, counts, intensity):
    n = probe.shape[1]
    sizes = (lax.axis_size("gx"), lax.axis_size("gy"))
    tiles = sizes[0]
    slots = offsets.shape[2]
    ay = lax.axis_index("gy")
    chips = sizes[1] // 2
    chip = ay // 2
    chip = jnp.where(2 * chip < chips, chip, chips // 2 + chips - 1 - chip)
    info = jnp.stack([lax.axis_index("gx"), 2 * chip + ay % 2]).astype(jnp.int32)
    meta = jnp.concatenate([offsets.reshape(-1), counts.reshape(-1)]).astype(F32)
    meta = jnp.pad(meta, (0, n - meta.shape[0])).reshape(1, n)
    meta = jnp.broadcast_to(meta, (8, n))

    own = place_tiles(jnp.concatenate([object_field[0].reshape(2 * n, n), meta]))
    own1 = place_tiles(object_field[1])
    own2 = place_tiles(intensity[0, 0, :BATCH])
    packed = column(own)
    own3 = place_tiles(intensity[0, 0, BATCH:])
    tiles1 = column(own1)
    measured = [column(own2)]
    tiles0 = [x[: 2 * n].reshape(2, n, n) for x in packed]
    meta = jnp.stack([x[2 * n, : 2 * slots + 1] for x in packed]).astype(jnp.int32)
    offs, count = meta[:, : 2 * slots], meta[:, 2 * slots]
    tab = jnp.asarray(dft_tables(n))
    wave = jnp.stack([jnp.cos(propagator), jnp.sin(propagator)])
    pair, state = (2, n, n), (tiles, 2, 2, n, n)
    half, waves = (tiles, 2, n, n), (2, tiles * BATCH * n, n)

    def roll(b):
        return call(functools.partial(kernel_roll, b), [offs], [probe], [(tiles, 2, 2, n, n)])[0]

    def start(parts):
        pe, po = call(kernel_place, [info], parts, [half] * 2)
        ro = swap_cols(po)
        return [pe, swap_core(pe), po, ro]

    sums0 = start(tiles0)
    sums1 = start(tiles1)
    probes = [roll(0)]
    obj0, obj1 = [], []
    for b in range(NB):
        first, last = b == 0, b == NB - 1
        part = pair if last else half
        out0, inner = call(
            functools.partial(kernel_a, b, sizes, first), [info, offs],
            [*obj0, *sums0, probes[b], wave, tab], [state, waves],
        )
        if first:
            measured.append(column(after(own3[:BATCH], inner)))
        out1, back, he, ho = call(
            functools.partial(kernel_b, b, sizes, first, last, tiles), [info, offs, count],
            [*obj1, *sums1, inner, *measured[b], tab], [state, waves, part, part],
        )
        ro = swap_cols(ho)
        sums1 = [he, swap_core(he), ho, ro]
        ge, go = call(
            functools.partial(kernel_c, b, sizes, last), [info, offs, count],
            [back, probes[b], wave, tab], [part, part],
        )
        ro = swap_cols(go)
        sums0 = [ge, swap_core(ge), go, ro]
        obj0, obj1 = [out0], [out1]
        if not last:
            probes.append(roll(b + 1))
        if b + 2 < NB:
            at = (b + 1) * BATCH
            measured.append(column(own3[at : at + BATCH]))
    (last1,) = call(kernel_end, [info], [*obj1, *sums1], [pair])
    (last0,) = call(kernel_end, [info], [*obj0, *sums0], [pair])
    return jnp.stack([place_tiles(last0), place_tiles(last1)])


def solution(mesh):
    in_specs = (
        P(None, None, "gx", "gy"),
        P(),
        P(),
        P("gx", "gy", None, None),
        P("gx", "gy"),
        P("gx", "gy", None, None, None),
    )
    out_specs = P(None, None, "gx", "gy")
    return jax.shard_map(local, mesh=mesh, in_specs=in_specs, out_specs=out_specs, check_vma=False)
```

```python
import functools
import math

import jax
import jax.numpy as jnp
import numpy as np
from jax import lax
from jax.experimental import pallas as pl
from jax.experimental.pallas import tpu as pltpu
from jax.sharding import PartitionSpec as P


BATCH = 2
NB = 6
STEP = 0.08
F32 = jnp.float32
BF16 = jnp.bfloat16


def chip_order(size):
    chips = size // 2
    return [k if 2 * k < chips else chips // 2 + chips - 1 - k for k in range(chips)]


def both(pairs):
    return [p for i, j in pairs for p in ((i, j), (j, i))]


def swap_core(value):
    size = lax.axis_size("gy")
    return lax.ppermute(value, "gy", both([(i, i + 1) for i in range(0, size, 2)]))


def swap_cols(value):
    order = chip_order(lax.axis_size("gy"))
    return lax.ppermute(value, "gy", both([(2 * i + 1, 2 * j) for i, j in zip(order, order[1:])]))


def place_tiles(value):
    order = chip_order(lax.axis_size("gy"))
    return lax.ppermute(value, "gy", [(2 * i + m, 2 * j + m) for i, j in enumerate(order) for m in range(2)])


def column(value):
    size = lax.axis_size("gx")
    parts = [value]
    for k in range(1, size):
        parts.append(lax.ppermute(value, "gx", [(i, (i + k) % size) for i in range(size)]))
    return parts


def dft_tables(n):
    index = np.arange(n)
    phase = (index[:, None] * index[None, :] % n) * (2.0 * math.pi / n)
    c, s = np.cos(phase) / math.sqrt(n), np.sin(phase) / math.sqrt(n)
    fwd = np.block([[c, -s], [s, c]]).astype(np.float32)
    inv = np.block([[c, s], [-s, c]]).astype(np.float32)
    out = []
    for m in (fwd, inv):
        hi = m.astype(jnp.bfloat16)
        lo = (m - hi.astype(np.float32)).astype(jnp.bfloat16)
        out += [hi, lo]
    return np.stack(out)


def split(x):
    hi = x.astype(BF16)
    return hi, (x - hi.astype(F32)).astype(BF16)


def dot(a, b):
    return jnp.dot(a, b, preferred_element_type=F32)


def right(x, tab, inverse):
    n = x[0].shape[1]
    hi, lo = split(jnp.concatenate(x, 1))
    mh, ml = tab[2 * inverse], tab[2 * inverse + 1]
    y = dot(hi, mh) + (dot(lo, mh) + dot(hi, ml))
    return y[:, :n], y[:, n:]


def left(x, tab, inverse):
    n = x[0].shape[0]
    hi, lo = split(jnp.concatenate(x, 0))
    mh, ml = tab[2 - 2 * inverse], tab[3 - 2 * inverse]
    y = dot(mh, hi) + (dot(mh, lo) + dot(ml, hi))
    return y[:n], y[n:]


def there_and_back(x, tab, between):
    n = x.shape[2]

    def one(inverse, _):
        y = stack(left(side(right((x[0], x[1]), tab, inverse)), tab, inverse))
        x[0], x[1] = y

        @pl.when(inverse == 0)
        def _():
            lax.fori_loop(0, x.shape[1] // n, lambda s, _: between(s), None)

    lax.fori_loop(0, 2, one, None)


def at_position(s, n):
    return pl.ds(pl.multiple_of(s * n, n), n)


def load(x, s):
    rows = at_position(s, x.shape[2])
    return x[0, rows], x[1, rows]


def save(x, s, value):
    rows = at_position(s, x.shape[2])
    x[0, rows], x[1, rows] = value


def side(x):
    n = x[0].shape[1]
    return tuple(jnp.concatenate([a[i : i + n] for i in range(0, a.shape[0], n)], 1) for a in x)


def stack(x):
    n = x[0].shape[0]
    return tuple(jnp.concatenate([a[:, i : i + n] for i in range(0, a.shape[1], n)], 0) for a in x)


def cmul(a, b):
    return a[0] * b[0] - a[1] * b[1], a[0] * b[1] + a[1] * b[0]


def conj_mul(a, b):
    return a[0] * b[0] + a[1] * b[1], a[0] * b[1] - a[1] * b[0]


def iota(n, dim):
    return lax.broadcasted_iota(jnp.int32, (n, n), dim)


def slot_mask(start, core, n):
    return (1 - 2 * core) * (iota(n, 1) - start) - core < 0


def pick(mask, slot, x):
    return jnp.where(mask, x, 0.0) if slot == 0 else jnp.where(mask, 0.0, x)


def masks_of(info, offsets, sizes, j, slot, n):
    tile = info[0] - j
    tile = jnp.where(tile < 0, tile + sizes[0], tile)
    r, q = offsets[j, 2 * slot], offsets[j, 2 * slot + 1]
    i = iota(n, 0)
    upper = i >= jnp.maximum(r, jnp.where(tile == 0, n // 2, 0))
    lower = i < jnp.minimum(r, jnp.where(tile == sizes[0] - 1, n // 2, n))
    return upper, lower, slot_mask(q, info[1] % 2, n)


def gather(obj, j, masks):
    upper, lower, cols = masks
    k = jnp.where(j == 0, obj.shape[0], j) - 1
    return tuple(
        jnp.where(
            upper,
            jnp.where(cols, obj[j, 0, p], obj[j, 1, p]),
            jnp.where(lower, jnp.where(cols, obj[k, 0, p], obj[k, 1, p]), 0.0),
        )
        for p in range(2)
    )


def scatter(grads, outs, info, offsets, sizes, period, last):
    tiles, n = sizes[0], grads.shape[2]

    def block(k):
        total = [[0.0, 0.0], [0.0, 0.0]]
        for j, half in ((k, 0), (jnp.where(k == tiles - 1, 0, k + 1), 1)):
            for m in range(BATCH):
                masks = masks_of(info, offsets, sizes, j, period * BATCH + m, n)
                grad = load(grads, j * BATCH + m)
                for p in range(2):
                    g = jnp.where(masks[half], grad[p], 0.0)
                    for slot in range(2):
                        total[slot][p] = total[slot][p] + pick(masks[2], slot, g)
        return total

    if last:
        first, final = block(0), block(tiles - 1)
        mine = iota(n, 0) >= n // 2
        for slot in range(2):
            for p in range(2):
                outs[slot][p] = jnp.where(mine, first[slot][p], final[slot][p])
        return

    def write(k, _):
        total = block(k)
        for slot in range(2):
            for p in range(2):
                outs[slot][k, p] = total[slot][p]

    lax.fori_loop(0, tiles, write, None)


def advance(obj_in, obj_out, sums, info, sizes, step):
    tiles, n = obj_out.shape[0], obj_out.shape[-1]

    def block(k, _):
        core, j = info[1] % 2, iota(n, 1)
        low = jnp.where(jnp.logical_and(core == 0, info[1] == 0), n // 2, 0)
        high = jnp.where(jnp.logical_and(core == 1, info[1] == sizes[1] - 1), n // 2, n)
        inside = jnp.logical_and(j >= low, j < high)
        for slot in range(2):
            own, got = sums[2 * slot], sums[2 * slot + 1]
            for p in range(2):
                s = own[k, p] + got[k, p]
                if obj_in is not None:
                    s = step * s if slot == 0 else jnp.where(inside, step * s, 0.0)
                    s = obj_in[k, slot, p] - s
                obj_out[k, slot, p] = s

    lax.fori_loop(0, tiles, block, None)


def kernel_a(sizes, first, info, offsets, at, *refs):
    period = at[0]
    obj_in = None if first else refs[0]
    *sums, probe, wave, tab, obj_out, inner = refs[0 if first else 1 :]
    advance(obj_in, obj_out, sums, info, sizes, STEP)
    n = obj_out.shape[-1]

    def enter(j, _):
        for m in range(BATCH):
            patch = gather(obj_out, j, masks_of(info, offsets, sizes, j, period * BATCH + m, n))
            save(inner, j * BATCH + m, cmul((probe[j, m, 0], probe[j, m, 1]), patch))

    lax.fori_loop(0, sizes[0], enter, None)
    there_and_back(inner, tab, lambda s: save(inner, s, cmul(load(inner, s), (wave[0], wave[1]))))


def kernel_b(sizes, last, tiles, info, offsets, counts, at, step, obj_in, *refs):
    period = at[0]
    sums, inner, measured = refs[:4], refs[4], refs[5 : 5 + tiles]
    tab, obj_out, back, he, ho, level, kept = refs[5 + tiles :]
    advance(obj_in, obj_out, sums, info, sizes, step[0])
    n = obj_out.shape[-1]
    for j in range(tiles):
        for m in range(BATCH):
            level[j * BATCH + m] = measured[j][m]

    def enter(j, _):
        for m in range(BATCH):
            s = j * BATCH + m
            patch = gather(obj_out, j, masks_of(info, offsets, sizes, j, period * BATCH + m, n))
            save(kept, s, patch)
            save(back, s, cmul(load(inner, s), patch))

    def residual(s):
        a, b = load(back, s)
        e = a * a + b * b - level[s]
        save(back, s, (e * a, e * b))

    def leave(j, _):
        for m in range(BATCH):
            s = j * BATCH + m
            x = load(back, s)
            save(back, s, conj_mul(load(kept, s), x))
            live = jnp.where(period * BATCH + m < counts[j], 1.0, 0.0)
            g = conj_mul(load(inner, s), x)
            save(kept, s, (g[0] * live, g[1] * live))

    lax.fori_loop(0, tiles, enter, None)
    there_and_back(back, tab, residual)
    lax.fori_loop(0, tiles, leave, None)
    scatter(kept, (he, ho), info, offsets, sizes, period, last)


def kernel_c(sizes, last, info, offsets, counts, at, back, probe, wave, tab, ge, go, x):
    period = at[0]
    x[...] = back[...]
    there_and_back(x, tab, lambda s: save(x, s, conj_mul((wave[0], wave[1]), load(x, s))))

    def leave(j, _):
        for m in range(BATCH):
            s = j * BATCH + m
            live = jnp.where(period * BATCH + m < counts[j], 1.0, 0.0)
            g = conj_mul((probe[j, m, 0], probe[j, m, 1]), load(x, s))
            save(x, s, (g[0] * live, g[1] * live))

    lax.fori_loop(0, sizes[0], leave, None)
    scatter(x, (ge, go), info, offsets, sizes, period, last)


def kernel_roll(offsets, at, probe, out):
    period = at[0]
    tiles, n = out.shape[0], out.shape[-1]
    for j in range(tiles):
        for m in range(BATCH):
            r = lax.rem(offsets[j, 2 * (period * BATCH + m)], n)
            q = lax.rem(offsets[j, 2 * (period * BATCH + m) + 1], n)
            for p in range(2):
                out[j, m, p] = pltpu.roll(pltpu.roll(probe[p], r, 0), q, 1)


def kernel_place(info, *refs):
    *tiles, pe, po = refs
    n = pe.shape[-1]
    cols = slot_mask(n // 2, info[1] % 2, n)
    mine = iota(n, 0) >= n // 2
    for p in range(2):
        rolled = [pltpu.roll(pltpu.roll(tile[p], n // 2, 0), n // 2, 1) for tile in tiles]
        for k in range(len(tiles)):
            x = jnp.where(mine, rolled[k], rolled[(k + 1) % len(tiles)])
            pe[k, p] = pick(cols, 0, x)
            po[k, p] = pick(cols, 1, x)


def kernel_end(info, obj, fe, re, fo, ro, out):
    tiles, n = obj.shape[0], obj.shape[-1]
    cols = slot_mask(n // 2, info[1] % 2, n)
    mine = iota(n, 0) >= n // 2
    for p in range(2):
        x = [jnp.where(mine, obj[0, slot, p], obj[tiles - 1, slot, p]) for slot in range(2)]
        x = jnp.where(cols, x[0] - STEP * (fe[p] + re[p]), x[1] - STEP * (fo[p] + ro[p]))
        out[p] = pltpu.roll(pltpu.roll(x, n // 2, 0), n // 2, 1)


def call(kernel, scalars, arrays, outs, scratch=()):
    return pl.pallas_call(
        kernel,
        out_shape=[jax.ShapeDtypeStruct(s, F32) for s in outs],
        in_specs=[pl.BlockSpec(memory_space=pltpu.SMEM)] * len(scalars)
        + [pl.BlockSpec(memory_space=pltpu.VMEM)] * len(arrays),
        out_specs=[pl.BlockSpec(memory_space=pltpu.VMEM)] * len(outs),
        scratch_shapes=[pltpu.VMEM(x, F32) for x in scratch],
        compiler_params=pltpu.CompilerParams(vmem_limit_bytes=20 * 1024 * 1024),
    )(*scalars, *arrays)


def after(value, other):
    return lax.optimization_barrier((value, other))[0]


def local(object_field, probe, propagator, offsets, counts, intensity):
    n = probe.shape[1]
    sizes = (lax.axis_size("gx"), lax.axis_size("gy"))
    tiles = sizes[0]
    slots = offsets.shape[2]
    ay = lax.axis_index("gy")
    chips = sizes[1] // 2
    chip = ay // 2
    chip = jnp.where(2 * chip < chips, chip, chips // 2 + chips - 1 - chip)
    info = jnp.stack([lax.axis_index("gx"), 2 * chip + ay % 2]).astype(jnp.int32)
    meta = jnp.concatenate([offsets.reshape(-1), counts.reshape(-1)]).astype(F32)
    meta = jnp.pad(meta, (0, n - meta.shape[0])).reshape(1, n)
    meta = jnp.broadcast_to(meta, (8, n))

    own = place_tiles(jnp.concatenate([object_field[0].reshape(2 * n, n), meta]))
    own1 = place_tiles(object_field[1])
    own2 = place_tiles(intensity[0, 0, :BATCH])
    packed = column(own)
    own3 = place_tiles(intensity[0, 0, BATCH:])
    tiles1 = column(own1)
    measured = [column(own2)]
    tiles0 = [x[: 2 * n].reshape(2, n, n) for x in packed]
    meta = jnp.stack([x[2 * n, : 2 * slots + 1] for x in packed]).astype(jnp.int32)
    offs, count = meta[:, : 2 * slots], meta[:, 2 * slots]
    tab = jnp.asarray(dft_tables(n))
    wave = jnp.stack([jnp.cos(propagator), jnp.sin(propagator)])
    pair, state = (2, n, n), (tiles, 2, 2, n, n)
    half, waves = (tiles, 2, n, n), (2, tiles * BATCH * n, n)

    def at(b):
        return jnp.full((1,), b, jnp.int32)

    def roll(b):
        return call(kernel_roll, [offs, at(b)], [probe], [(tiles, 2, 2, n, n)])[0]

    def forward(b, obj, sums, probes):
        first = obj is None
        return call(
            functools.partial(kernel_a, sizes, first), [info, offs, at(b)],
            [*([] if first else [obj]), *sums, probes, wave, tab], [state, waves],
        )

    def backward(b, obj, sums, step, inner, measured, probes, last):
        part = pair if last else half
        obj, back, he, ho = call(
            functools.partial(kernel_b, sizes, last, tiles), [info, offs, count, at(b), step],
            [obj, *sums, inner, *measured, tab], [state, waves, part, part], [(tiles * BATCH, n, n), waves],
        )
        ge, go = call(
            functools.partial(kernel_c, sizes, last), [info, offs, count, at(b)],
            [back, probes, wave, tab], [part, part], [waves],
        )
        return obj, he, ho, ge, go

    def start(parts):
        pe, po = call(kernel_place, [info], parts, [half] * 2)
        ro = swap_cols(po)
        return [pe, swap_core(pe), po, ro]

    sums0 = start(tiles0)
    sums1 = start(tiles1)
    probes = roll(0)
    obj0, inner = forward(0, None, sums0, probes)

    def round_of(b, carry):
        obj0, obj1, sums1, step, inner, measured, probes = carry
        if b == 0:
            measured = [*measured, column(after(own3[:BATCH], inner))]
        obj1, he, ho, ge, go = backward(b, obj1, sums1, step, inner, measured[0], probes, False)
        ro = swap_cols(go)
        sums0 = [ge, swap_core(ge), go, ro]
        later = measured[1:]
        if b + 2 < NB:
            later = [*later, column(own3[(b + 1) * BATCH : (b + 2) * BATCH])]
        he, ho = after((he, ho), ge)
        ro = swap_cols(ho)
        sums1 = [he, swap_core(he), ho, ro]
        probes = roll(b + 1)
        obj0, inner = forward(b + 1, obj0, sums0, probes)
        return obj0, obj1, sums1, jnp.full((1,), STEP, F32), inner, later, probes

    carry = (obj0, jnp.zeros(state, F32), sums1, jnp.full((1,), -1.0, F32), inner, measured, probes)
    for b in range(NB - 1):
        carry = round_of(b, carry)
    obj0, obj1, sums1, step, inner, measured, probes = carry
    obj1, he, ho, ge, go = backward(NB - 1, obj1, sums1, step, inner, measured[0], probes, True)
    ro = swap_cols(go)
    sums0 = [ge, swap_core(ge), go, ro]
    he, ho = after((he, ho), ge)
    ro = swap_cols(ho)
    sums1 = [he, swap_core(he), ho, ro]
    (last0,) = call(kernel_end, [info], [obj0, *sums0], [pair])
    (last1,) = call(kernel_end, [info], [obj1, *sums1], [pair])
    return jnp.stack([place_tiles(last0), place_tiles(last1)])


def solution(mesh):
    in_specs = (
        P(None, None, "gx", "gy"),
        P(),
        P(),
        P("gx", "gy", None, None),
        P("gx", "gy"),
        P("gx", "gy", None, None, None),
    )
    out_specs = P(None, None, "gx", "gy")
    return jax.shard_map(local, mesh=mesh, in_specs=in_specs, out_specs=out_specs, check_vma=False)
```

```python
import functools
import math

import jax
import jax.numpy as jnp
import numpy as np
from jax import lax
from jax.experimental import pallas as pl
from jax.experimental.pallas import tpu as pltpu
from jax.sharding import PartitionSpec as P


BATCH = 2
NB = 6
STEP = 0.08
F32 = jnp.float32
BF16 = jnp.bfloat16


def chip_order(size):
    chips = size // 2
    return [k if 2 * k < chips else chips // 2 + chips - 1 - k for k in range(chips)]


def both(pairs):
    return [p for i, j in pairs for p in ((i, j), (j, i))]


def swap_core(value):
    size = lax.axis_size("gy")
    return lax.ppermute(value, "gy", both([(i, i + 1) for i in range(0, size, 2)]))


def swap_cols(value):
    order = chip_order(lax.axis_size("gy"))
    return lax.ppermute(value, "gy", both([(2 * i + 1, 2 * j) for i, j in zip(order, order[1:])]))


def place_tiles(value):
    order = chip_order(lax.axis_size("gy"))
    return lax.ppermute(value, "gy", [(2 * i + m, 2 * j + m) for i, j in enumerate(order) for m in range(2)])


def column(value):
    size = lax.axis_size("gx")
    parts = [value]
    for k in range(1, size):
        parts.append(lax.ppermute(value, "gx", [(i, (i + k) % size) for i in range(size)]))
    return parts


def dft_tables(n):
    index = np.arange(n)
    phase = (index[:, None] * index[None, :] % n) * (2.0 * math.pi / n)
    c, s = np.cos(phase) / math.sqrt(n), np.sin(phase) / math.sqrt(n)
    fwd = np.block([[c, -s], [s, c]]).astype(np.float32)
    inv = np.block([[c, s], [-s, c]]).astype(np.float32)
    out = []
    for m in (fwd, inv):
        hi = m.astype(jnp.bfloat16)
        lo = (m - hi.astype(np.float32)).astype(jnp.bfloat16)
        out += [hi, lo]
    return np.stack(out)


def split(x):
    hi = x.astype(BF16)
    return hi, (x - hi.astype(F32)).astype(BF16)


def dot(a, b):
    return jnp.dot(a, b, preferred_element_type=F32)


def right(x, tab, inverse):
    n = x[0].shape[1]
    hi, lo = split(jnp.concatenate(x, 1))
    mh, ml = tab[2 * inverse], tab[2 * inverse + 1]
    y = dot(hi, mh) + (dot(lo, mh) + dot(hi, ml))
    return y[:, :n], y[:, n:]


def left(x, tab, inverse):
    n = x[0].shape[0]
    hi, lo = split(jnp.concatenate(x, 0))
    mh, ml = tab[2 - 2 * inverse], tab[3 - 2 * inverse]
    y = dot(mh, hi) + (dot(mh, lo) + dot(ml, hi))
    return y[:n], y[n:]


def side(x):
    n = x[0].shape[1]
    return tuple(jnp.concatenate([a[i : i + n] for i in range(0, a.shape[0], n)], 1) for a in x)


def stack(x):
    n = x[0].shape[0]
    return tuple(jnp.concatenate([a[:, i : i + n] for i in range(0, a.shape[1], n)], 0) for a in x)


def cmul(a, b):
    return a[0] * b[0] - a[1] * b[1], a[0] * b[1] + a[1] * b[0]


def conj_mul(a, b):
    return a[0] * b[0] + a[1] * b[1], a[0] * b[1] - a[1] * b[0]


def iota(n, dim):
    return lax.broadcasted_iota(jnp.int32, (n, n), dim)


def slot_mask(start, core, n):
    return (1 - 2 * core) * (iota(n, 1) - start) - core < 0


def pick(mask, slot, x):
    return jnp.where(mask, x, 0.0) if slot == 0 else jnp.where(mask, 0.0, x)


def masks_of(info, offsets, sizes, j, slot, n):
    tile = info[0] - j
    tile = jnp.where(tile < 0, tile + sizes[0], tile)
    r, q = offsets[j, 2 * slot], offsets[j, 2 * slot + 1]
    i = iota(n, 0)
    upper = i >= jnp.maximum(r, jnp.where(tile == 0, n // 2, 0))
    lower = i < jnp.minimum(r, jnp.where(tile == sizes[0] - 1, n // 2, n))
    return upper, lower, slot_mask(q, info[1] % 2, n)


def gather(obj, j, masks):
    upper, lower, cols = masks
    k = (j - 1) % obj.shape[0]
    return tuple(
        jnp.where(
            upper,
            jnp.where(cols, obj[j, 0, p], obj[j, 1, p]),
            jnp.where(lower, jnp.where(cols, obj[k, 0, p], obj[k, 1, p]), 0.0),
        )
        for p in range(2)
    )


def scatter(grads, masks, tiles, k, slot, p):
    total = 0.0
    for j, half in ((k, 0), ((k + 1) % tiles, 1)):
        for m in range(BATCH):
            rows = masks[j][m][half]
            total = total + pick(masks[j][m][2], slot, jnp.where(rows, grads[j][m][p], 0.0))
    return total


def emit(grads, masks, tiles, outs, last):
    for slot, out in enumerate(outs):
        for p in range(2):
            if last:
                n = out.shape[-1]
                mine = iota(n, 0) >= n // 2
                out[p] = jnp.where(
                    mine, scatter(grads, masks, tiles, 0, slot, p), scatter(grads, masks, tiles, tiles - 1, slot, p)
                )
            else:
                for k in range(tiles):
                    out[k, p] = scatter(grads, masks, tiles, k, slot, p)


def advance(obj_in, obj_out, sums, info, sizes, first):
    tiles, n = obj_out.shape[0], obj_out.shape[-1]
    if not first:
        core, j = info[1] % 2, iota(n, 1)
        low = jnp.where(jnp.logical_and(core == 0, info[1] == 0), n // 2, 0)
        high = jnp.where(jnp.logical_and(core == 1, info[1] == sizes[1] - 1), n // 2, n)
        inside = jnp.logical_and(j >= low, j < high)
    for slot in range(2):
        own, got = sums[2 * slot], sums[2 * slot + 1]
        for k in range(tiles):
            for p in range(2):
                s = own[k, p] + got[k, p]
                if not first:
                    s = STEP * s if slot == 0 else jnp.where(inside, STEP * s, 0.0)
                    s = obj_in[k, slot, p] - s
                obj_out[k, slot, p] = s


def rows_of(x, tiles, n):
    at = lambda a, j, m: a[(j * BATCH + m) * n : (j * BATCH + m + 1) * n]
    return [[(at(x[0], j, m), at(x[1], j, m)) for m in range(BATCH)] for j in range(tiles)]


def stacked(parts):
    flat = [part for row in parts for part in row]
    return tuple(jnp.concatenate([part[p] for part in flat], 0) for p in range(2))


def tiled(wave, count):
    return tuple(jnp.concatenate([wave[p]] * count, 1) for p in range(2))


def kernel_a(period, sizes, first, info, offsets, *refs):
    obj_in = None if first else refs[0]
    *sums, probe, wave, tab, obj_out, inner = refs[0 if first else 1 :]
    advance(obj_in, obj_out, sums, info, sizes, first)
    tiles, n = obj_out.shape[0], obj_out.shape[-1]
    parts = []
    for j in range(tiles):
        parts.append([])
        for m in range(BATCH):
            patch = gather(obj_out, j, masks_of(info, offsets, sizes, j, period * BATCH + m, n))
            parts[j].append(cmul((probe[j, m, 0], probe[j, m, 1]), patch))
    x = left(side(right(stacked(parts), tab, 0)), tab, 0)
    x = left(cmul(x, tiled(wave, tiles * BATCH)), tab, 1)
    x = right(stack(x), tab, 1)
    inner[0] = x[0]
    inner[1] = x[1]


def kernel_b(period, sizes, first, last, tiles, info, offsets, counts, *refs):
    obj_in = None if first else refs[0]
    refs = refs[0 if first else 1 :]
    sums, inner, measured = refs[:4], refs[4], refs[5 : 5 + tiles]
    probe, wave, tab, obj_out, ge, go, he, ho = refs[5 + tiles :]
    advance(obj_in, obj_out, sums, info, sizes, first)
    n = obj_out.shape[-1]
    masks = [[masks_of(info, offsets, sizes, j, period * BATCH + m, n) for m in range(BATCH)] for j in range(tiles)]
    seconds = [[gather(obj_out, j, masks[j][m]) for m in range(BATCH)] for j in range(tiles)]
    waves = rows_of((inner[0], inner[1]), tiles, n)
    x = stacked([[cmul(waves[j][m], seconds[j][m]) for m in range(BATCH)] for j in range(tiles)])
    x = left(side(right(x, tab, 0)), tab, 0)
    level = jnp.concatenate([measured[j][m] for j in range(tiles) for m in range(BATCH)], 1)
    e = x[0] * x[0] + x[1] * x[1] - level
    x = right(stack(left((e * x[0], e * x[1]), tab, 1)), tab, 1)
    exits = rows_of(x, tiles, n)
    x = stacked([[conj_mul(seconds[j][m], exits[j][m]) for m in range(BATCH)] for j in range(tiles)])
    x = left(side(right(x, tab, 0)), tab, 0)
    emit(live_grads(waves, exits, counts, period), masks, tiles, (he, ho), last)
    x = left(conj_mul(tiled(wave, tiles * BATCH), x), tab, 1)
    exits = rows_of(right(stack(x), tab, 1), tiles, n)
    probes = [[(probe[j, m, 0], probe[j, m, 1]) for m in range(BATCH)] for j in range(tiles)]
    emit(live_grads(probes, exits, counts, period), masks, tiles, (ge, go), last)


def live_grads(forward, backward, counts, period):
    grads = []
    for j, row in enumerate(forward):
        grads.append([])
        for m, wave in enumerate(row):
            live = jnp.where(period * BATCH + m < counts[j], 1.0, 0.0)
            g = conj_mul(wave, backward[j][m])
            grads[j].append((g[0] * live, g[1] * live))
    return grads


def kernel_roll(period, offsets, probe, out):
    tiles, n = out.shape[0], out.shape[-1]
    for j in range(tiles):
        for m in range(BATCH):
            r = lax.rem(offsets[j, 2 * (period * BATCH + m)], n)
            q = lax.rem(offsets[j, 2 * (period * BATCH + m) + 1], n)
            for p in range(2):
                out[j, m, p] = pltpu.roll(pltpu.roll(probe[p], r, 0), q, 1)


def kernel_place(info, *refs):
    *tiles, pe, po = refs
    n = pe.shape[-1]
    cols = slot_mask(n // 2, info[1] % 2, n)
    mine = iota(n, 0) >= n // 2
    for p in range(2):
        rolled = [pltpu.roll(pltpu.roll(tile[p], n // 2, 0), n // 2, 1) for tile in tiles]
        for k in range(len(tiles)):
            x = jnp.where(mine, rolled[k], rolled[(k + 1) % len(tiles)])
            pe[k, p] = pick(cols, 0, x)
            po[k, p] = pick(cols, 1, x)


def kernel_end(info, obj, fe, re, fo, ro, out):
    tiles, n = obj.shape[0], obj.shape[-1]
    cols = slot_mask(n // 2, info[1] % 2, n)
    mine = iota(n, 0) >= n // 2
    for p in range(2):
        x = [jnp.where(mine, obj[0, slot, p], obj[tiles - 1, slot, p]) for slot in range(2)]
        x = jnp.where(cols, x[0] - STEP * (fe[p] + re[p]), x[1] - STEP * (fo[p] + ro[p]))
        out[p] = pltpu.roll(pltpu.roll(x, n // 2, 0), n // 2, 1)


def call(kernel, scalars, arrays, outs):
    return pl.pallas_call(
        kernel,
        out_shape=[jax.ShapeDtypeStruct(s, F32) for s in outs],
        in_specs=[pl.BlockSpec(memory_space=pltpu.SMEM)] * len(scalars)
        + [pl.BlockSpec(memory_space=pltpu.VMEM)] * len(arrays),
        out_specs=[pl.BlockSpec(memory_space=pltpu.VMEM)] * len(outs),
        compiler_params=pltpu.CompilerParams(vmem_limit_bytes=24 * 1024 * 1024),
    )(*scalars, *arrays)


def after(value, other):
    return lax.optimization_barrier((value, other))[0]


def local(object_field, probe, propagator, offsets, counts, intensity):
    n = probe.shape[1]
    sizes = (lax.axis_size("gx"), lax.axis_size("gy"))
    tiles = sizes[0]
    slots = offsets.shape[2]
    ay = lax.axis_index("gy")
    chips = sizes[1] // 2
    chip = ay // 2
    chip = jnp.where(2 * chip < chips, chip, chips // 2 + chips - 1 - chip)
    info = jnp.stack([lax.axis_index("gx"), 2 * chip + ay % 2]).astype(jnp.int32)
    meta = jnp.concatenate([offsets.reshape(-1), counts.reshape(-1)]).astype(F32)
    meta = jnp.pad(meta, (0, n - meta.shape[0])).reshape(1, n)
    meta = jnp.broadcast_to(meta, (8, n))

    own = place_tiles(jnp.concatenate([object_field[0].reshape(2 * n, n), meta]))
    own1 = place_tiles(object_field[1])
    own2 = place_tiles(intensity[0, 0, :BATCH])
    packed = column(own)
    own3 = place_tiles(intensity[0, 0, BATCH:])
    tiles1 = column(own1)
    measured = [column(own2)]
    tiles0 = [x[: 2 * n].reshape(2, n, n) for x in packed]
    meta = jnp.stack([x[2 * n, : 2 * slots + 1] for x in packed]).astype(jnp.int32)
    offs, count = meta[:, : 2 * slots], meta[:, 2 * slots]
    tab = jnp.asarray(dft_tables(n))
    wave = jnp.stack([jnp.cos(propagator), jnp.sin(propagator)])
    pair, state = (2, n, n), (tiles, 2, 2, n, n)
    half, waves = (tiles, 2, n, n), (2, tiles * BATCH * n, n)

    def roll(b):
        return call(functools.partial(kernel_roll, b), [offs], [probe], [(tiles, 2, 2, n, n)])[0]

    def start(parts):
        pe, po = call(kernel_place, [info], parts, [half] * 2)
        ro = swap_cols(po)
        return [pe, swap_core(pe), po, ro]

    sums0 = start(tiles0)
    sums1 = start(tiles1)
    probes = [roll(0)]
    obj0, obj1 = [], []
    for b in range(NB):
        first, last = b == 0, b == NB - 1
        part = pair if last else half
        out0, inner = call(
            functools.partial(kernel_a, b, sizes, first), [info, offs],
            [*obj0, *sums0, probes[b], wave, tab], [state, waves],
        )
        if first:
            measured.append(column(after(own3[:BATCH], inner)))
        out1, ge, go, he, ho = call(
            functools.partial(kernel_b, b, sizes, first, last, tiles), [info, offs, count],
            [*obj1, *sums1, inner, *measured[b], probes[b], wave, tab], [state, part, part, part, part],
        )
        obj0, obj1 = [out0], [out1]
        ro = swap_cols(go)
        sums0 = [ge, swap_core(ge), go, ro]
        ro = swap_cols(ho)
        sums1 = [he, swap_core(he), ho, ro]
        if not last:
            probes.append(roll(b + 1))
        if b % 2 == 0 and b + 2 < NB:
            pieces = column(own3[(b + 1) * BATCH : (b + 3) * BATCH])
            measured += [[x[i * BATCH : (i + 1) * BATCH] for x in pieces] for i in range(2)]
    (last1,) = call(kernel_end, [info], [*obj1, *sums1], [pair])
    (last0,) = call(kernel_end, [info], [*obj0, *sums0], [pair])
    return jnp.stack([place_tiles(last0), place_tiles(last1)])


def solution(mesh):
    in_specs = (
        P(None, None, "gx", "gy"),
        P(),
        P(),
        P("gx", "gy", None, None),
        P("gx", "gy"),
        P("gx", "gy", None, None, None),
    )
    out_specs = P(None, None, "gx", "gy")
    return jax.shard_map(local, mesh=mesh, in_specs=in_specs, out_specs=out_specs, check_vma=False)
```

```python
import functools
import math

import jax
import jax.numpy as jnp
import numpy as np
from jax import lax
from jax.experimental import pallas as pl
from jax.experimental.pallas import tpu as pltpu
from jax.sharding import PartitionSpec as P


BATCH = 2
NB = 6
STEP = 0.08
F32 = jnp.float32
BF16 = jnp.bfloat16


def chip_order(size):
    chips = size // 2
    return [k if 2 * k < chips else chips // 2 + chips - 1 - k for k in range(chips)]


def both(pairs):
    return [p for i, j in pairs for p in ((i, j), (j, i))]


def swap_core(value):
    size = lax.axis_size("gy")
    return lax.ppermute(value, "gy", both([(i, i + 1) for i in range(0, size, 2)]))


def swap_cols(value):
    order = chip_order(lax.axis_size("gy"))
    return lax.ppermute(value, "gy", both([(2 * i + 1, 2 * j) for i, j in zip(order, order[1:])]))


def place_tiles(value):
    order = chip_order(lax.axis_size("gy"))
    return lax.ppermute(value, "gy", [(2 * i + m, 2 * j + m) for i, j in enumerate(order) for m in range(2)])


def column(value):
    size = lax.axis_size("gx")
    parts = [value]
    for k in range(1, size):
        parts.append(lax.ppermute(value, "gx", [(i, (i + k) % size) for i in range(size)]))
    return parts


def dft_tables(n):
    index = np.arange(n)
    phase = (index[:, None] * index[None, :] % n) * (2.0 * math.pi / n)
    c, s = np.cos(phase) / math.sqrt(n), np.sin(phase) / math.sqrt(n)
    fwd = np.block([[c, -s], [s, c]]).astype(np.float32)
    inv = np.block([[c, s], [-s, c]]).astype(np.float32)
    out = []
    for m in (fwd, inv):
        hi = m.astype(jnp.bfloat16)
        lo = (m - hi.astype(np.float32)).astype(jnp.bfloat16)
        out += [hi, lo]
    return np.stack(out)


def split(x):
    hi = x.astype(BF16)
    return hi, (x - hi.astype(F32)).astype(BF16)


def dot(a, b):
    return jnp.dot(a, b, preferred_element_type=F32)


def right(x, tab, inverse):
    n = x[0].shape[1]
    hi, lo = split(jnp.concatenate(x, 1))
    mh, ml = tab[2 * inverse], tab[2 * inverse + 1]
    y = dot(hi, mh) + (dot(lo, mh) + dot(hi, ml))
    return y[:, :n], y[:, n:]


def left(x, tab, inverse):
    n = x[0].shape[0]
    hi, lo = split(jnp.concatenate(x, 0))
    mh, ml = tab[2 - 2 * inverse], tab[3 - 2 * inverse]
    y = dot(mh, hi) + (dot(mh, lo) + dot(ml, hi))
    return y[:n], y[n:]


def side(x):
    n = x[0].shape[1]
    return tuple(jnp.concatenate([a[i : i + n] for i in range(0, a.shape[0], n)], 1) for a in x)


def stack(x):
    n = x[0].shape[0]
    return tuple(jnp.concatenate([a[:, i : i + n] for i in range(0, a.shape[1], n)], 0) for a in x)


def there_and_back(x, tab, between):
    n = x.shape[2]

    def one(inverse, _):
        y = stack(left(side(right((x[0], x[1]), tab, inverse)), tab, inverse))
        x[0], x[1] = y

        @pl.when(inverse == 0)
        def _():
            lax.fori_loop(0, x.shape[1] // n, lambda s, _: between(s), None)

    lax.fori_loop(0, 2, one, None)


def at_position(s, n):
    return pl.ds(pl.multiple_of(s * n, n), n)


def load(x, s):
    rows = at_position(s, x.shape[2])
    return x[0, rows], x[1, rows]


def save(x, s, value):
    rows = at_position(s, x.shape[2])
    x[0, rows], x[1, rows] = value


def cmul(a, b):
    return a[0] * b[0] - a[1] * b[1], a[0] * b[1] + a[1] * b[0]


def conj_mul(a, b):
    return a[0] * b[0] + a[1] * b[1], a[0] * b[1] - a[1] * b[0]


def iota(n, dim):
    return lax.broadcasted_iota(jnp.int32, (n, n), dim)


def slot_mask(start, core, n):
    return (1 - 2 * core) * (iota(n, 1) - start) - core < 0


def pick(mask, slot, x):
    return jnp.where(mask, x, 0.0) if slot == 0 else jnp.where(mask, 0.0, x)


def masks_of(info, offsets, sizes, j, slot, n):
    tile = info[0] - j
    tile = jnp.where(tile < 0, tile + sizes[0], tile)
    r, q = offsets[j, 2 * slot], offsets[j, 2 * slot + 1]
    i = iota(n, 0)
    upper = i >= jnp.maximum(r, jnp.where(tile == 0, n // 2, 0))
    lower = i < jnp.minimum(r, jnp.where(tile == sizes[0] - 1, n // 2, n))
    return upper, lower, slot_mask(q, info[1] % 2, n)


def gather(obj, j, masks):
    upper, lower, cols = masks
    k = (j - 1) % obj.shape[0] if isinstance(j, int) else jnp.where(j == 0, obj.shape[0], j) - 1
    return tuple(
        jnp.where(
            upper,
            jnp.where(cols, obj[j, 0, p], obj[j, 1, p]),
            jnp.where(lower, jnp.where(cols, obj[k, 0, p], obj[k, 1, p]), 0.0),
        )
        for p in range(2)
    )


def scatter(grads, masks, tiles, k, slot, p):
    total = 0.0
    for j, half in ((k, 0), ((k + 1) % tiles, 1)):
        for m in range(BATCH):
            rows = masks[j][m][half]
            total = total + pick(masks[j][m][2], slot, jnp.where(rows, grads[j][m][p], 0.0))
    return total


def emit(grads, masks, tiles, outs, last):
    for slot, out in enumerate(outs):
        for p in range(2):
            if last:
                n = out.shape[-1]
                mine = iota(n, 0) >= n // 2
                out[p] = jnp.where(
                    mine, scatter(grads, masks, tiles, 0, slot, p), scatter(grads, masks, tiles, tiles - 1, slot, p)
                )
            else:
                for k in range(tiles):
                    out[k, p] = scatter(grads, masks, tiles, k, slot, p)


def advance(obj_in, obj_out, sums, info, sizes, first):
    tiles, n = obj_out.shape[0], obj_out.shape[-1]
    if not first:
        core, j = info[1] % 2, iota(n, 1)
        low = jnp.where(jnp.logical_and(core == 0, info[1] == 0), n // 2, 0)
        high = jnp.where(jnp.logical_and(core == 1, info[1] == sizes[1] - 1), n // 2, n)
        inside = jnp.logical_and(j >= low, j < high)
    for slot in range(2):
        own, got = sums[2 * slot], sums[2 * slot + 1]
        for k in range(tiles):
            for p in range(2):
                s = own[k, p] + got[k, p]
                if not first:
                    s = STEP * s if slot == 0 else jnp.where(inside, STEP * s, 0.0)
                    s = obj_in[k, slot, p] - s
                obj_out[k, slot, p] = s


def rows_of(x, tiles, n):
    at = lambda a, j, m: a[(j * BATCH + m) * n : (j * BATCH + m + 1) * n]
    return [[(at(x[0], j, m), at(x[1], j, m)) for m in range(BATCH)] for j in range(tiles)]


def stacked(parts):
    flat = [part for row in parts for part in row]
    return tuple(jnp.concatenate([part[p] for part in flat], 0) for p in range(2))


def tiled(wave, count):
    return tuple(jnp.concatenate([wave[p]] * count, 1) for p in range(2))


def kernel_a(period, sizes, first, info, offsets, *refs):
    obj_in = None if first else refs[0]
    *sums, probe, wave, tab, obj_out, inner = refs[0 if first else 1 :]
    advance(obj_in, obj_out, sums, info, sizes, first)
    n = obj_out.shape[-1]

    def enter(j, _):
        for m in range(BATCH):
            patch = gather(obj_out, j, masks_of(info, offsets, sizes, j, period * BATCH + m, n))
            save(inner, j * BATCH + m, cmul((probe[j, m, 0], probe[j, m, 1]), patch))

    lax.fori_loop(0, sizes[0], enter, None)
    there_and_back(inner, tab, lambda s: save(inner, s, cmul(load(inner, s), (wave[0], wave[1]))))


def kernel_b(period, sizes, first, last, tiles, info, offsets, counts, *refs):
    obj_in = None if first else refs[0]
    refs = refs[0 if first else 1 :]
    sums, inner, measured = refs[:4], refs[4], refs[5 : 5 + tiles]
    probe, wave, tab, obj_out, ge, go, he, ho = refs[5 + tiles :]
    advance(obj_in, obj_out, sums, info, sizes, first)
    n = obj_out.shape[-1]
    masks = [[masks_of(info, offsets, sizes, j, period * BATCH + m, n) for m in range(BATCH)] for j in range(tiles)]
    seconds = [[gather(obj_out, j, masks[j][m]) for m in range(BATCH)] for j in range(tiles)]
    waves = rows_of((inner[0], inner[1]), tiles, n)
    x = stacked([[cmul(waves[j][m], seconds[j][m]) for m in range(BATCH)] for j in range(tiles)])
    x = left(side(right(x, tab, 0)), tab, 0)
    level = jnp.concatenate([measured[j][m] for j in range(tiles) for m in range(BATCH)], 1)
    e = x[0] * x[0] + x[1] * x[1] - level
    x = right(stack(left((e * x[0], e * x[1]), tab, 1)), tab, 1)
    exits = rows_of(x, tiles, n)
    x = stacked([[conj_mul(seconds[j][m], exits[j][m]) for m in range(BATCH)] for j in range(tiles)])
    x = left(side(right(x, tab, 0)), tab, 0)
    emit(live_grads(waves, exits, counts, period), masks, tiles, (he, ho), last)
    x = left(conj_mul(tiled(wave, tiles * BATCH), x), tab, 1)
    exits = rows_of(right(stack(x), tab, 1), tiles, n)
    probes = [[(probe[j, m, 0], probe[j, m, 1]) for m in range(BATCH)] for j in range(tiles)]
    emit(live_grads(probes, exits, counts, period), masks, tiles, (ge, go), last)


def live_grads(forward, backward, counts, period):
    grads = []
    for j, row in enumerate(forward):
        grads.append([])
        for m, wave in enumerate(row):
            live = jnp.where(period * BATCH + m < counts[j], 1.0, 0.0)
            g = conj_mul(wave, backward[j][m])
            grads[j].append((g[0] * live, g[1] * live))
    return grads


def kernel_roll(period, offsets, probe, out):
    tiles, n = out.shape[0], out.shape[-1]

    def one(j, _):
        for m in range(BATCH):
            r = lax.rem(offsets[j, 2 * (period * BATCH + m)], n)
            q = lax.rem(offsets[j, 2 * (period * BATCH + m) + 1], n)
            for p in range(2):
                out[j, m, p] = pltpu.roll(pltpu.roll(probe[p], r, 0), q, 1)

    lax.fori_loop(0, tiles, one, None)


def kernel_place(info, *refs):
    *tiles, pe, po = refs
    n = pe.shape[-1]
    cols = slot_mask(n // 2, info[1] % 2, n)
    mine = iota(n, 0) >= n // 2
    for p in range(2):
        rolled = [pltpu.roll(pltpu.roll(tile[p], n // 2, 0), n // 2, 1) for tile in tiles]
        for k in range(len(tiles)):
            x = jnp.where(mine, rolled[k], rolled[(k + 1) % len(tiles)])
            pe[k, p] = pick(cols, 0, x)
            po[k, p] = pick(cols, 1, x)


def kernel_end(info, obj, fe, re, fo, ro, out):
    tiles, n = obj.shape[0], obj.shape[-1]
    cols = slot_mask(n // 2, info[1] % 2, n)
    mine = iota(n, 0) >= n // 2
    for p in range(2):
        x = [jnp.where(mine, obj[0, slot, p], obj[tiles - 1, slot, p]) for slot in range(2)]
        x = jnp.where(cols, x[0] - STEP * (fe[p] + re[p]), x[1] - STEP * (fo[p] + ro[p]))
        out[p] = pltpu.roll(pltpu.roll(x, n // 2, 0), n // 2, 1)


def call(kernel, scalars, arrays, outs):
    return pl.pallas_call(
        kernel,
        out_shape=[jax.ShapeDtypeStruct(s, F32) for s in outs],
        in_specs=[pl.BlockSpec(memory_space=pltpu.SMEM)] * len(scalars)
        + [pl.BlockSpec(memory_space=pltpu.VMEM)] * len(arrays),
        out_specs=[pl.BlockSpec(memory_space=pltpu.VMEM)] * len(outs),
        compiler_params=pltpu.CompilerParams(vmem_limit_bytes=24 * 1024 * 1024),
    )(*scalars, *arrays)


def after(value, other):
    return lax.optimization_barrier((value, other))[0]


def local(object_field, probe, propagator, offsets, counts, intensity):
    n = probe.shape[1]
    sizes = (lax.axis_size("gx"), lax.axis_size("gy"))
    tiles = sizes[0]
    slots = offsets.shape[2]
    ay = lax.axis_index("gy")
    chips = sizes[1] // 2
    chip = ay // 2
    chip = jnp.where(2 * chip < chips, chip, chips // 2 + chips - 1 - chip)
    info = jnp.stack([lax.axis_index("gx"), 2 * chip + ay % 2]).astype(jnp.int32)
    meta = jnp.concatenate([offsets.reshape(-1), counts.reshape(-1)]).astype(F32)
    meta = jnp.pad(meta, (0, n - meta.shape[0])).reshape(1, n)
    meta = jnp.broadcast_to(meta, (8, n))

    own = place_tiles(jnp.concatenate([object_field[0].reshape(2 * n, n), meta]))
    own1 = place_tiles(object_field[1])
    own2 = place_tiles(intensity[0, 0, :BATCH])
    packed = column(own)
    own3 = place_tiles(intensity[0, 0, BATCH:])
    tiles1 = column(own1)
    measured = [column(own2)]
    tiles0 = [x[: 2 * n].reshape(2, n, n) for x in packed]
    meta = jnp.stack([x[2 * n, : 2 * slots + 1] for x in packed]).astype(jnp.int32)
    offs, count = meta[:, : 2 * slots], meta[:, 2 * slots]
    tab = jnp.asarray(dft_tables(n))
    wave = jnp.stack([jnp.cos(propagator), jnp.sin(propagator)])
    pair, state = (2, n, n), (tiles, 2, 2, n, n)
    half, waves = (tiles, 2, n, n), (2, tiles * BATCH * n, n)

    def roll(b):
        return call(functools.partial(kernel_roll, b), [offs], [probe], [(tiles, 2, 2, n, n)])[0]

    def start(parts):
        pe, po = call(kernel_place, [info], parts, [half] * 2)
        ro = swap_cols(po)
        return [pe, swap_core(pe), po, ro]

    sums0 = start(tiles0)
    sums1 = start(tiles1)
    probes = [roll(0)]
    obj0, obj1 = [], []
    for b in range(NB):
        first, last = b == 0, b == NB - 1
        part = pair if last else half
        out0, inner = call(
            functools.partial(kernel_a, b, sizes, first), [info, offs],
            [*obj0, *sums0, probes[b], wave, tab], [state, waves],
        )
        if first:
            measured.append(column(after(own3[:BATCH], inner)))
        out1, ge, go, he, ho = call(
            functools.partial(kernel_b, b, sizes, first, last, tiles), [info, offs, count],
            [*obj1, *sums1, inner, *measured[b], probes[b], wave, tab], [state, part, part, part, part],
        )
        obj0, obj1 = [out0], [out1]
        ro = swap_cols(go)
        sums0 = [ge, swap_core(ge), go, ro]
        ro = swap_cols(ho)
        sums1 = [he, swap_core(he), ho, ro]
        if not last:
            probes.append(roll(b + 1))
        if b % 2 == 0 and b + 2 < NB:
            pieces = column(own3[(b + 1) * BATCH : (b + 3) * BATCH])
            measured += [[x[i * BATCH : (i + 1) * BATCH] for x in pieces] for i in range(2)]
    (last1,) = call(kernel_end, [info], [*obj1, *sums1], [pair])
    (last0,) = call(kernel_end, [info], [*obj0, *sums0], [pair])
    return jnp.stack([place_tiles(last0), place_tiles(last1)])


def solution(mesh):
    in_specs = (
        P(None, None, "gx", "gy"),
        P(),
        P(),
        P("gx", "gy", None, None),
        P("gx", "gy"),
        P("gx", "gy", None, None, None),
    )
    out_specs = P(None, None, "gx", "gy")
    return jax.shard_map(local, mesh=mesh, in_specs=in_specs, out_specs=out_specs, check_vma=False)
```

```python
import functools
import math

import jax
import jax.numpy as jnp
import numpy as np
from jax import lax
from jax.experimental import pallas as pl
from jax.experimental.pallas import tpu as pltpu
from jax.sharding import PartitionSpec as P


BATCH = 2
NB = 6
STEP = 0.08
F32 = jnp.float32
BF16 = jnp.bfloat16


def chip_order(size):
    chips = size // 2
    return [k if 2 * k < chips else chips // 2 + chips - 1 - k for k in range(chips)]


def both(pairs):
    return [p for i, j in pairs for p in ((i, j), (j, i))]


def swap_core(value):
    size = lax.axis_size("gy")
    return lax.ppermute(value, "gy", both([(i, i + 1) for i in range(0, size, 2)]))


def swap_cols(value):
    order = chip_order(lax.axis_size("gy"))
    return lax.ppermute(value, "gy", both([(2 * i + 1, 2 * j) for i, j in zip(order, order[1:])]))


def place_tiles(value):
    order = chip_order(lax.axis_size("gy"))
    return lax.ppermute(value, "gy", [(2 * i + m, 2 * j + m) for i, j in enumerate(order) for m in range(2)])


def column(value):
    size = lax.axis_size("gx")
    parts = [value]
    for k in range(1, size):
        parts.append(lax.ppermute(value, "gx", [(i, (i + k) % size) for i in range(size)]))
    return parts


def dft_tables(n):
    index = np.arange(n)
    phase = (index[:, None] * index[None, :] % n) * (2.0 * math.pi / n)
    c, s = np.cos(phase) / math.sqrt(n), np.sin(phase) / math.sqrt(n)
    fwd = np.block([[c, -s], [s, c]]).astype(np.float32)
    inv = np.block([[c, s], [-s, c]]).astype(np.float32)
    out = []
    for m in (fwd, inv):
        hi = m.astype(jnp.bfloat16)
        lo = (m - hi.astype(np.float32)).astype(jnp.bfloat16)
        out += [hi, lo]
    return np.stack(out)


def split(x):
    hi = x.astype(BF16)
    return hi, (x - hi.astype(F32)).astype(BF16)


def dot(a, b):
    return jnp.dot(a, b, preferred_element_type=F32)


def right(x, tab, inverse):
    n = x[0].shape[1]
    hi, lo = split(jnp.concatenate(x, 1))
    mh, ml = tab[2 * inverse], tab[2 * inverse + 1]
    y = dot(jnp.concatenate([hi, lo, hi], 1), jnp.concatenate([mh, mh, ml], 0))
    return y[:, :n], y[:, n:]


def left(x, tab, inverse):
    n = x[0].shape[0]
    hi, lo = split(jnp.concatenate(x, 0))
    mh, ml = tab[2 - 2 * inverse], tab[3 - 2 * inverse]
    y = dot(jnp.concatenate([mh, mh, ml], 1), jnp.concatenate([hi, lo, hi], 0))
    return y[:n], y[n:]


def side(x):
    n = x[0].shape[1]
    return tuple(jnp.concatenate([a[i : i + n] for i in range(0, a.shape[0], n)], 1) for a in x)


def stack(x):
    n = x[0].shape[0]
    return tuple(jnp.concatenate([a[:, i : i + n] for i in range(0, a.shape[1], n)], 0) for a in x)


def cmul(a, b):
    return a[0] * b[0] - a[1] * b[1], a[0] * b[1] + a[1] * b[0]


def conj_mul(a, b):
    return a[0] * b[0] + a[1] * b[1], a[0] * b[1] - a[1] * b[0]


def iota(n, dim):
    return lax.broadcasted_iota(jnp.int32, (n, n), dim)


def slot_mask(start, core, n):
    return (1 - 2 * core) * (iota(n, 1) - start) - core < 0


def pick(mask, slot, x):
    return jnp.where(mask, x, 0.0) if slot == 0 else jnp.where(mask, 0.0, x)


def masks_of(info, offsets, sizes, j, slot, n):
    tile = info[0] - j
    tile = jnp.where(tile < 0, tile + sizes[0], tile)
    r, q = offsets[j, 2 * slot], offsets[j, 2 * slot + 1]
    i = iota(n, 0)
    upper = i >= jnp.maximum(r, jnp.where(tile == 0, n // 2, 0))
    lower = i < jnp.minimum(r, jnp.where(tile == sizes[0] - 1, n // 2, n))
    return upper, lower, slot_mask(q, info[1] % 2, n)


def gather(obj, j, masks):
    upper, lower, cols = masks
    k = (j - 1) % obj.shape[0]
    return tuple(
        jnp.where(
            upper,
            jnp.where(cols, obj[j, 0, p], obj[j, 1, p]),
            jnp.where(lower, jnp.where(cols, obj[k, 0, p], obj[k, 1, p]), 0.0),
        )
        for p in range(2)
    )


def scatter(grads, masks, tiles, k, slot, p):
    total = 0.0
    for j, half in ((k, 0), ((k + 1) % tiles, 1)):
        for m in range(BATCH):
            rows = masks[j][m][half]
            total = total + pick(masks[j][m][2], slot, jnp.where(rows, grads[j][m][p], 0.0))
    return total


def emit(grads, masks, tiles, outs, last):
    for slot, out in enumerate(outs):
        for p in range(2):
            if last:
                n = out.shape[-1]
                mine = iota(n, 0) >= n // 2
                out[p] = jnp.where(
                    mine, scatter(grads, masks, tiles, 0, slot, p), scatter(grads, masks, tiles, tiles - 1, slot, p)
                )
            else:
                for k in range(tiles):
                    out[k, p] = scatter(grads, masks, tiles, k, slot, p)


def advance(obj_in, obj_out, sums, info, sizes, first):
    tiles, n = obj_out.shape[0], obj_out.shape[-1]
    if not first:
        core, j = info[1] % 2, iota(n, 1)
        low = jnp.where(jnp.logical_and(core == 0, info[1] == 0), n // 2, 0)
        high = jnp.where(jnp.logical_and(core == 1, info[1] == sizes[1] - 1), n // 2, n)
        inside = jnp.logical_and(j >= low, j < high)
    for slot in range(2):
        own, got = sums[2 * slot], sums[2 * slot + 1]
        for k in range(tiles):
            for p in range(2):
                s = own[k, p] + got[k, p]
                if not first:
                    s = STEP * s if slot == 0 else jnp.where(inside, STEP * s, 0.0)
                    s = obj_in[k, slot, p] - s
                obj_out[k, slot, p] = s


def rows_of(x, tiles, n):
    at = lambda a, j, m: a[(j * BATCH + m) * n : (j * BATCH + m + 1) * n]
    return [[(at(x[0], j, m), at(x[1], j, m)) for m in range(BATCH)] for j in range(tiles)]


def stacked(parts):
    flat = [part for row in parts for part in row]
    return tuple(jnp.concatenate([part[p] for part in flat], 0) for p in range(2))


def tiled(wave, count):
    return tuple(jnp.concatenate([wave[p]] * count, 1) for p in range(2))


def kernel_a(period, sizes, first, info, offsets, *refs):
    obj_in = None if first else refs[0]
    *sums, probe, wave, tab, obj_out, inner = refs[0 if first else 1 :]
    advance(obj_in, obj_out, sums, info, sizes, first)
    tiles, n = obj_out.shape[0], obj_out.shape[-1]
    parts = []
    for j in range(tiles):
        parts.append([])
        for m in range(BATCH):
            patch = gather(obj_out, j, masks_of(info, offsets, sizes, j, period * BATCH + m, n))
            parts[j].append(cmul((probe[j, m, 0], probe[j, m, 1]), patch))
    x = left(side(right(stacked(parts), tab, 0)), tab, 0)
    x = left(cmul(x, tiled(wave, tiles * BATCH)), tab, 1)
    x = right(stack(x), tab, 1)
    inner[0] = x[0]
    inner[1] = x[1]


def kernel_b(period, sizes, first, last, tiles, info, offsets, counts, *refs):
    obj_in = None if first else refs[0]
    refs = refs[0 if first else 1 :]
    sums, inner, measured = refs[:4], refs[4], refs[5 : 5 + tiles]
    probe, wave, tab, obj_out, ge, go, he, ho = refs[5 + tiles :]
    advance(obj_in, obj_out, sums, info, sizes, first)
    n = obj_out.shape[-1]
    masks = [[masks_of(info, offsets, sizes, j, period * BATCH + m, n) for m in range(BATCH)] for j in range(tiles)]
    seconds = [[gather(obj_out, j, masks[j][m]) for m in range(BATCH)] for j in range(tiles)]
    waves = rows_of((inner[0], inner[1]), tiles, n)
    x = stacked([[cmul(waves[j][m], seconds[j][m]) for m in range(BATCH)] for j in range(tiles)])
    x = left(side(right(x, tab, 0)), tab, 0)
    level = jnp.concatenate([measured[j][m] for j in range(tiles) for m in range(BATCH)], 1)
    e = x[0] * x[0] + x[1] * x[1] - level
    x = right(stack(left((e * x[0], e * x[1]), tab, 1)), tab, 1)
    exits = rows_of(x, tiles, n)
    x = stacked([[conj_mul(seconds[j][m], exits[j][m]) for m in range(BATCH)] for j in range(tiles)])
    x = left(side(right(x, tab, 0)), tab, 0)
    emit(live_grads(waves, exits, counts, period), masks, tiles, (he, ho), last)
    x = left(conj_mul(tiled(wave, tiles * BATCH), x), tab, 1)
    exits = rows_of(right(stack(x), tab, 1), tiles, n)
    probes = [[(probe[j, m, 0], probe[j, m, 1]) for m in range(BATCH)] for j in range(tiles)]
    emit(live_grads(probes, exits, counts, period), masks, tiles, (ge, go), last)


def live_grads(forward, backward, counts, period):
    grads = []
    for j, row in enumerate(forward):
        grads.append([])
        for m, wave in enumerate(row):
            live = jnp.where(period * BATCH + m < counts[j], 1.0, 0.0)
            g = conj_mul(wave, backward[j][m])
            grads[j].append((g[0] * live, g[1] * live))
    return grads


def kernel_roll(period, offsets, probe, out):
    tiles, n = out.shape[0], out.shape[-1]
    for j in range(tiles):
        for m in range(BATCH):
            r = lax.rem(offsets[j, 2 * (period * BATCH + m)], n)
            q = lax.rem(offsets[j, 2 * (period * BATCH + m) + 1], n)
            for p in range(2):
                out[j, m, p] = pltpu.roll(pltpu.roll(probe[p], r, 0), q, 1)


def kernel_place(info, *refs):
    *tiles, pe, po = refs
    n = pe.shape[-1]
    cols = slot_mask(n // 2, info[1] % 2, n)
    mine = iota(n, 0) >= n // 2
    for p in range(2):
        rolled = [pltpu.roll(pltpu.roll(tile[p], n // 2, 0), n // 2, 1) for tile in tiles]
        for k in range(len(tiles)):
            x = jnp.where(mine, rolled[k], rolled[(k + 1) % len(tiles)])
            pe[k, p] = pick(cols, 0, x)
            po[k, p] = pick(cols, 1, x)


def kernel_end(info, obj, fe, re, fo, ro, out):
    tiles, n = obj.shape[0], obj.shape[-1]
    cols = slot_mask(n // 2, info[1] % 2, n)
    mine = iota(n, 0) >= n // 2
    for p in range(2):
        x = [jnp.where(mine, obj[0, slot, p], obj[tiles - 1, slot, p]) for slot in range(2)]
        x = jnp.where(cols, x[0] - STEP * (fe[p] + re[p]), x[1] - STEP * (fo[p] + ro[p]))
        out[p] = pltpu.roll(pltpu.roll(x, n // 2, 0), n // 2, 1)


def call(kernel, scalars, arrays, outs):
    return pl.pallas_call(
        kernel,
        out_shape=[jax.ShapeDtypeStruct(s, F32) for s in outs],
        in_specs=[pl.BlockSpec(memory_space=pltpu.SMEM)] * len(scalars)
        + [pl.BlockSpec(memory_space=pltpu.VMEM)] * len(arrays),
        out_specs=[pl.BlockSpec(memory_space=pltpu.VMEM)] * len(outs),
        compiler_params=pltpu.CompilerParams(vmem_limit_bytes=24 * 1024 * 1024),
    )(*scalars, *arrays)


def local(object_field, probe, propagator, offsets, counts, intensity):
    n = probe.shape[1]
    sizes = (lax.axis_size("gx"), lax.axis_size("gy"))
    tiles = sizes[0]
    slots = offsets.shape[2]
    ay = lax.axis_index("gy")
    chips = sizes[1] // 2
    chip = ay // 2
    chip = jnp.where(2 * chip < chips, chip, chips // 2 + chips - 1 - chip)
    info = jnp.stack([lax.axis_index("gx"), 2 * chip + ay % 2]).astype(jnp.int32)
    meta = jnp.concatenate([offsets.reshape(-1), counts.reshape(-1)]).astype(F32)
    meta = jnp.pad(meta, (0, n - meta.shape[0])).reshape(1, n)
    meta = jnp.broadcast_to(meta, (8, n))

    own = place_tiles(jnp.concatenate([object_field[0].reshape(2 * n, n), meta]))
    own1 = place_tiles(object_field[1])
    own2 = place_tiles(intensity[0, 0, :BATCH])
    packed = column(own)
    own3 = place_tiles(intensity[0, 0, BATCH:])
    tiles1 = column(own1)
    measured = [column(own2)]
    tiles0 = [x[: 2 * n].reshape(2, n, n) for x in packed]
    meta = jnp.stack([x[2 * n, : 2 * slots + 1] for x in packed]).astype(jnp.int32)
    offs, count = meta[:, : 2 * slots], meta[:, 2 * slots]
    tab = jnp.asarray(dft_tables(n))
    wave = jnp.stack([jnp.cos(propagator), jnp.sin(propagator)])
    pair, state = (2, n, n), (tiles, 2, 2, n, n)
    half, waves = (tiles, 2, n, n), (2, tiles * BATCH * n, n)

    def roll(b):
        return call(functools.partial(kernel_roll, b), [offs], [probe], [(tiles, 2, 2, n, n)])[0]

    def start(parts):
        pe, po = call(kernel_place, [info], parts, [half] * 2)
        ro = swap_cols(po)
        return [pe, swap_core(pe), po, ro]

    sums0 = start(tiles0)
    sums1 = start(tiles1)
    probes = [roll(0)]
    obj0, obj1 = [], []
    for b in range(NB):
        first, last = b == 0, b == NB - 1
        part = pair if last else half
        out0, inner = call(
            functools.partial(kernel_a, b, sizes, first), [info, offs],
            [*obj0, *sums0, probes[b], wave, tab], [state, waves],
        )
        out1, ge, go, he, ho = call(
            functools.partial(kernel_b, b, sizes, first, last, tiles), [info, offs, count],
            [*obj1, *sums1, inner, *measured[b], probes[b], wave, tab], [state, part, part, part, part],
        )
        obj0, obj1 = [out0], [out1]
        ro = swap_cols(go)
        sums0 = [ge, swap_core(ge), go, ro]
        ro = swap_cols(ho)
        sums1 = [he, swap_core(he), ho, ro]
        if not last:
            probes.append(roll(b + 1))
        if first:
            measured.append(column(own3[:BATCH]))
        if b + 2 < NB:
            measured.append(column(own3[(b + 1) * BATCH : (b + 2) * BATCH]))
    (last1,) = call(kernel_end, [info], [*obj1, *sums1], [pair])
    (last0,) = call(kernel_end, [info], [*obj0, *sums0], [pair])
    return jnp.stack([place_tiles(last0), place_tiles(last1)])


def solution(mesh):
    in_specs = (
        P(None, None, "gx", "gy"),
        P(),
        P(),
        P("gx", "gy", None, None),
        P("gx", "gy"),
        P("gx", "gy", None, None, None),
    )
    out_specs = P(None, None, "gx", "gy")
    return jax.shard_map(local, mesh=mesh, in_specs=in_specs, out_specs=out_specs, check_vma=False)
```

```python
import functools
import math

import jax
import jax.numpy as jnp
import numpy as np
from jax import lax
from jax.experimental import pallas as pl
from jax.experimental.pallas import tpu as pltpu
from jax.sharding import PartitionSpec as P


BATCH = 2
NB = 6
STEP = 0.08
F32 = jnp.float32
BF16 = jnp.bfloat16


def chip_order(size):
    chips = size // 2
    return [k if 2 * k < chips else chips // 2 + chips - 1 - k for k in range(chips)]


def both(pairs):
    return [p for i, j in pairs for p in ((i, j), (j, i))]


def swap_core(value):
    size = lax.axis_size("gy")
    return lax.ppermute(value, "gy", both([(i, i + 1) for i in range(0, size, 2)]))


def swap_cols(value):
    order = chip_order(lax.axis_size("gy"))
    return lax.ppermute(value, "gy", both([(2 * i + 1, 2 * j) for i, j in zip(order, order[1:])]))


def place_tiles(value):
    order = chip_order(lax.axis_size("gy"))
    return lax.ppermute(value, "gy", [(2 * i + m, 2 * j + m) for i, j in enumerate(order) for m in range(2)])


def column(value):
    size = lax.axis_size("gx")
    parts = [value]
    for k in range(1, size):
        parts.append(lax.ppermute(value, "gx", [(i, (i + k) % size) for i in range(size)]))
    return parts


def dft_tables(n):
    index = np.arange(n)
    phase = (index[:, None] * index[None, :] % n) * (2.0 * math.pi / n)
    c, s = np.cos(phase) / math.sqrt(n), np.sin(phase) / math.sqrt(n)
    fwd = np.block([[c, -s], [s, c]]).astype(np.float32)
    inv = np.block([[c, s], [-s, c]]).astype(np.float32)
    out = []
    for m in (fwd, inv):
        hi = m.astype(jnp.bfloat16)
        lo = (m - hi.astype(np.float32)).astype(jnp.bfloat16)
        out += [hi, lo]
    return np.stack(out)


def split(x):
    hi = x.astype(BF16)
    return hi, (x - hi.astype(F32)).astype(BF16)


def dot(a, b):
    return jnp.dot(a, b, preferred_element_type=F32)


def right(x, tab, inverse):
    n = x[0].shape[1]
    hi, lo = split(jnp.concatenate(x, 1))
    mh, ml = tab[2 * inverse], tab[2 * inverse + 1]
    y = dot(jnp.concatenate([hi, lo, hi], 1), jnp.concatenate([mh, mh, ml], 0))
    return y[:, :n], y[:, n:]


def left(x, tab, inverse):
    n = x[0].shape[0]
    hi, lo = split(jnp.concatenate(x, 0))
    mh, ml = tab[2 - 2 * inverse], tab[3 - 2 * inverse]
    y = dot(jnp.concatenate([mh, mh, ml], 1), jnp.concatenate([hi, lo, hi], 0))
    return y[:n], y[n:]


def side(x):
    n = x[0].shape[1]
    return tuple(jnp.concatenate([a[i : i + n] for i in range(0, a.shape[0], n)], 1) for a in x)


def stack(x):
    n = x[0].shape[0]
    return tuple(jnp.concatenate([a[:, i : i + n] for i in range(0, a.shape[1], n)], 0) for a in x)


def cmul(a, b):
    return a[0] * b[0] - a[1] * b[1], a[0] * b[1] + a[1] * b[0]


def conj_mul(a, b):
    return a[0] * b[0] + a[1] * b[1], a[0] * b[1] - a[1] * b[0]


def iota(n, dim):
    return lax.broadcasted_iota(jnp.int32, (n, n), dim)


def slot_mask(start, core, n):
    return (1 - 2 * core) * (iota(n, 1) - start) - core < 0


def pick(mask, slot, x):
    return jnp.where(mask, x, 0.0) if slot == 0 else jnp.where(mask, 0.0, x)


def masks_of(info, offsets, sizes, j, slot, n):
    tile = info[0] - j
    tile = jnp.where(tile < 0, tile + sizes[0], tile)
    r, q = offsets[j, 2 * slot], offsets[j, 2 * slot + 1]
    i = iota(n, 0)
    upper = i >= jnp.maximum(r, jnp.where(tile == 0, n // 2, 0))
    lower = i < jnp.minimum(r, jnp.where(tile == sizes[0] - 1, n // 2, n))
    return upper, lower, slot_mask(q, info[1] % 2, n)


def gather(obj, j, masks):
    upper, lower, cols = masks
    k = (j - 1) % obj.shape[0]
    return tuple(
        jnp.where(
            upper,
            jnp.where(cols, obj[j, 0, p], obj[j, 1, p]),
            jnp.where(lower, jnp.where(cols, obj[k, 0, p], obj[k, 1, p]), 0.0),
        )
        for p in range(2)
    )


def scatter(grads, masks, tiles, k, slot, p):
    total = 0.0
    for j, half in ((k, 0), ((k + 1) % tiles, 1)):
        for m in range(BATCH):
            rows = masks[j][m][half]
            total = total + pick(masks[j][m][2], slot, jnp.where(rows, grads[j][m][p], 0.0))
    return total


def emit(grads, masks, tiles, outs, last):
    for slot, out in enumerate(outs):
        for p in range(2):
            if last:
                n = out.shape[-1]
                mine = iota(n, 0) >= n // 2
                out[p] = jnp.where(
                    mine, scatter(grads, masks, tiles, 0, slot, p), scatter(grads, masks, tiles, tiles - 1, slot, p)
                )
            else:
                for k in range(tiles):
                    out[k, p] = scatter(grads, masks, tiles, k, slot, p)


def advance(obj_in, obj_out, sums, info, sizes, first):
    tiles, n = obj_out.shape[0], obj_out.shape[-1]
    if not first:
        core, j = info[1] % 2, iota(n, 1)
        low = jnp.where(jnp.logical_and(core == 0, info[1] == 0), n // 2, 0)
        high = jnp.where(jnp.logical_and(core == 1, info[1] == sizes[1] - 1), n // 2, n)
        inside = jnp.logical_and(j >= low, j < high)
    for slot in range(2):
        own, got = sums[2 * slot], sums[2 * slot + 1]
        for k in range(tiles):
            for p in range(2):
                s = own[k, p] + got[k, p]
                if not first:
                    s = STEP * s if slot == 0 else jnp.where(inside, STEP * s, 0.0)
                    s = obj_in[k, slot, p] - s
                obj_out[k, slot, p] = s


def rows_of(x, tiles, n):
    at = lambda a, j, m: a[(j * BATCH + m) * n : (j * BATCH + m + 1) * n]
    return [[(at(x[0], j, m), at(x[1], j, m)) for m in range(BATCH)] for j in range(tiles)]


def stacked(parts):
    flat = [part for row in parts for part in row]
    return tuple(jnp.concatenate([part[p] for part in flat], 0) for p in range(2))


def tiled(wave, count):
    return tuple(jnp.concatenate([wave[p]] * count, 1) for p in range(2))


def kernel_a(period, sizes, first, info, offsets, *refs):
    obj_in = None if first else refs[0]
    *sums, probe, wave, tab, obj_out, inner = refs[0 if first else 1 :]
    advance(obj_in, obj_out, sums, info, sizes, first)
    tiles, n = obj_out.shape[0], obj_out.shape[-1]
    parts = []
    for j in range(tiles):
        parts.append([])
        for m in range(BATCH):
            patch = gather(obj_out, j, masks_of(info, offsets, sizes, j, period * BATCH + m, n))
            parts[j].append(cmul((probe[j, m, 0], probe[j, m, 1]), patch))
    x = left(side(right(stacked(parts), tab, 0)), tab, 0)
    x = left(cmul(x, tiled(wave, tiles * BATCH)), tab, 1)
    x = right(stack(x), tab, 1)
    inner[0] = x[0]
    inner[1] = x[1]


def kernel_b(period, sizes, first, last, tiles, info, offsets, counts, *refs):
    obj_in = None if first else refs[0]
    refs = refs[0 if first else 1 :]
    sums, inner, measured = refs[:4], refs[4], refs[5 : 5 + tiles]
    if last:
        tab, obj_out, back, he, ho = refs[5 + tiles :]
    else:
        probe, wave, tab, obj_out, ge, go, he, ho = refs[5 + tiles :]
    advance(obj_in, obj_out, sums, info, sizes, first)
    n = obj_out.shape[-1]
    masks = [[masks_of(info, offsets, sizes, j, period * BATCH + m, n) for m in range(BATCH)] for j in range(tiles)]
    seconds = [[gather(obj_out, j, masks[j][m]) for m in range(BATCH)] for j in range(tiles)]
    waves = rows_of((inner[0], inner[1]), tiles, n)
    x = stacked([[cmul(waves[j][m], seconds[j][m]) for m in range(BATCH)] for j in range(tiles)])
    x = left(side(right(x, tab, 0)), tab, 0)
    level = jnp.concatenate([measured[j][m] for j in range(tiles) for m in range(BATCH)], 1)
    e = x[0] * x[0] + x[1] * x[1] - level
    x = right(stack(left((e * x[0], e * x[1]), tab, 1)), tab, 1)
    exits = rows_of(x, tiles, n)
    x = stacked([[conj_mul(seconds[j][m], exits[j][m]) for m in range(BATCH)] for j in range(tiles)])
    if last:
        back[0] = x[0]
        back[1] = x[1]
        emit(live_grads(waves, exits, counts, period), masks, tiles, (he, ho), True)
        return
    x = left(side(right(x, tab, 0)), tab, 0)
    emit(live_grads(waves, exits, counts, period), masks, tiles, (he, ho), False)
    x = left(conj_mul(tiled(wave, tiles * BATCH), x), tab, 1)
    exits = rows_of(right(stack(x), tab, 1), tiles, n)
    probes = [[(probe[j, m, 0], probe[j, m, 1]) for m in range(BATCH)] for j in range(tiles)]
    emit(live_grads(probes, exits, counts, period), masks, tiles, (ge, go), False)


def live_grads(forward, backward, counts, period):
    grads = []
    for j, row in enumerate(forward):
        grads.append([])
        for m, wave in enumerate(row):
            live = jnp.where(period * BATCH + m < counts[j], 1.0, 0.0)
            g = conj_mul(wave, backward[j][m])
            grads[j].append((g[0] * live, g[1] * live))
    return grads


def kernel_c(period, sizes, info, offsets, counts, back, probe, wave, tab, ge, go):
    tiles, n = probe.shape[0], probe.shape[-1]
    masks = [[masks_of(info, offsets, sizes, j, period * BATCH + m, n) for m in range(BATCH)] for j in range(tiles)]
    x = left(side(right((back[0], back[1]), tab, 0)), tab, 0)
    x = left(conj_mul(tiled(wave, tiles * BATCH), x), tab, 1)
    waves = rows_of(right(stack(x), tab, 1), tiles, n)
    probes = [[(probe[j, m, 0], probe[j, m, 1]) for m in range(BATCH)] for j in range(tiles)]
    emit(live_grads(probes, waves, counts, period), masks, tiles, (ge, go), True)


def kernel_roll(period, offsets, probe, out):
    tiles, n = out.shape[0], out.shape[-1]
    for j in range(tiles):
        for m in range(BATCH):
            r = lax.rem(offsets[j, 2 * (period * BATCH + m)], n)
            q = lax.rem(offsets[j, 2 * (period * BATCH + m) + 1], n)
            for p in range(2):
                out[j, m, p] = pltpu.roll(pltpu.roll(probe[p], r, 0), q, 1)


def kernel_place(info, *refs):
    *tiles, pe, po = refs
    n = pe.shape[-1]
    cols = slot_mask(n // 2, info[1] % 2, n)
    mine = iota(n, 0) >= n // 2
    for p in range(2):
        rolled = [pltpu.roll(pltpu.roll(tile[p], n // 2, 0), n // 2, 1) for tile in tiles]
        for k in range(len(tiles)):
            x = jnp.where(mine, rolled[k], rolled[(k + 1) % len(tiles)])
            pe[k, p] = pick(cols, 0, x)
            po[k, p] = pick(cols, 1, x)


def kernel_end(info, obj, fe, re, fo, ro, out):
    tiles, n = obj.shape[0], obj.shape[-1]
    cols = slot_mask(n // 2, info[1] % 2, n)
    mine = iota(n, 0) >= n // 2
    for p in range(2):
        x = [jnp.where(mine, obj[0, slot, p], obj[tiles - 1, slot, p]) for slot in range(2)]
        x = jnp.where(cols, x[0] - STEP * (fe[p] + re[p]), x[1] - STEP * (fo[p] + ro[p]))
        out[p] = pltpu.roll(pltpu.roll(x, n // 2, 0), n // 2, 1)


def call(kernel, scalars, arrays, outs):
    return pl.pallas_call(
        kernel,
        out_shape=[jax.ShapeDtypeStruct(s, F32) for s in outs],
        in_specs=[pl.BlockSpec(memory_space=pltpu.SMEM)] * len(scalars)
        + [pl.BlockSpec(memory_space=pltpu.VMEM)] * len(arrays),
        out_specs=[pl.BlockSpec(memory_space=pltpu.VMEM)] * len(outs),
        compiler_params=pltpu.CompilerParams(vmem_limit_bytes=24 * 1024 * 1024),
    )(*scalars, *arrays)


def local(object_field, probe, propagator, offsets, counts, intensity):
    n = probe.shape[1]
    sizes = (lax.axis_size("gx"), lax.axis_size("gy"))
    tiles = sizes[0]
    slots = offsets.shape[2]
    ay = lax.axis_index("gy")
    chips = sizes[1] // 2
    chip = ay // 2
    chip = jnp.where(2 * chip < chips, chip, chips // 2 + chips - 1 - chip)
    info = jnp.stack([lax.axis_index("gx"), 2 * chip + ay % 2]).astype(jnp.int32)
    meta = jnp.concatenate([offsets.reshape(-1), counts.reshape(-1)]).astype(F32)
    meta = jnp.pad(meta, (0, n - meta.shape[0])).reshape(1, n)
    meta = jnp.broadcast_to(meta, (8, n))

    own = place_tiles(jnp.concatenate([object_field[0].reshape(2 * n, n), meta]))
    own1 = place_tiles(object_field[1])
    own2 = place_tiles(intensity[0, 0, :BATCH])
    packed = column(own)
    own3 = place_tiles(intensity[0, 0, BATCH:])
    tiles1 = column(own1)
    measured = [column(own2)]
    tiles0 = [x[: 2 * n].reshape(2, n, n) for x in packed]
    meta = jnp.stack([x[2 * n, : 2 * slots + 1] for x in packed]).astype(jnp.int32)
    offs, count = meta[:, : 2 * slots], meta[:, 2 * slots]
    tab = jnp.asarray(dft_tables(n))
    wave = jnp.stack([jnp.cos(propagator), jnp.sin(propagator)])
    pair, state = (2, n, n), (tiles, 2, 2, n, n)
    half, waves = (tiles, 2, n, n), (2, tiles * BATCH * n, n)

    def roll(b):
        return call(functools.partial(kernel_roll, b), [offs], [probe], [(tiles, 2, 2, n, n)])[0]

    def start(parts):
        pe, po = call(kernel_place, [info], parts, [half] * 2)
        ro = swap_cols(po)
        return [pe, swap_core(pe), po, ro]

    sums0 = start(tiles0)
    sums1 = start(tiles1)
    measured.append(column(own3[:BATCH]))
    probes = [roll(0)]
    obj0, obj1 = [], []
    for b in range(NB):
        first, last = b == 0, b == NB - 1
        out0, inner = call(
            functools.partial(kernel_a, b, sizes, first), [info, offs],
            [*obj0, *sums0, probes[b], wave, tab], [state, waves],
        )
        if last:
            break
        out1, ge, go, he, ho = call(
            functools.partial(kernel_b, b, sizes, first, False, tiles), [info, offs, count],
            [*obj1, *sums1, inner, *measured[b], probes[b], wave, tab], [state, half, half, half, half],
        )
        obj0, obj1 = [out0], [out1]
        ro = swap_cols(go)
        sums0 = [ge, swap_core(ge), go, ro]
        ro = swap_cols(ho)
        sums1 = [he, swap_core(he), ho, ro]
        probes.append(roll(b + 1))
        if b + 2 < NB:
            measured.append(column(own3[(b + 1) * BATCH : (b + 2) * BATCH]))
    b = NB - 1
    out1, back, he, ho = call(
        functools.partial(kernel_b, b, sizes, False, True, tiles), [info, offs, count],
        [*obj1, *sums1, inner, *measured[b], tab], [state, waves, pair, pair],
    )
    sums1 = [he, swap_core(he), ho, swap_cols(ho)]
    ge, go = call(
        functools.partial(kernel_c, b, sizes), [info, offs, count],
        [back, probes[b], wave, tab], [pair, pair],
    )
    sums0 = [ge, swap_core(ge), go, swap_cols(go)]
    (last1,) = call(kernel_end, [info], [out1, *sums1], [pair])
    (last0,) = call(kernel_end, [info], [out0, *sums0], [pair])
    last1 = place_tiles(last1)
    last0 = place_tiles(last0)
    return jnp.stack([last0, last1])


def solution(mesh):
    in_specs = (
        P(None, None, "gx", "gy"),
        P(),
        P(),
        P("gx", "gy", None, None),
        P("gx", "gy"),
        P("gx", "gy", None, None, None),
    )
    out_specs = P(None, None, "gx", "gy")
    return jax.shard_map(local, mesh=mesh, in_specs=in_specs, out_specs=out_specs, check_vma=False)
```

```python
import functools
import math

import jax
import jax.numpy as jnp
import numpy as np
from jax import lax
from jax.experimental import pallas as pl
from jax.experimental.pallas import tpu as pltpu
from jax.sharding import PartitionSpec as P


BATCH = 2
NB = 6
STEP = 0.08
F32 = jnp.float32
BF16 = jnp.bfloat16


def chip_order(size):
    chips = size // 2
    return [k if 2 * k < chips else chips // 2 + chips - 1 - k for k in range(chips)]


def both(pairs):
    return [p for i, j in pairs for p in ((i, j), (j, i))]


def swap_core(value):
    size = lax.axis_size("gy")
    return lax.ppermute(value, "gy", both([(i, i + 1) for i in range(0, size, 2)]))


def swap_cols(value):
    order = chip_order(lax.axis_size("gy"))
    return lax.ppermute(value, "gy", both([(2 * i + 1, 2 * j) for i, j in zip(order, order[1:])]))


def place_tiles(value):
    order = chip_order(lax.axis_size("gy"))
    return lax.ppermute(value, "gy", [(2 * i + m, 2 * j + m) for i, j in enumerate(order) for m in range(2)])


def column(value):
    size = lax.axis_size("gx")
    parts = [value]
    for k in range(1, size):
        parts.append(lax.ppermute(value, "gx", [(i, (i + k) % size) for i in range(size)]))
    return parts


def dft_tables(n):
    index = np.arange(n)
    phase = (index[:, None] * index[None, :] % n) * (2.0 * math.pi / n)
    quarters = []
    for m in (np.cos(phase) / math.sqrt(n), np.sin(phase) / math.sqrt(n)):
        m = m.astype(np.float32)
        hi = m.astype(jnp.bfloat16)
        quarters.append((jnp.asarray(hi), jnp.asarray((m - hi.astype(np.float32)).astype(jnp.bfloat16))))
    out = []
    for sign in (-1, 1):
        for c, s in zip(*quarters):
            out.append(jnp.concatenate([jnp.concatenate([c, sign * s], 1), jnp.concatenate([-sign * s, c], 1)], 0))
    return jnp.stack(out)


def split(x):
    hi = x.astype(BF16)
    return hi, (x - hi.astype(F32)).astype(BF16)


def dot(a, b):
    return jnp.dot(a, b, preferred_element_type=F32)


def right(x, tab, inverse):
    n = x[0].shape[1]
    hi, lo = split(jnp.concatenate(x, 1))
    mh, ml = tab[2 * inverse], tab[2 * inverse + 1]
    y = dot(jnp.concatenate([hi, lo, hi], 1), jnp.concatenate([mh, mh, ml], 0))
    return y[:, :n], y[:, n:]


def left(x, tab, inverse):
    n = x[0].shape[0]
    hi, lo = split(jnp.concatenate(x, 0))
    mh, ml = tab[2 - 2 * inverse], tab[3 - 2 * inverse]
    y = dot(jnp.concatenate([mh, mh, ml], 1), jnp.concatenate([hi, lo, hi], 0))
    return y[:n], y[n:]


def side(x):
    n = x[0].shape[1]
    return tuple(jnp.concatenate([a[i : i + n] for i in range(0, a.shape[0], n)], 1) for a in x)


def stack(x):
    n = x[0].shape[0]
    return tuple(jnp.concatenate([a[:, i : i + n] for i in range(0, a.shape[1], n)], 0) for a in x)


def there_and_back(x, tab, between):
    n = x.shape[2]

    def one(inverse, _):
        y = stack(left(side(right((x[0], x[1]), tab, inverse)), tab, inverse))
        x[0], x[1] = y

        @pl.when(inverse == 0)
        def _():
            lax.fori_loop(0, x.shape[1] // n, lambda s, _: between(s), None)

    lax.fori_loop(0, 2, one, None)


def at_position(s, n):
    return pl.ds(s * n if isinstance(s, int) else pl.multiple_of(s * n, n), n)


def load(x, s):
    rows = at_position(s, x.shape[2])
    return x[0, rows], x[1, rows]


def save(x, s, value):
    rows = at_position(s, x.shape[2])
    x[0, rows], x[1, rows] = value


def cmul(a, b):
    return a[0] * b[0] - a[1] * b[1], a[0] * b[1] + a[1] * b[0]


def conj_mul(a, b):
    return a[0] * b[0] + a[1] * b[1], a[0] * b[1] - a[1] * b[0]


def iota(n, dim):
    return lax.broadcasted_iota(jnp.int32, (n, n), dim)


def slot_mask(start, core, n):
    return (1 - 2 * core) * (iota(n, 1) - start) - core < 0


def pick(mask, slot, x):
    return jnp.where(mask, x, 0.0) if slot == 0 else jnp.where(mask, 0.0, x)


def masks_of(info, offsets, sizes, j, slot, n):
    tile = info[0] - j
    tile = jnp.where(tile < 0, tile + sizes[0], tile)
    r, q = offsets[j, 2 * slot], offsets[j, 2 * slot + 1]
    i = iota(n, 0)
    upper = i >= jnp.maximum(r, jnp.where(tile == 0, n // 2, 0))
    lower = i < jnp.minimum(r, jnp.where(tile == sizes[0] - 1, n // 2, n))
    return upper, lower, slot_mask(q, info[1] % 2, n)


def gather(obj, j, masks):
    upper, lower, cols = masks
    k = (j - 1) % obj.shape[0] if isinstance(j, int) else jnp.where(j == 0, obj.shape[0], j) - 1
    return tuple(
        jnp.where(
            upper,
            jnp.where(cols, obj[j, 0, p], obj[j, 1, p]),
            jnp.where(lower, jnp.where(cols, obj[k, 0, p], obj[k, 1, p]), 0.0),
        )
        for p in range(2)
    )


def scatter(grads, masks, tiles, k, slot, p):
    total = 0.0
    for j, half in ((k, 0), ((k + 1) % tiles, 1)):
        for m in range(BATCH):
            rows = masks[j][m][half]
            total = total + pick(masks[j][m][2], slot, jnp.where(rows, grads[j][m][p], 0.0))
    return total


def emit(grads, masks, tiles, outs, last):
    for slot, out in enumerate(outs):
        for p in range(2):
            if last:
                n = out.shape[-1]
                mine = iota(n, 0) >= n // 2
                out[p] = jnp.where(
                    mine, scatter(grads, masks, tiles, 0, slot, p), scatter(grads, masks, tiles, tiles - 1, slot, p)
                )
            else:
                for k in range(tiles):
                    out[k, p] = scatter(grads, masks, tiles, k, slot, p)


def scatter_all(grads, outs, info, offsets, sizes, period):
    tiles, n = sizes[0], grads.shape[2]

    def block(k):
        total = [[0.0, 0.0], [0.0, 0.0]]
        for j, half in ((k, 0), (jnp.where(k == tiles - 1, 0, k + 1), 1)):
            for m in range(BATCH):
                masks = masks_of(info, offsets, sizes, j, period * BATCH + m, n)
                grad = load(grads, j * BATCH + m)
                for p in range(2):
                    g = jnp.where(masks[half], grad[p], 0.0)
                    for slot in range(2):
                        total[slot][p] = total[slot][p] + pick(masks[2], slot, g)
        return total

    def write(k, _):
        total = block(k)
        for slot in range(2):
            for p in range(2):
                outs[slot][k, p] = total[slot][p]

    lax.fori_loop(0, tiles, write, None)


def advance(obj_in, obj_out, sums, info, sizes, first):
    tiles, n = obj_out.shape[0], obj_out.shape[-1]
    core, j = info[1] % 2, iota(n, 1)
    low = jnp.where(jnp.logical_and(core == 0, info[1] == 0), n // 2, 0)
    high = jnp.where(jnp.logical_and(core == 1, info[1] == sizes[1] - 1), n // 2, n)

    def block(k, _):
        inside = jnp.logical_and(j >= low, j < high)
        for slot in range(2):
            own, got = sums[2 * slot], sums[2 * slot + 1]
            for p in range(2):
                s = own[k, p] + got[k, p]
                if not first:
                    s = STEP * s if slot == 0 else jnp.where(inside, STEP * s, 0.0)
                    s = obj_in[k, slot, p] - s
                obj_out[k, slot, p] = s

    lax.fori_loop(0, tiles, block, None)


def rows_of(x, tiles, n):
    at = lambda a, j, m: a[(j * BATCH + m) * n : (j * BATCH + m + 1) * n]
    return [[(at(x[0], j, m), at(x[1], j, m)) for m in range(BATCH)] for j in range(tiles)]


def stacked(parts):
    flat = [part for row in parts for part in row]
    return tuple(jnp.concatenate([part[p] for part in flat], 0) for p in range(2))


def tiled(wave, count):
    return tuple(jnp.concatenate([wave[p]] * count, 1) for p in range(2))


def kernel_a(period, sizes, first, info, offsets, *refs):
    obj_in = None if first else refs[0]
    *sums, probe, wave, tab, obj_out, inner = refs[0 if first else 1 :]
    advance(obj_in, obj_out, sums, info, sizes, first)
    n = obj_out.shape[-1]

    def enter(j, _):
        for m in range(BATCH):
            patch = gather(obj_out, j, masks_of(info, offsets, sizes, j, period * BATCH + m, n))
            save(inner, j * BATCH + m, cmul((probe[j, m, 0], probe[j, m, 1]), patch))

    lax.fori_loop(0, sizes[0], enter, None)
    there_and_back(inner, tab, lambda s: save(inner, s, cmul(load(inner, s), (wave[0], wave[1]))))


def kernel_g(period, sizes, first, tiles, info, offsets, counts, *refs):
    obj_in = None if first else refs[0]
    refs = refs[0 if first else 1 :]
    sums, inner, measured = refs[:4], refs[4], refs[5 : 5 + tiles]
    probe, wave, tab, obj_out, ge, go, he, ho, x, kept = refs[5 + tiles :]
    advance(obj_in, obj_out, sums, info, sizes, first)
    n = obj_out.shape[-1]
    count = tiles * BATCH
    for j in range(tiles):
        for m in range(BATCH):
            s = j * BATCH + m
            patch = gather(obj_out, j, masks_of(info, offsets, sizes, j, period * BATCH + m, n))
            save(kept, s, patch)
            save(x, s, cmul(load(inner, s), patch))

    def alive(j, m):
        return jnp.where(period * BATCH + m < counts[j], 1.0, 0.0)

    def exit_plane(j, _):
        for m in range(BATCH):
            s = j * BATCH + m
            wave_out, patch = load(x, s), load(kept, s)
            g = conj_mul(load(inner, s), wave_out)
            save(x, s, conj_mul(patch, wave_out))
            save(kept, s, (g[0] * alive(j, m), g[1] * alive(j, m)))

    def entrance_plane(j, _):
        for m in range(BATCH):
            s = j * BATCH + m
            g = conj_mul((probe[j, m, 0], probe[j, m, 1]), load(x, s))
            save(x, s, (g[0] * alive(j, m), g[1] * alive(j, m)))

    def there_and_back_again(turn, _):
        y = left(side(right((x[0], x[1]), tab, 0)), tab, 0)
        level = jnp.concatenate([measured[j][m] for j in range(tiles) for m in range(BATCH)], 1)
        e = y[0] * y[0] + y[1] * y[1] - level
        q = conj_mul(tiled(wave, count), y)
        z = tuple(jnp.where(turn == 0, e * y[p], q[p]) for p in range(2))
        z = right(stack(left(z, tab, 1)), tab, 1)
        x[0] = z[0]
        x[1] = z[1]

        @pl.when(turn == 0)
        def _():
            lax.fori_loop(0, tiles, exit_plane, None)
            scatter_all(kept, (he, ho), info, offsets, sizes, period)

    lax.fori_loop(0, 2, there_and_back_again, None)
    lax.fori_loop(0, tiles, entrance_plane, None)
    scatter_all(x, (ge, go), info, offsets, sizes, period)


def kernel_b(period, sizes, tiles, info, offsets, counts, obj_in, *refs):
    sums, inner, measured = refs[:4], refs[4], refs[5 : 5 + tiles]
    tab, obj_out, back, he, ho = refs[5 + tiles :]
    advance(obj_in, obj_out, sums, info, sizes, False)
    n = obj_out.shape[-1]
    masks = [[masks_of(info, offsets, sizes, j, period * BATCH + m, n) for m in range(BATCH)] for j in range(tiles)]
    seconds = [[gather(obj_out, j, masks[j][m]) for m in range(BATCH)] for j in range(tiles)]
    waves = rows_of((inner[0], inner[1]), tiles, n)
    x = stacked([[cmul(waves[j][m], seconds[j][m]) for m in range(BATCH)] for j in range(tiles)])
    x = left(side(right(x, tab, 0)), tab, 0)
    level = jnp.concatenate([measured[j][m] for j in range(tiles) for m in range(BATCH)], 1)
    e = x[0] * x[0] + x[1] * x[1] - level
    x = right(stack(left((e * x[0], e * x[1]), tab, 1)), tab, 1)
    exits = rows_of(x, tiles, n)
    x = stacked([[conj_mul(seconds[j][m], exits[j][m]) for m in range(BATCH)] for j in range(tiles)])
    back[0] = x[0]
    back[1] = x[1]
    emit(live_grads(waves, exits, counts, period), masks, tiles, (he, ho), True)


def live_grads(forward, backward, counts, period):
    grads = []
    for j, row in enumerate(forward):
        grads.append([])
        for m, wave in enumerate(row):
            live = jnp.where(period * BATCH + m < counts[j], 1.0, 0.0)
            g = conj_mul(wave, backward[j][m])
            grads[j].append((g[0] * live, g[1] * live))
    return grads


def kernel_c(period, sizes, info, offsets, counts, back, probe, wave, tab, ge, go):
    tiles, n = probe.shape[0], probe.shape[-1]
    masks = [[masks_of(info, offsets, sizes, j, period * BATCH + m, n) for m in range(BATCH)] for j in range(tiles)]
    x = left(side(right((back[0], back[1]), tab, 0)), tab, 0)
    x = left(conj_mul(tiled(wave, tiles * BATCH), x), tab, 1)
    waves = rows_of(right(stack(x), tab, 1), tiles, n)
    probes = [[(probe[j, m, 0], probe[j, m, 1]) for m in range(BATCH)] for j in range(tiles)]
    emit(live_grads(probes, waves, counts, period), masks, tiles, (ge, go), True)


def kernel_roll(period, offsets, probe, out):
    tiles, n = out.shape[0], out.shape[-1]

    def one(j, _):
        for m in range(BATCH):
            r = lax.rem(offsets[j, 2 * (period * BATCH + m)], n)
            q = lax.rem(offsets[j, 2 * (period * BATCH + m) + 1], n)
            for p in range(2):
                out[j, m, p] = pltpu.roll(pltpu.roll(probe[p], r, 0), q, 1)

    lax.fori_loop(0, tiles, one, None)


def kernel_place(info, *refs):
    *tiles, pe, po = refs
    n = pe.shape[-1]
    cols = slot_mask(n // 2, info[1] % 2, n)
    mine = iota(n, 0) >= n // 2
    for p in range(2):
        rolled = [pltpu.roll(pltpu.roll(tile[p], n // 2, 0), n // 2, 1) for tile in tiles]
        for k in range(len(tiles)):
            x = jnp.where(mine, rolled[k], rolled[(k + 1) % len(tiles)])
            pe[k, p] = pick(cols, 0, x)
            po[k, p] = pick(cols, 1, x)


def kernel_end(info, obj, fe, re, fo, ro, out):
    tiles, n = obj.shape[0], obj.shape[-1]
    cols = slot_mask(n // 2, info[1] % 2, n)
    mine = iota(n, 0) >= n // 2
    for p in range(2):
        x = [jnp.where(mine, obj[0, slot, p], obj[tiles - 1, slot, p]) for slot in range(2)]
        x = jnp.where(cols, x[0] - STEP * (fe[p] + re[p]), x[1] - STEP * (fo[p] + ro[p]))
        out[p] = pltpu.roll(pltpu.roll(x, n // 2, 0), n // 2, 1)


def call(kernel, scalars, arrays, outs, scratch=()):
    return pl.pallas_call(
        kernel,
        out_shape=[jax.ShapeDtypeStruct(s, F32) for s in outs],
        in_specs=[pl.BlockSpec(memory_space=pltpu.SMEM)] * len(scalars)
        + [pl.BlockSpec(memory_space=pltpu.VMEM)] * len(arrays),
        out_specs=[pl.BlockSpec(memory_space=pltpu.VMEM)] * len(outs),
        scratch_shapes=[pltpu.VMEM(x, F32) for x in scratch],
        compiler_params=pltpu.CompilerParams(vmem_limit_bytes=24 * 1024 * 1024),
    )(*scalars, *arrays)


def local(object_field, probe, propagator, offsets, counts, intensity):
    n = probe.shape[1]
    sizes = (lax.axis_size("gx"), lax.axis_size("gy"))
    tiles = sizes[0]
    slots = offsets.shape[2]
    ay = lax.axis_index("gy")
    chips = sizes[1] // 2
    chip = ay // 2
    chip = jnp.where(2 * chip < chips, chip, chips // 2 + chips - 1 - chip)
    info = jnp.stack([lax.axis_index("gx"), 2 * chip + ay % 2]).astype(jnp.int32)
    meta = jnp.concatenate([offsets.reshape(-1), counts.reshape(-1)]).astype(F32)
    meta = jnp.pad(meta, (0, n - meta.shape[0])).reshape(1, n)
    meta = jnp.broadcast_to(meta, (8, n))

    own = place_tiles(jnp.concatenate([object_field[0].reshape(2 * n, n), meta]))
    own1 = place_tiles(jnp.concatenate([object_field[1], intensity[0, 0, :BATCH]]))
    own1, own2 = own1[:2], own1[2:]
    packed = column(own)
    own3 = place_tiles(intensity[0, 0, BATCH:])
    tiles1 = column(own1)
    measured = [column(own2)]
    tiles0 = [x[: 2 * n].reshape(2, n, n) for x in packed]
    meta = jnp.stack([x[2 * n, : 2 * slots + 1] for x in packed]).astype(jnp.int32)
    offs, count = meta[:, : 2 * slots], meta[:, 2 * slots]
    tab = dft_tables(n)
    wave = jnp.stack([jnp.cos(propagator), jnp.sin(propagator)])
    pair, state = (2, n, n), (tiles, 2, 2, n, n)
    half, waves = (tiles, 2, n, n), (2, tiles * BATCH * n, n)

    def roll(b):
        return call(functools.partial(kernel_roll, b), [offs], [probe], [(tiles, 2, 2, n, n)])[0]

    def start(parts):
        pe, po = call(kernel_place, [info], parts, [half] * 2)
        ro = swap_cols(po)
        return [pe, swap_core(pe), po, ro]

    sums0 = start(tiles0)
    sums1 = start(tiles1)
    measured.append(column(own3[:BATCH]))
    probes = [roll(0)]
    obj0, obj1 = [], []
    for b in range(NB):
        first, last = b == 0, b == NB - 1
        out0, inner = call(
            functools.partial(kernel_a, b, sizes, first), [info, offs],
            [*obj0, *sums0, probes[b], wave, tab], [state, waves],
        )
        if last:
            break
        out1, ge, go, he, ho = call(
            functools.partial(kernel_g, b, sizes, first, tiles), [info, offs, count],
            [*obj1, *sums1, inner, *measured[b], probes[b], wave, tab], [state, half, half, half, half], [waves, waves],
        )
        obj0, obj1 = [out0], [out1]
        ro = swap_cols(go)
        sums0 = [ge, swap_core(ge), go, ro]
        ro = swap_cols(ho)
        sums1 = [he, swap_core(he), ho, ro]
        probes.append(roll(b + 1))
        if b + 2 < NB:
            measured.append(column(own3[(b + 1) * BATCH : (b + 2) * BATCH]))
    b = NB - 1
    out1, back, he, ho = call(
        functools.partial(kernel_b, b, sizes, tiles), [info, offs, count],
        [*obj1, *sums1, inner, *measured[b], tab], [state, waves, pair, pair],
    )
    sums1 = [he, swap_core(he), ho, swap_cols(ho)]
    ge, go = call(
        functools.partial(kernel_c, b, sizes), [info, offs, count],
        [back, probes[b], wave, tab], [pair, pair],
    )
    sums0 = [ge, swap_core(ge), go, swap_cols(go)]
    (last1,) = call(kernel_end, [info], [out1, *sums1], [pair])
    (last0,) = call(kernel_end, [info], [out0, *sums0], [pair])
    last1 = place_tiles(last1)
    last0 = place_tiles(last0)
    return jnp.stack([last0, last1])


def solution(mesh):
    in_specs = (
        P(None, None, "gx", "gy"),
        P(),
        P(),
        P("gx", "gy", None, None),
        P("gx", "gy"),
        P("gx", "gy", None, None, None),
    )
    out_specs = P(None, None, "gx", "gy")
    return jax.shard_map(local, mesh=mesh, in_specs=in_specs, out_specs=out_specs, check_vma=False)
```

```python
import functools
import math

import jax
import jax.numpy as jnp
import numpy as np
from jax import lax
from jax.experimental import pallas as pl
from jax.experimental.pallas import tpu as pltpu
from jax.sharding import PartitionSpec as P


BATCH = 2
NB = 6
STEP = 0.08
F32 = jnp.float32
BF16 = jnp.bfloat16


def chip_order(size):
    chips = size // 2
    return [k if 2 * k < chips else chips // 2 + chips - 1 - k for k in range(chips)]


def both(pairs):
    return [p for i, j in pairs for p in ((i, j), (j, i))]


def swap_core(value):
    size = lax.axis_size("gy")
    return lax.ppermute(value, "gy", both([(i, i + 1) for i in range(0, size, 2)]))


def swap_cols(value):
    order = chip_order(lax.axis_size("gy"))
    return lax.ppermute(value, "gy", both([(2 * i + 1, 2 * j) for i, j in zip(order, order[1:])]))


def place_tiles(value):
    order = chip_order(lax.axis_size("gy"))
    return lax.ppermute(value, "gy", [(2 * i + m, 2 * j + m) for i, j in enumerate(order) for m in range(2)])


def column(value):
    size = lax.axis_size("gx")
    parts = [value]
    for k in range(1, size):
        parts.append(lax.ppermute(value, "gx", [(i, (i + k) % size) for i in range(size)]))
    return parts


def dft_tables(n):
    index = np.arange(n)
    phase = (index[:, None] * index[None, :] % n) * (2.0 * math.pi / n)
    quarters = []
    for m in (np.cos(phase) / math.sqrt(n), np.sin(phase) / math.sqrt(n)):
        m = m.astype(np.float32)
        hi = m.astype(jnp.bfloat16)
        quarters.append((jnp.asarray(hi), jnp.asarray((m - hi.astype(np.float32)).astype(jnp.bfloat16))))
    out = []
    for sign in (-1, 1):
        for c, s in zip(*quarters):
            out.append(jnp.concatenate([jnp.concatenate([c, sign * s], 1), jnp.concatenate([-sign * s, c], 1)], 0))
    return jnp.stack(out)


def split(x):
    hi = x.astype(BF16)
    return hi, (x - hi.astype(F32)).astype(BF16)


def dot(a, b):
    return jnp.dot(a, b, preferred_element_type=F32)


def right(x, tab, inverse):
    n = x[0].shape[1]
    hi, lo = split(jnp.concatenate(x, 1))
    mh, ml = tab[2 * inverse], tab[2 * inverse + 1]
    y = dot(jnp.concatenate([hi, lo, hi], 1), jnp.concatenate([mh, mh, ml], 0))
    return y[:, :n], y[:, n:]


def left(x, tab, inverse):
    n = x[0].shape[0]
    hi, lo = split(jnp.concatenate(x, 0))
    mh, ml = tab[2 - 2 * inverse], tab[3 - 2 * inverse]
    y = dot(jnp.concatenate([mh, mh, ml], 1), jnp.concatenate([hi, lo, hi], 0))
    return y[:n], y[n:]


def side(x):
    n = x[0].shape[1]
    return tuple(jnp.concatenate([a[i : i + n] for i in range(0, a.shape[0], n)], 1) for a in x)


def stack(x):
    n = x[0].shape[0]
    return tuple(jnp.concatenate([a[:, i : i + n] for i in range(0, a.shape[1], n)], 0) for a in x)


def there_and_back(x, tab, wave):
    count = x.shape[1] // x.shape[2]

    def one(inverse, _):
        y = left(side(right((x[0], x[1]), tab, inverse)), tab, inverse)
        z = cmul(tiled(wave, count), y)
        y = stack(tuple(jnp.where(inverse == 0, z[p], y[p]) for p in range(2)))
        x[0], x[1] = y

    lax.fori_loop(0, 2, one, None)


def at_position(s, n):
    return pl.ds(s * n if isinstance(s, int) else pl.multiple_of(s * n, n), n)


def load(x, s):
    rows = at_position(s, x.shape[2])
    return x[0, rows], x[1, rows]


def save(x, s, value):
    rows = at_position(s, x.shape[2])
    x[0, rows], x[1, rows] = value


def cmul(a, b):
    return a[0] * b[0] - a[1] * b[1], a[0] * b[1] + a[1] * b[0]


def conj_mul(a, b):
    return a[0] * b[0] + a[1] * b[1], a[0] * b[1] - a[1] * b[0]


def iota(n, dim):
    return lax.broadcasted_iota(jnp.int32, (n, n), dim)


def slot_mask(start, core, n):
    return (1 - 2 * core) * (iota(n, 1) - start) - core < 0


def pick(mask, slot, x):
    return jnp.where(mask, x, 0.0) if slot == 0 else jnp.where(mask, 0.0, x)


def masks_of(info, offsets, sizes, j, slot, n):
    tile = info[0] - j
    tile = jnp.where(tile < 0, tile + sizes[0], tile)
    r, q = offsets[j, 2 * slot], offsets[j, 2 * slot + 1]
    i = iota(n, 0)
    upper = i >= jnp.maximum(r, jnp.where(tile == 0, n // 2, 0))
    lower = i < jnp.minimum(r, jnp.where(tile == sizes[0] - 1, n // 2, n))
    return upper, lower, slot_mask(q, info[1] % 2, n)


def gather(obj, j, masks):
    upper, lower, cols = masks
    k = (j - 1) % obj.shape[0] if isinstance(j, int) else jnp.where(j == 0, obj.shape[0], j) - 1
    return tuple(
        jnp.where(
            upper,
            jnp.where(cols, obj[j, 0, p], obj[j, 1, p]),
            jnp.where(lower, jnp.where(cols, obj[k, 0, p], obj[k, 1, p]), 0.0),
        )
        for p in range(2)
    )


def scatter(grads, masks, tiles, k, slot, p):
    total = 0.0
    for j, half in ((k, 0), ((k + 1) % tiles, 1)):
        for m in range(BATCH):
            rows = masks[j][m][half]
            total = total + pick(masks[j][m][2], slot, jnp.where(rows, grads[j][m][p], 0.0))
    return total


def emit(grads, masks, tiles, outs, last):
    for slot, out in enumerate(outs):
        for p in range(2):
            if last:
                n = out.shape[-1]
                mine = iota(n, 0) >= n // 2
                out[p] = jnp.where(
                    mine, scatter(grads, masks, tiles, 0, slot, p), scatter(grads, masks, tiles, tiles - 1, slot, p)
                )
            else:
                for k in range(tiles):
                    out[k, p] = scatter(grads, masks, tiles, k, slot, p)


def scatter_all(fields, info, offsets, sizes, period):
    tiles, n = sizes[0], fields[0][0].shape[2]

    def write(k, _):
        row_sum, near = [[0.0, 0.0] for _ in fields], [[0.0, 0.0] for _ in fields]
        for j, half in ((k, 0), (jnp.where(k == tiles - 1, 0, k + 1), 1)):
            for m in range(BATCH):
                masks = masks_of(info, offsets, sizes, j, period * BATCH + m, n)
                for i, (grads, _, _) in enumerate(fields):
                    grad = load(grads, j * BATCH + m)
                    for p in range(2):
                        g = jnp.where(masks[half], grad[p], 0.0)
                        row_sum[i][p] = row_sum[i][p] + g
                        near[i][p] = near[i][p] + jnp.where(masks[2], g, 0.0)
        for i, (_, slot0, slot1) in enumerate(fields):
            for p in range(2):
                slot0[k, p] = near[i][p]
                slot1[k, p] = row_sum[i][p] - near[i][p]

    lax.fori_loop(0, tiles, write, None)


def advance(obj_in, obj_out, sums, info, sizes, first):
    tiles, n = obj_out.shape[0], obj_out.shape[-1]
    core, j = info[1] % 2, iota(n, 1)
    low = jnp.where(jnp.logical_and(core == 0, info[1] == 0), n // 2, 0)
    high = jnp.where(jnp.logical_and(core == 1, info[1] == sizes[1] - 1), n // 2, n)

    def block(k, _):
        inside = jnp.logical_and(j >= low, j < high)
        for slot in range(2):
            own, got = sums[2 * slot], sums[2 * slot + 1]
            for p in range(2):
                s = own[k, p] + got[k, p]
                if not first:
                    s = STEP * s if slot == 0 else jnp.where(inside, STEP * s, 0.0)
                    s = obj_in[k, slot, p] - s
                obj_out[k, slot, p] = s

    lax.fori_loop(0, tiles, block, None)


def rows_of(x, tiles, n):
    at = lambda a, j, m: a[(j * BATCH + m) * n : (j * BATCH + m + 1) * n]
    return [[(at(x[0], j, m), at(x[1], j, m)) for m in range(BATCH)] for j in range(tiles)]


def stacked(parts):
    flat = [part for row in parts for part in row]
    return tuple(jnp.concatenate([part[p] for part in flat], 0) for p in range(2))


def tiled(wave, count):
    return tuple(jnp.concatenate([wave[p]] * count, 1) for p in range(2))


def kernel_a(period, sizes, first, info, offsets, *refs):
    obj_in = None if first else refs[0]
    *sums, probe, wave, tab, obj_out, inner = refs[0 if first else 1 :]
    advance(obj_in, obj_out, sums, info, sizes, first)
    n = obj_out.shape[-1]

    def enter(j, _):
        for m in range(BATCH):
            patch = gather(obj_out, j, masks_of(info, offsets, sizes, j, period * BATCH + m, n))
            save(inner, j * BATCH + m, cmul((probe[j, m, 0], probe[j, m, 1]), patch))

    lax.fori_loop(0, sizes[0], enter, None)
    there_and_back(inner, tab, wave)


def kernel_g(period, sizes, first, tiles, info, offsets, counts, *refs):
    obj_in = None if first else refs[0]
    refs = refs[0 if first else 1 :]
    sums, inner, measured = refs[:4], refs[4], refs[5 : 5 + tiles]
    probe, wave, tab, obj_out, ge, go, he, ho, x, kept = refs[5 + tiles :]
    advance(obj_in, obj_out, sums, info, sizes, first)
    n = obj_out.shape[-1]
    count = tiles * BATCH
    for j in range(tiles):
        for m in range(BATCH):
            s = j * BATCH + m
            patch = gather(obj_out, j, masks_of(info, offsets, sizes, j, period * BATCH + m, n))
            save(kept, s, patch)
            save(x, s, cmul(load(inner, s), patch))

    def alive(j, m):
        return jnp.where(period * BATCH + m < counts[j], 1.0, 0.0)

    def exit_plane(j, _):
        for m in range(BATCH):
            s = j * BATCH + m
            wave_out, patch = load(x, s), load(kept, s)
            g = conj_mul(load(inner, s), wave_out)
            save(x, s, conj_mul(patch, wave_out))
            save(kept, s, (g[0] * alive(j, m), g[1] * alive(j, m)))

    def entrance_plane(j, _):
        for m in range(BATCH):
            s = j * BATCH + m
            g = conj_mul((probe[j, m, 0], probe[j, m, 1]), load(x, s))
            save(x, s, (g[0] * alive(j, m), g[1] * alive(j, m)))

    def there_and_back_again(turn, _):
        y = left(side(right((x[0], x[1]), tab, 0)), tab, 0)
        level = jnp.concatenate([measured[j][m] for j in range(tiles) for m in range(BATCH)], 1)
        e = y[0] * y[0] + y[1] * y[1] - level
        q = conj_mul(tiled(wave, count), y)
        z = tuple(jnp.where(turn == 0, e * y[p], q[p]) for p in range(2))
        z = right(stack(left(z, tab, 1)), tab, 1)
        x[0] = z[0]
        x[1] = z[1]

        @pl.when(turn == 0)
        def _():
            lax.fori_loop(0, tiles, exit_plane, None)

    lax.fori_loop(0, 2, there_and_back_again, None)
    lax.fori_loop(0, tiles, entrance_plane, None)
    scatter_all(((x, ge, go), (kept, he, ho)), info, offsets, sizes, period)


def kernel_b(period, sizes, tiles, info, offsets, counts, obj_in, *refs):
    sums, inner, measured = refs[:4], refs[4], refs[5 : 5 + tiles]
    tab, obj_out, back, he, ho = refs[5 + tiles :]
    advance(obj_in, obj_out, sums, info, sizes, False)
    n = obj_out.shape[-1]
    masks = [[masks_of(info, offsets, sizes, j, period * BATCH + m, n) for m in range(BATCH)] for j in range(tiles)]
    seconds = [[gather(obj_out, j, masks[j][m]) for m in range(BATCH)] for j in range(tiles)]
    waves = rows_of((inner[0], inner[1]), tiles, n)
    x = stacked([[cmul(waves[j][m], seconds[j][m]) for m in range(BATCH)] for j in range(tiles)])
    x = left(side(right(x, tab, 0)), tab, 0)
    level = jnp.concatenate([measured[j][m] for j in range(tiles) for m in range(BATCH)], 1)
    e = x[0] * x[0] + x[1] * x[1] - level
    x = right(stack(left((e * x[0], e * x[1]), tab, 1)), tab, 1)
    exits = rows_of(x, tiles, n)
    x = stacked([[conj_mul(seconds[j][m], exits[j][m]) for m in range(BATCH)] for j in range(tiles)])
    back[0] = x[0]
    back[1] = x[1]
    emit(live_grads(waves, exits, counts, period), masks, tiles, (he, ho), True)


def live_grads(forward, backward, counts, period):
    grads = []
    for j, row in enumerate(forward):
        grads.append([])
        for m, wave in enumerate(row):
            live = jnp.where(period * BATCH + m < counts[j], 1.0, 0.0)
            g = conj_mul(wave, backward[j][m])
            grads[j].append((g[0] * live, g[1] * live))
    return grads


def kernel_c(period, sizes, info, offsets, counts, back, probe, wave, tab, ge, go):
    tiles, n = probe.shape[0], probe.shape[-1]
    masks = [[masks_of(info, offsets, sizes, j, period * BATCH + m, n) for m in range(BATCH)] for j in range(tiles)]
    x = left(side(right((back[0], back[1]), tab, 0)), tab, 0)
    x = left(conj_mul(tiled(wave, tiles * BATCH), x), tab, 1)
    waves = rows_of(right(stack(x), tab, 1), tiles, n)
    probes = [[(probe[j, m, 0], probe[j, m, 1]) for m in range(BATCH)] for j in range(tiles)]
    emit(live_grads(probes, waves, counts, period), masks, tiles, (ge, go), True)


def kernel_roll(period, offsets, probe, out):
    tiles, n = out.shape[0], out.shape[-1]

    def one(j, _):
        for m in range(BATCH):
            r = lax.rem(offsets[j, 2 * (period * BATCH + m)], n)
            q = lax.rem(offsets[j, 2 * (period * BATCH + m) + 1], n)
            for p in range(2):
                out[j, m, p] = pltpu.roll(pltpu.roll(probe[p], r, 0), q, 1)

    lax.fori_loop(0, tiles, one, None)


def kernel_place(info, *refs):
    *tiles, pe, po = refs
    n = pe.shape[-1]
    cols = slot_mask(n // 2, info[1] % 2, n)
    mine = iota(n, 0) >= n // 2
    for p in range(2):
        rolled = [pltpu.roll(pltpu.roll(tile[p], n // 2, 0), n // 2, 1) for tile in tiles]
        for k in range(len(tiles)):
            x = jnp.where(mine, rolled[k], rolled[(k + 1) % len(tiles)])
            pe[k, p] = pick(cols, 0, x)
            po[k, p] = pick(cols, 1, x)


def kernel_end(info, obj, fe, re, fo, ro, out):
    tiles, n = obj.shape[0], obj.shape[-1]
    cols = slot_mask(n // 2, info[1] % 2, n)
    mine = iota(n, 0) >= n // 2
    for p in range(2):
        x = [jnp.where(mine, obj[0, slot, p], obj[tiles - 1, slot, p]) for slot in range(2)]
        x = jnp.where(cols, x[0] - STEP * (fe[p] + re[p]), x[1] - STEP * (fo[p] + ro[p]))
        out[p] = pltpu.roll(pltpu.roll(x, n // 2, 0), n // 2, 1)


def call(kernel, scalars, arrays, outs, scratch=()):
    return pl.pallas_call(
        kernel,
        out_shape=[jax.ShapeDtypeStruct(s, F32) for s in outs],
        in_specs=[pl.BlockSpec(memory_space=pltpu.SMEM)] * len(scalars)
        + [pl.BlockSpec(memory_space=pltpu.VMEM)] * len(arrays),
        out_specs=[pl.BlockSpec(memory_space=pltpu.VMEM)] * len(outs),
        scratch_shapes=[pltpu.VMEM(x, F32) for x in scratch],
        compiler_params=pltpu.CompilerParams(vmem_limit_bytes=24 * 1024 * 1024),
    )(*scalars, *arrays)


def local(object_field, probe, propagator, offsets, counts, intensity):
    n = probe.shape[1]
    sizes = (lax.axis_size("gx"), lax.axis_size("gy"))
    tiles = sizes[0]
    slots = offsets.shape[2]
    ay = lax.axis_index("gy")
    chips = sizes[1] // 2
    chip = ay // 2
    chip = jnp.where(2 * chip < chips, chip, chips // 2 + chips - 1 - chip)
    info = jnp.stack([lax.axis_index("gx"), 2 * chip + ay % 2]).astype(jnp.int32)
    meta = jnp.concatenate([offsets.reshape(-1), counts.reshape(-1)]).astype(F32)
    meta = jnp.pad(meta, (0, n - meta.shape[0])).reshape(1, n)
    meta = jnp.broadcast_to(meta, (8, n))

    own = place_tiles(jnp.concatenate([object_field[0].reshape(2 * n, n), meta]))
    own1 = place_tiles(jnp.concatenate([object_field[1], intensity[0, 0, :BATCH]]))
    own1, own2 = own1[:2], own1[2:]
    packed = column(own)
    own3 = place_tiles(intensity[0, 0, BATCH:])
    tiles1 = column(own1)
    measured = [column(own2)]
    tiles0 = [x[: 2 * n].reshape(2, n, n) for x in packed]
    meta = jnp.stack([x[2 * n, : 2 * slots + 1] for x in packed]).astype(jnp.int32)
    offs, count = meta[:, : 2 * slots], meta[:, 2 * slots]
    tab = dft_tables(n)
    wave = jnp.stack([jnp.cos(propagator), jnp.sin(propagator)])
    pair, state = (2, n, n), (tiles, 2, 2, n, n)
    half, waves = (tiles, 2, n, n), (2, tiles * BATCH * n, n)

    def roll(b):
        return call(functools.partial(kernel_roll, b), [offs], [probe], [(tiles, 2, 2, n, n)])[0]

    def start(parts):
        pe, po = call(kernel_place, [info], parts, [half] * 2)
        ro = swap_cols(po)
        return [pe, swap_core(pe), po, ro]

    sums0 = start(tiles0)
    sums1 = start(tiles1)
    measured.append(column(own3[:BATCH]))
    probes = [roll(0)]
    obj0, obj1 = [], []
    for b in range(NB):
        first, last = b == 0, b == NB - 1
        out0, inner = call(
            functools.partial(kernel_a, b, sizes, first), [info, offs],
            [*obj0, *sums0, probes[b], wave, tab], [state, waves],
        )
        if last:
            break
        out1, ge, go, he, ho = call(
            functools.partial(kernel_g, b, sizes, first, tiles), [info, offs, count],
            [*obj1, *sums1, inner, *measured[b], probes[b], wave, tab], [state, half, half, half, half], [waves, waves],
        )
        obj0, obj1 = [out0], [out1]
        ro = swap_cols(go)
        sums0 = [ge, swap_core(ge), go, ro]
        ro = swap_cols(ho)
        sums1 = [he, swap_core(he), ho, ro]
        probes.append(roll(b + 1))
        if b + 2 < NB:
            measured.append(column(own3[(b + 1) * BATCH : (b + 2) * BATCH]))
    b = NB - 1
    out1, back, he, ho = call(
        functools.partial(kernel_b, b, sizes, tiles), [info, offs, count],
        [*obj1, *sums1, inner, *measured[b], tab], [state, waves, pair, pair],
    )
    sums1 = [he, swap_core(he), ho, swap_cols(ho)]
    ge, go = call(
        functools.partial(kernel_c, b, sizes), [info, offs, count],
        [back, probes[b], wave, tab], [pair, pair],
    )
    sums0 = [ge, swap_core(ge), go, swap_cols(go)]
    (last1,) = call(kernel_end, [info], [out1, *sums1], [pair])
    (last0,) = call(kernel_end, [info], [out0, *sums0], [pair])
    last1 = place_tiles(last1)
    last0 = place_tiles(last0)
    return jnp.stack([last0, last1])


def solution(mesh):
    in_specs = (
        P(None, None, "gx", "gy"),
        P(),
        P(),
        P("gx", "gy", None, None),
        P("gx", "gy"),
        P("gx", "gy", None, None, None),
    )
    out_specs = P(None, None, "gx", "gy")
    return jax.shard_map(local, mesh=mesh, in_specs=in_specs, out_specs=out_specs, check_vma=False)
```

```python
import functools
import math

import jax
import jax.numpy as jnp
import numpy as np
from jax import lax
from jax.experimental import pallas as pl
from jax.experimental.pallas import tpu as pltpu
from jax.sharding import PartitionSpec as P


BATCH = 2
NB = 6
STEP = 0.08
F32 = jnp.float32
BF16 = jnp.bfloat16


def chip_order(size):
    chips = size // 2
    return [k if 2 * k < chips else chips // 2 + chips - 1 - k for k in range(chips)]


def both(pairs):
    return [p for i, j in pairs for p in ((i, j), (j, i))]


def swap_core(value):
    size = lax.axis_size("gy")
    return lax.ppermute(value, "gy", both([(i, i + 1) for i in range(0, size, 2)]))


def swap_cols(value):
    order = chip_order(lax.axis_size("gy"))
    return lax.ppermute(value, "gy", both([(2 * i + 1, 2 * j) for i, j in zip(order, order[1:])]))


def place_tiles(value):
    order = chip_order(lax.axis_size("gy"))
    return lax.ppermute(value, "gy", [(2 * i + m, 2 * j + m) for i, j in enumerate(order) for m in range(2)])


def column(value):
    size = lax.axis_size("gx")
    parts = [value]
    for k in range(1, size):
        parts.append(lax.ppermute(value, "gx", [(i, (i + k) % size) for i in range(size)]))
    return parts


def dft_tables(n):
    index = np.arange(n)
    phase = (index[:, None] * index[None, :] % n) * (2.0 * math.pi / n)
    quarters = []
    for m in (np.cos(phase) / math.sqrt(n), np.sin(phase) / math.sqrt(n)):
        m = m.astype(np.float32)
        hi = m.astype(jnp.bfloat16)
        quarters.append((jnp.asarray(hi), jnp.asarray((m - hi.astype(np.float32)).astype(jnp.bfloat16))))
    out = []
    for sign in (-1, 1):
        for c, s in zip(*quarters):
            out.append(jnp.concatenate([jnp.concatenate([c, sign * s], 1), jnp.concatenate([-sign * s, c], 1)], 0))
    return jnp.stack(out)


def split(x):
    hi = x.astype(BF16)
    return hi, (x - hi.astype(F32)).astype(BF16)


def dot(a, b):
    return jnp.dot(a, b, preferred_element_type=F32)


def right(x, tab, inverse):
    n = x[0].shape[1]
    hi, lo = split(jnp.concatenate(x, 1))
    mh, ml = tab[2 * inverse], tab[2 * inverse + 1]
    y = dot(jnp.concatenate([hi, lo, hi], 1), jnp.concatenate([mh, mh, ml], 0))
    return y[:, :n], y[:, n:]


def left(x, tab, inverse):
    n = x[0].shape[0]
    hi, lo = split(jnp.concatenate(x, 0))
    mh, ml = tab[2 - 2 * inverse], tab[3 - 2 * inverse]
    y = dot(jnp.concatenate([mh, mh, ml], 1), jnp.concatenate([hi, lo, hi], 0))
    return y[:n], y[n:]


def side(x):
    n = x[0].shape[1]
    return tuple(jnp.concatenate([a[i : i + n] for i in range(0, a.shape[0], n)], 1) for a in x)


def stack(x):
    n = x[0].shape[0]
    return tuple(jnp.concatenate([a[:, i : i + n] for i in range(0, a.shape[1], n)], 0) for a in x)


def there_and_back(x, tab, wave):
    count = x.shape[1] // x.shape[2]

    def one(inverse, _):
        y = left(side(right((x[0], x[1]), tab, inverse)), tab, inverse)
        z = cmul(tiled(wave, count), y)
        y = stack(tuple(jnp.where(inverse == 0, z[p], y[p]) for p in range(2)))
        x[0], x[1] = y

    lax.fori_loop(0, 2, one, None)


def at_position(s, n):
    return pl.ds(s * n if isinstance(s, int) else pl.multiple_of(s * n, n), n)


def load(x, s):
    rows = at_position(s, x.shape[2])
    return x[0, rows], x[1, rows]


def save(x, s, value):
    rows = at_position(s, x.shape[2])
    x[0, rows], x[1, rows] = value


def cmul(a, b):
    return a[0] * b[0] - a[1] * b[1], a[0] * b[1] + a[1] * b[0]


def conj_mul(a, b):
    return a[0] * b[0] + a[1] * b[1], a[0] * b[1] - a[1] * b[0]


def iota(n, dim):
    return lax.broadcasted_iota(jnp.int32, (n, n), dim)


def slot_mask(start, core, n):
    return (1 - 2 * core) * (iota(n, 1) - start) - core < 0


def pick(mask, slot, x):
    return jnp.where(mask, x, 0.0) if slot == 0 else jnp.where(mask, 0.0, x)


def masks_of(info, offsets, sizes, j, slot, n):
    tile = info[0] - j
    tile = jnp.where(tile < 0, tile + sizes[0], tile)
    r, q = offsets[j, 2 * slot], offsets[j, 2 * slot + 1]
    i = iota(n, 0)
    upper = i >= jnp.maximum(r, jnp.where(tile == 0, n // 2, 0))
    lower = i < jnp.minimum(r, jnp.where(tile == sizes[0] - 1, n // 2, n))
    return upper, lower, slot_mask(q, info[1] % 2, n)


def gather(obj, j, masks):
    upper, lower, cols = masks
    k = (j - 1) % obj.shape[0] if isinstance(j, int) else jnp.where(j == 0, obj.shape[0], j) - 1
    return tuple(
        jnp.where(
            upper,
            jnp.where(cols, obj[j, 0, p], obj[j, 1, p]),
            jnp.where(lower, jnp.where(cols, obj[k, 0, p], obj[k, 1, p]), 0.0),
        )
        for p in range(2)
    )


def scatter(grads, masks, tiles, k, slot, p):
    total = 0.0
    for j, half in ((k, 0), ((k + 1) % tiles, 1)):
        for m in range(BATCH):
            rows = masks[j][m][half]
            total = total + pick(masks[j][m][2], slot, jnp.where(rows, grads[j][m][p], 0.0))
    return total


def emit(grads, masks, tiles, outs, last):
    for slot, out in enumerate(outs):
        for p in range(2):
            if last:
                n = out.shape[-1]
                mine = iota(n, 0) >= n // 2
                out[p] = jnp.where(
                    mine, scatter(grads, masks, tiles, 0, slot, p), scatter(grads, masks, tiles, tiles - 1, slot, p)
                )
            else:
                for k in range(tiles):
                    out[k, p] = scatter(grads, masks, tiles, k, slot, p)


def scatter_all(fields, info, offsets, sizes, period):
    tiles, n = sizes[0], fields[0][0].shape[2]

    def write(k, _):
        row_sum, near = [[0.0, 0.0] for _ in fields], [[0.0, 0.0] for _ in fields]
        for j, half in ((k, 0), (jnp.where(k == tiles - 1, 0, k + 1), 1)):
            for m in range(BATCH):
                masks = masks_of(info, offsets, sizes, j, period * BATCH + m, n)
                for i, (grads, _, _) in enumerate(fields):
                    grad = load(grads, j * BATCH + m)
                    for p in range(2):
                        g = jnp.where(masks[half], grad[p], 0.0)
                        row_sum[i][p] = row_sum[i][p] + g
                        near[i][p] = near[i][p] + jnp.where(masks[2], g, 0.0)
        for i, (_, slot0, slot1) in enumerate(fields):
            for p in range(2):
                slot0[k, p] = near[i][p]
                slot1[k, p] = row_sum[i][p] - near[i][p]

    lax.fori_loop(0, tiles, write, None)


def advance(obj_in, obj_out, sums, info, sizes, first):
    tiles, n = obj_out.shape[0], obj_out.shape[-1]
    core, j = info[1] % 2, iota(n, 1)
    low = jnp.where(jnp.logical_and(core == 0, info[1] == 0), n // 2, 0)
    high = jnp.where(jnp.logical_and(core == 1, info[1] == sizes[1] - 1), n // 2, n)

    def block(k, _):
        inside = jnp.logical_and(j >= low, j < high)
        for slot in range(2):
            own, got = sums[2 * slot], sums[2 * slot + 1]
            for p in range(2):
                s = own[k, p] + got[k, p]
                if not first:
                    s = STEP * s if slot == 0 else jnp.where(inside, STEP * s, 0.0)
                    s = obj_in[k, slot, p] - s
                obj_out[k, slot, p] = s

    lax.fori_loop(0, tiles, block, None)


def rows_of(x, tiles, n):
    at = lambda a, j, m: a[(j * BATCH + m) * n : (j * BATCH + m + 1) * n]
    return [[(at(x[0], j, m), at(x[1], j, m)) for m in range(BATCH)] for j in range(tiles)]


def stacked(parts):
    flat = [part for row in parts for part in row]
    return tuple(jnp.concatenate([part[p] for part in flat], 0) for p in range(2))


def tiled(wave, count):
    return tuple(jnp.concatenate([wave[p]] * count, 1) for p in range(2))


def kernel_a(period, sizes, first, info, offsets, *refs):
    obj_in = None if first else refs[0]
    *sums, probe, wave, tab, obj_out, inner = refs[0 if first else 1 :]
    advance(obj_in, obj_out, sums, info, sizes, first)
    n = obj_out.shape[-1]

    def enter(j, _):
        for m in range(BATCH):
            patch = gather(obj_out, j, masks_of(info, offsets, sizes, j, period * BATCH + m, n))
            save(inner, j * BATCH + m, cmul((probe[j, m, 0], probe[j, m, 1]), patch))

    lax.fori_loop(0, sizes[0], enter, None)
    there_and_back(inner, tab, wave)


def levels_of(measured, period):
    size = measured[0].shape[0]
    start = period * BATCH % size
    return jnp.concatenate([x[start + m] for x in measured for m in range(BATCH)], 1)


def kernel_g(period, sizes, first, tiles, info, offsets, counts, *refs):
    obj_in = None if first else refs[0]
    refs = refs[0 if first else 1 :]
    sums, inner, measured = refs[:4], refs[4], refs[5 : 5 + tiles]
    probe, wave, tab, obj_out, ge, go, he, ho, x, kept = refs[5 + tiles :]
    advance(obj_in, obj_out, sums, info, sizes, first)
    n = obj_out.shape[-1]
    count = tiles * BATCH
    for j in range(tiles):
        for m in range(BATCH):
            s = j * BATCH + m
            patch = gather(obj_out, j, masks_of(info, offsets, sizes, j, period * BATCH + m, n))
            save(kept, s, patch)
            save(x, s, cmul(load(inner, s), patch))

    def alive(j, m):
        return jnp.where(period * BATCH + m < counts[j], 1.0, 0.0)

    def exit_plane(j, _):
        for m in range(BATCH):
            s = j * BATCH + m
            wave_out, patch = load(x, s), load(kept, s)
            g = conj_mul(load(inner, s), wave_out)
            save(x, s, conj_mul(patch, wave_out))
            save(kept, s, (g[0] * alive(j, m), g[1] * alive(j, m)))

    def entrance_plane(j, _):
        for m in range(BATCH):
            s = j * BATCH + m
            g = conj_mul((probe[j, m, 0], probe[j, m, 1]), load(x, s))
            save(x, s, (g[0] * alive(j, m), g[1] * alive(j, m)))

    def there_and_back_again(turn, _):
        y = left(side(right((x[0], x[1]), tab, 0)), tab, 0)
        level = levels_of(measured, period)
        e = y[0] * y[0] + y[1] * y[1] - level
        q = conj_mul(tiled(wave, count), y)
        z = tuple(jnp.where(turn == 0, e * y[p], q[p]) for p in range(2))
        z = right(stack(left(z, tab, 1)), tab, 1)
        x[0] = z[0]
        x[1] = z[1]

        @pl.when(turn == 0)
        def _():
            lax.fori_loop(0, tiles, exit_plane, None)

    lax.fori_loop(0, 2, there_and_back_again, None)
    lax.fori_loop(0, tiles, entrance_plane, None)
    scatter_all(((x, ge, go), (kept, he, ho)), info, offsets, sizes, period)


def kernel_b(period, sizes, tiles, info, offsets, counts, obj_in, *refs):
    sums, inner, measured = refs[:4], refs[4], refs[5 : 5 + tiles]
    tab, obj_out, back, he, ho = refs[5 + tiles :]
    advance(obj_in, obj_out, sums, info, sizes, False)
    n = obj_out.shape[-1]
    masks = [[masks_of(info, offsets, sizes, j, period * BATCH + m, n) for m in range(BATCH)] for j in range(tiles)]
    seconds = [[gather(obj_out, j, masks[j][m]) for m in range(BATCH)] for j in range(tiles)]
    waves = rows_of((inner[0], inner[1]), tiles, n)
    x = stacked([[cmul(waves[j][m], seconds[j][m]) for m in range(BATCH)] for j in range(tiles)])
    x = left(side(right(x, tab, 0)), tab, 0)
    level = levels_of(measured, period)
    e = x[0] * x[0] + x[1] * x[1] - level
    x = right(stack(left((e * x[0], e * x[1]), tab, 1)), tab, 1)
    exits = rows_of(x, tiles, n)
    x = stacked([[conj_mul(seconds[j][m], exits[j][m]) for m in range(BATCH)] for j in range(tiles)])
    back[0] = x[0]
    back[1] = x[1]
    emit(live_grads(waves, exits, counts, period), masks, tiles, (he, ho), True)


def live_grads(forward, backward, counts, period):
    grads = []
    for j, row in enumerate(forward):
        grads.append([])
        for m, wave in enumerate(row):
            live = jnp.where(period * BATCH + m < counts[j], 1.0, 0.0)
            g = conj_mul(wave, backward[j][m])
            grads[j].append((g[0] * live, g[1] * live))
    return grads


def kernel_c(period, sizes, info, offsets, counts, back, probe, wave, tab, ge, go):
    tiles, n = probe.shape[0], probe.shape[-1]
    masks = [[masks_of(info, offsets, sizes, j, period * BATCH + m, n) for m in range(BATCH)] for j in range(tiles)]
    x = left(side(right((back[0], back[1]), tab, 0)), tab, 0)
    x = left(conj_mul(tiled(wave, tiles * BATCH), x), tab, 1)
    waves = rows_of(right(stack(x), tab, 1), tiles, n)
    probes = [[(probe[j, m, 0], probe[j, m, 1]) for m in range(BATCH)] for j in range(tiles)]
    emit(live_grads(probes, waves, counts, period), masks, tiles, (ge, go), True)


def kernel_roll(period, offsets, probe, out):
    tiles, n = out.shape[0], out.shape[-1]

    def one(j, _):
        for m in range(BATCH):
            r = lax.rem(offsets[j, 2 * (period * BATCH + m)], n)
            q = lax.rem(offsets[j, 2 * (period * BATCH + m) + 1], n)
            for p in range(2):
                out[j, m, p] = pltpu.roll(pltpu.roll(probe[p], r, 0), q, 1)

    lax.fori_loop(0, tiles, one, None)


def kernel_place(info, *refs):
    *tiles, pe, po = refs
    n = pe.shape[-1]
    cols = slot_mask(n // 2, info[1] % 2, n)
    mine = iota(n, 0) >= n // 2
    for p in range(2):
        rolled = [pltpu.roll(pltpu.roll(tile[p], n // 2, 0), n // 2, 1) for tile in tiles]
        for k in range(len(tiles)):
            x = jnp.where(mine, rolled[k], rolled[(k + 1) % len(tiles)])
            pe[k, p] = pick(cols, 0, x)
            po[k, p] = pick(cols, 1, x)


def kernel_end(info, obj, fe, re, fo, ro, out):
    tiles, n = obj.shape[0], obj.shape[-1]
    cols = slot_mask(n // 2, info[1] % 2, n)
    mine = iota(n, 0) >= n // 2
    for p in range(2):
        x = [jnp.where(mine, obj[0, slot, p], obj[tiles - 1, slot, p]) for slot in range(2)]
        x = jnp.where(cols, x[0] - STEP * (fe[p] + re[p]), x[1] - STEP * (fo[p] + ro[p]))
        out[p] = pltpu.roll(pltpu.roll(x, n // 2, 0), n // 2, 1)


def call(kernel, scalars, arrays, outs, scratch=()):
    return pl.pallas_call(
        kernel,
        out_shape=[jax.ShapeDtypeStruct(s, F32) for s in outs],
        in_specs=[pl.BlockSpec(memory_space=pltpu.SMEM)] * len(scalars)
        + [pl.BlockSpec(memory_space=pltpu.VMEM)] * len(arrays),
        out_specs=[pl.BlockSpec(memory_space=pltpu.VMEM)] * len(outs),
        scratch_shapes=[pltpu.VMEM(x, F32) for x in scratch],
        compiler_params=pltpu.CompilerParams(vmem_limit_bytes=24 * 1024 * 1024),
    )(*scalars, *arrays)


def local(object_field, probe, propagator, offsets, counts, intensity):
    n = probe.shape[1]
    sizes = (lax.axis_size("gx"), lax.axis_size("gy"))
    tiles = sizes[0]
    slots = offsets.shape[2]
    ay = lax.axis_index("gy")
    chips = sizes[1] // 2
    chip = ay // 2
    chip = jnp.where(2 * chip < chips, chip, chips // 2 + chips - 1 - chip)
    info = jnp.stack([lax.axis_index("gx"), 2 * chip + ay % 2]).astype(jnp.int32)
    meta = jnp.concatenate([offsets.reshape(-1), counts.reshape(-1)]).astype(F32)
    meta = jnp.pad(meta, (0, n - meta.shape[0])).reshape(1, n)
    meta = jnp.broadcast_to(meta, (8, n))

    own = place_tiles(jnp.concatenate([object_field[0].reshape(2 * n, n), meta]))
    own1 = place_tiles(jnp.concatenate([object_field[1], intensity[0, 0, :BATCH]]))
    own1, own2 = own1[:2], own1[2:]
    packed = column(own)
    own3 = place_tiles(intensity[0, 0, BATCH:])
    tiles1 = column(own1)
    measured = [column(own2)]
    tiles0 = [x[: 2 * n].reshape(2, n, n) for x in packed]
    meta = jnp.stack([x[2 * n, : 2 * slots + 1] for x in packed]).astype(jnp.int32)
    offs, count = meta[:, : 2 * slots], meta[:, 2 * slots]
    tab = dft_tables(n)
    wave = jnp.stack([jnp.cos(propagator), jnp.sin(propagator)])
    pair, state = (2, n, n), (tiles, 2, 2, n, n)
    half, waves = (tiles, 2, n, n), (2, tiles * BATCH * n, n)

    def roll(b):
        return call(functools.partial(kernel_roll, b), [offs], [probe], [(tiles, 2, 2, n, n)])[0]

    def start(parts):
        pe, po = call(kernel_place, [info], parts, [half] * 2)
        ro = swap_cols(po)
        return [pe, swap_core(pe), po, ro]

    sums0 = start(tiles0)
    sums1 = start(tiles1)
    measured.append(column(own3[:BATCH]))
    probes = [roll(0)]
    obj0, obj1 = [], []
    for b in range(NB):
        first, last = b == 0, b == NB - 1
        out0, inner = call(
            functools.partial(kernel_a, b, sizes, first), [info, offs],
            [*obj0, *sums0, probes[b], wave, tab], [state, waves],
        )
        if last:
            break
        out1, ge, go, he, ho = call(
            functools.partial(kernel_g, b, sizes, first, tiles), [info, offs, count],
            [*obj1, *sums1, inner, *measured[b], probes[b], wave, tab], [state, half, half, half, half], [waves, waves],
        )
        obj0, obj1 = [out0], [out1]
        ro = swap_cols(go)
        sums0 = [ge, swap_core(ge), go, ro]
        ro = swap_cols(ho)
        sums1 = [he, swap_core(he), ho, ro]
        probes.append(roll(b + 1))
        if b % 2 == 0 and b + 2 < NB:
            pieces = column(own3[(b + 1) * BATCH : (b + 3) * BATCH])
            measured += [pieces, pieces]
    b = NB - 1
    out1, back, he, ho = call(
        functools.partial(kernel_b, b, sizes, tiles), [info, offs, count],
        [*obj1, *sums1, inner, *measured[b], tab], [state, waves, pair, pair],
    )
    sums1 = [he, swap_core(he), ho, swap_cols(ho)]
    ge, go = call(
        functools.partial(kernel_c, b, sizes), [info, offs, count],
        [back, probes[b], wave, tab], [pair, pair],
    )
    sums0 = [ge, swap_core(ge), go, swap_cols(go)]
    (last1,) = call(kernel_end, [info], [out1, *sums1], [pair])
    (last0,) = call(kernel_end, [info], [out0, *sums0], [pair])
    last1 = place_tiles(last1)
    last0 = place_tiles(last0)
    return jnp.stack([last0, last1])


def solution(mesh):
    in_specs = (
        P(None, None, "gx", "gy"),
        P(),
        P(),
        P("gx", "gy", None, None),
        P("gx", "gy"),
        P("gx", "gy", None, None, None),
    )
    out_specs = P(None, None, "gx", "gy")
    return jax.shard_map(local, mesh=mesh, in_specs=in_specs, out_specs=out_specs, check_vma=False)
```
